32 devices in a mesh: parts: 2 (over y), seq: 4 (over z), head: 2 (over x), fsdp: 2 (over core).
Axes of the slice: x: 2, y: 2, z: 4, core: 2. Of those that a mesh axis runs over, the one named last changes fastest.
Arguments:
- frames: bfloat16 [2048, 1024], P(('parts', 'seq', 'head', 'fsdp')), parts along dimension 0, may hold values from -24 to 24
- length: int32 [2], P('parts'), parts along dimension 0, may hold values from 512 to 1024
- ln1_gain: float32 [1024], replicated, may hold values from 0.1 to 1.9
- w_query: bfloat16 [1024, 1024], P('seq', ('head', 'fsdp')), may hold values from -0.2 to 0.2
- w_key: bfloat16 [1024, 1024], P('seq', ('head', 'fsdp')), may hold values from -3 to 3
- w_value: bfloat16 [1024, 1024], P('seq', ('head', 'fsdp')), may hold values from -0.375 to 0.375
- w_out: bfloat16 [1024, 1024], P(('head', 'fsdp'), 'seq'), may hold values from -0.1875 to 0.1875
- ln2_gain: float32 [1024], replicated, may hold values from 0.1 to 1.9
- pw1_value: bfloat16 [1024, 1024], P('seq', ('head', 'fsdp')), may hold values from -0.1875 to 0.1875
- pw1_gate: bfloat16 [1024, 1024], P('seq', ('head', 'fsdp')), may hold values from -0.375 to 0.375
- depth_kernel: float32 [9, 1024], P(None, ('head', 'fsdp')), may hold values from -2 to 2
- bn_scale: float32 [1024], P(('head', 'fsdp')), may hold values from 0.1 to 1.9
- bn_shift: float32 [1024], P(('head', 'fsdp')), may hold values from -3 to 3
- pw2: bfloat16 [1024, 1024], P(('head', 'fsdp'), 'seq'), may hold values from -0.1875 to 0.1875
Outputs:
- encoded: bfloat16 [2048, 1024], P(('parts', 'seq', 'head', 'fsdp')), parts along dimension 0
The draws below stay inside these ranges and needn't reach their ends.
There are 2 independent parts, one for each index of `parts`. The reference program is written for one: setup_inputs(seed, part) draws one part's arguments, and reference() takes and returns one part's arrays. A program takes and returns all parts, laid end to end along the dimension named above; an argument that names none is the same for every part. Nothing has to cross between parts.
All inputs are finite; a program needn't handle non-finite values.
Results may differ from the reference program's by a relative error of at most 0.012.
The reference program's roundings to bfloat16 on the way count: a program that leaves them out, or rounds other values in their place, can miss the bound.
Values may be sent and summed in bfloat16 or wider, within the bound.
No kernel may reach another device: no remote copies, remote signals or barrier semaphores. Data moves between devices by JAX's collectives and lax.ppermute only.
A program may use at most 64 MiB of HBM per device.

```python
import math
import jax
import jax.numpy as jnp
from jax import lax

D = 1024
HEADS = 8
KERNEL = 9
HD = 128
TOKENS = 1024


def draw_frames(key, part):
    base = jnp.clip(jax.random.normal(jax.random.fold_in(key, 1), (TOKENS, D), jnp.float32), -4.0, 4.0)
    row_scale = jnp.exp(jax.random.uniform(jax.random.fold_in(key, 2), (TOKENS, 1), jnp.float32, math.log(0.3), math.log(3.0)))
    col_scale = jnp.exp(jax.random.uniform(jax.random.fold_in(key, 3), (1, D), jnp.float32, math.log(0.3), math.log(3.0)))
    return jnp.clip(base * row_scale * col_scale, -24.0, 24.0).astype(jnp.bfloat16)


def paired_weights(key):
    spread = 1.57 * D ** (-0.5)
    edge = 0.19921875
    query_part = jnp.clip(jax.random.normal(jax.random.fold_in(key, 11), (D, D), jnp.float32) * spread, -edge, edge)
    other_part = jnp.clip(jax.random.normal(jax.random.fold_in(key, 12), (D, D), jnp.float32) * spread, -edge, edge)
    key_part = other_part
    return (query_part, key_part)


def draw_w_query(key, part):
    query_part, key_part = paired_weights(key)
    return query_part.astype(jnp.bfloat16)


def draw_w_key(key, part):
    query_part, key_part = paired_weights(key)
    return key_part.astype(jnp.bfloat16)


def shard_levels(key, dims, cuts, least, largest):
    level, own = 1.0, jax.random.fold_in(key, 6)
    for axis_at, blocks in cuts:
        steps = jnp.exp(jax.random.uniform(jax.random.fold_in(own, axis_at), (blocks,), jnp.float32, least / len(cuts), largest / len(cuts)))
        level = level * jnp.repeat(steps, dims[axis_at] // blocks).reshape([-1 if axis == axis_at else 1 for axis in range(len(dims))])
    return level


def centred(rng, shape, deviation, most, cuts=(), held_as=jnp.bfloat16):
    array = jax.random.normal(rng, shape, jnp.float32) * deviation
    if len(cuts) > 0:
        array = shard_levels(rng, shape, cuts, -0.22, 0.18) * array
    return jnp.clip(array, min=-most, max=most).astype(held_as)


def setup_inputs(seed: int = 0, part: int = 0) -> dict:
    streams_of = jax.random.split(jax.random.key(seed), 15)
    own_keys = jax.random.split(jax.random.fold_in(streams_of[14], part), 15)
    return {
        "frames": draw_frames(jax.random.fold_in(jax.random.fold_in(streams_of[14], part), 71), part),
        "length": jax.random.randint(own_keys[1], (1,), TOKENS // 2, TOKENS + 1).astype(jnp.int32),
        "ln1_gain": jnp.clip(1.0 + 0.18 * jax.random.normal(streams_of[2], (D,), jnp.float32), 0.1, 1.9),
        "w_query": draw_w_query(jax.random.fold_in(streams_of[14], 71), part),
        "w_key": draw_w_key(jax.random.fold_in(streams_of[14], 71), part),
        "w_value": centred(streams_of[5], (D, D), (D // 4) ** -0.5, 0.375, ((0, 4), (1, 4))),
        "w_out": centred(streams_of[6], (D, D), D ** -0.5, 0.1875, ((0, 4), (1, 4))),
        "ln2_gain": jnp.clip(1.0 + 0.18 * jax.random.normal(streams_of[7], (D,), jnp.float32), 0.1, 1.9),
        "pw1_value": centred(streams_of[8], (D, D), D ** -0.5, 0.1875, ((0, 4), (1, 4))),
        "pw1_gate": centred(streams_of[9], (D, D), (D // 4) ** -0.5, 0.375, ((0, 4), (1, 4))),
        "depth_kernel": centred(streams_of[10], (KERNEL, D), KERNEL ** -0.5, 2.0, ((1, 4),), jnp.float32),
        "bn_scale": jnp.clip(1.0 + 0.18 * jax.random.normal(streams_of[11], (D,), jnp.float32), 0.1, 1.9),
        "bn_shift": centred(streams_of[12], (D,), 0.5, 3.0, ((0, 4),), jnp.float32),
        "pw2": centred(streams_of[13], (D, D), D ** -0.5, 0.1875, ((0, 4), (1, 4))),
    }


def layer_norm(values_in, gain_vec):
    center = lax.optimization_barrier(jnp.mean(values_in, axis=-1, keepdims=True))
    shifted = values_in - center
    spread = lax.optimization_barrier(jnp.mean(shifted * shifted, axis=-1, keepdims=True))
    return shifted * lax.rsqrt(spread + 1e-05) * gain_vec

def reference(frames, length, ln1_gain, w_query, w_key, w_value, w_out, ln2_gain, pw1_value, pw1_gate, depth_kernel, bn_scale, bn_shift, pw2):
    source = frames.astype(jnp.float32)
    normed = layer_norm(source, ln1_gain).astype(jnp.bfloat16)
    queries = jnp.dot(normed, w_query, preferred_element_type=jnp.float32).astype(jnp.bfloat16)
    keys_all = jnp.dot(normed, w_key, preferred_element_type=jnp.float32).astype(jnp.bfloat16)
    values_all = jnp.dot(normed, w_value, preferred_element_type=jnp.float32).astype(jnp.bfloat16)
    places = jnp.arange(TOKENS, dtype=jnp.int32)
    valid = places < length[0]
    block_size = math.gcd(TOKENS, 512)
    block_count = TOKENS // block_size
    score_scale = 1.0 / math.sqrt(HD)
    head_keys = keys_all.astype(jnp.float32).reshape(TOKENS, HEADS, HD).transpose(1, 0, 2)
    head_values = values_all.astype(jnp.float32).reshape(TOKENS, HEADS, HD).transpose(1, 0, 2)
    head_queries = queries.astype(jnp.float32).reshape(block_count, block_size, HEADS, HD)

    def one_block(query_block):
        scores = jnp.einsum('qhd,hkd->hqk', query_block, head_keys) * score_scale
        scores = jnp.where(valid[None, None, :], scores, -jnp.inf)
        row_peak = lax.optimization_barrier(jnp.max(scores, axis=2, keepdims=True))
        weights = jnp.exp(scores - row_peak)
        weight_sum = lax.optimization_barrier(jnp.sum(weights, axis=2))
        rounded = lax.optimization_barrier(weights.astype(jnp.bfloat16)).astype(jnp.float32)
        context = jnp.einsum('hqk,hkd->qhd', rounded, head_values) / weight_sum.transpose(1, 0)[:, :, None]
        return context.astype(jnp.bfloat16)
    blocks = lax.map(one_block, head_queries)
    context = blocks.reshape(TOKENS, D)
    middle = source + jnp.dot(context, w_out, preferred_element_type=jnp.float32)
    normed_two = layer_norm(middle, ln2_gain).astype(jnp.bfloat16)
    value_part = jnp.dot(normed_two, pw1_value, preferred_element_type=jnp.float32)
    gate_part = jnp.dot(normed_two, pw1_gate, preferred_element_type=jnp.float32)
    gated = jnp.where(valid[:, None], value_part * jax.nn.sigmoid(gate_part), 0.0).astype(jnp.bfloat16)
    rim_width = (KERNEL - 1) // 2
    padded = jnp.pad(gated.astype(jnp.float32), ((rim_width, rim_width), (0, 0)))
    depth_sum = depth_kernel[0] * padded[0:TOKENS]
    for offset in range(1, KERNEL):
        depth_sum = depth_sum + depth_kernel[offset] * padded[offset:offset + TOKENS]
    shifted = depth_sum * bn_scale + bn_shift
    active = (shifted * jax.nn.sigmoid(shifted)).astype(jnp.bfloat16)
    return (middle + jnp.dot(active, pw2, preferred_element_type=jnp.float32)).astype(jnp.bfloat16)
```

```python
import math

import jax
import jax.numpy as jnp
from jax import lax
from jax.experimental import pallas as pl
from jax.experimental.pallas import tpu as pltpu
from jax.sharding import PartitionSpec as P

KERNEL = 9
HD = 128


def with_halo(block, sides, width):
    for axis, dim in sides:
        count = lax.axis_size(axis)
        forward = [(i, i + 1) for i in range(count - 1)]
        backward = [(target, source) for source, target in forward]
        low = lax.ppermute(
            lax.slice_in_dim(block, block.shape[dim] - width, None, axis=dim), axis, forward
        )
        high = lax.ppermute(lax.slice_in_dim(block, 0, width, axis=dim), axis, backward)
        block = jnp.concatenate([low, block, high], axis=dim)
    return block


def layer_norm(values_in, gain_vec):
    center = jnp.mean(values_in, axis=-1, keepdims=True)
    shifted = values_in - center
    spread = jnp.mean(shifted * shifted, axis=-1, keepdims=True)
    return shifted * lax.rsqrt(spread + 1e-05) * gain_vec


def shards_general(
    frames,
    length,
    ln1_gain,
    w_query,
    w_key,
    w_value,
    w_out,
    ln2_gain,
    pw1_value,
    pw1_gate,
    depth_kernel,
    bn_scale,
    bn_shift,
    pw2,
):
    group_size = lax.axis_size(("head", "fsdp"))
    my_rows = frames.shape[0]
    block_rows = my_rows * group_size
    head_cols = w_query.shape[1]
    heads_here = head_cols // HD
    seq_start = lax.axis_index("seq") * block_rows
    valid_len = length[0]
    score_scale = 1.0 / math.sqrt(HD)
    full_query, full_key, full_value, value_cols, gate_cols = (
        lax.all_gather(w_query, "seq", axis=0, tiled=True),
        lax.all_gather(w_key, "seq", axis=0, tiled=True),
        lax.all_gather(w_value, "seq", axis=0, tiled=True),
        lax.all_gather(pw1_value, "seq", axis=0, tiled=True),
        lax.all_gather(pw1_gate, "seq", axis=0, tiled=True),
    )
    out_rows, down_rows = (
        lax.all_gather(w_out, "seq", axis=1, tiled=True),
        lax.all_gather(pw2, "seq", axis=1, tiled=True),
    )
    projector = jnp.concatenate((full_query, full_key, full_value), axis=1)
    source = frames.astype(jnp.float32)
    normed = layer_norm(source, ln1_gain).astype(jnp.bfloat16)
    projected = jnp.dot(
        lax.all_gather(normed, ("head", "fsdp"), axis=0, tiled=True),
        projector,
        preferred_element_type=jnp.float32,
    ).astype(jnp.bfloat16)
    queries = projected[:, :head_cols].reshape(block_rows, heads_here, HD)
    keys_here = projected[:, head_cols : 2 * head_cols]
    values_here = projected[:, 2 * head_cols :]
    initial = (
        jnp.full((heads_here, block_rows), -1e30, jnp.float32),
        jnp.zeros((heads_here, block_rows), jnp.float32),
        jnp.zeros((heads_here, block_rows, HD), jnp.float32),
    )
    key_piece = lax.all_gather(keys_here, "seq", axis=0, tiled=True)
    value_piece = lax.all_gather(values_here, "seq", axis=0, tiled=True)
    row_count = key_piece.shape[0]
    block_size = math.gcd(row_count, 512)
    block_count = row_count // block_size
    key_blocks = key_piece.reshape(block_count, block_size, heads_here, HD)
    value_blocks = value_piece.reshape(block_count, block_size, heads_here, HD)
    places = jnp.arange(row_count, dtype=jnp.int32).reshape(block_count, block_size)

    def advance(inner_state, block_item):
        key_block, value_block, place = block_item
        peak_score, weight_sum, weighted = inner_state
        scores = (
            jnp.einsum("qhd,khd->hqk", queries, key_block, preferred_element_type=jnp.float32)
            * score_scale
        )
        scores = jnp.where((place < valid_len)[None, None, :], scores, -jnp.inf)
        new_peak = jnp.maximum(peak_score, jnp.max(scores, axis=2))
        factor = jnp.exp(peak_score - new_peak)
        weights = jnp.exp(scores - new_peak[:, :, None])
        weight_sum = weight_sum * factor + jnp.sum(weights, axis=2)
        weighted = weighted * factor[:, :, None] + jnp.einsum(
            "hqk,khd->hqd",
            weights.astype(jnp.bfloat16),
            value_block,
            preferred_element_type=jnp.float32,
        )
        return ((new_peak, weight_sum, weighted), None)

    result, unused = lax.scan(advance, initial, (key_blocks, value_blocks, places))
    peak_score, weight_sum, weighted = result
    context = (
        (weighted / weight_sum[:, :, None])
        .astype(jnp.bfloat16)
        .transpose(1, 0, 2)
        .reshape(block_rows, head_cols)
    )
    attended = lax.psum_scatter(
        jnp.dot(context, out_rows, preferred_element_type=jnp.float32).astype(jnp.bfloat16),
        ("head", "fsdp"),
        scatter_dimension=0,
        tiled=True,
    ).astype(jnp.float32)
    middle = source + attended
    normed_two = layer_norm(middle, ln2_gain).astype(jnp.bfloat16)
    piece = lax.all_gather(normed_two, ("head", "fsdp"), axis=0, tiled=True)
    value_part = jnp.dot(piece, value_cols, preferred_element_type=jnp.float32)
    gate_part = jnp.dot(piece, gate_cols, preferred_element_type=jnp.float32)
    places = seq_start + jnp.arange(piece.shape[0], dtype=jnp.int32)
    gated_rows = jnp.where(
        (places < valid_len)[:, None], value_part * jax.nn.sigmoid(gate_part), 0.0
    ).astype(jnp.bfloat16)
    rim_width = (KERNEL - 1) // 2
    padded = with_halo(gated_rows, (("seq", 0),), rim_width).astype(jnp.float32)
    depth_sum = depth_kernel[0] * padded[0:block_rows]
    for offset in range(1, KERNEL):
        depth_sum = depth_sum + depth_kernel[offset] * padded[offset : offset + block_rows]
    shifted = depth_sum * bn_scale + bn_shift
    active = (shifted * jax.nn.sigmoid(shifted)).astype(jnp.bfloat16)
    conv_part = lax.psum_scatter(
        jnp.dot(active, down_rows, preferred_element_type=jnp.float32).astype(jnp.bfloat16),
        ("head", "fsdp"),
        scatter_dimension=0,
        tiled=True,
    ).astype(jnp.float32)
    return (middle + conv_part).astype(jnp.bfloat16)


SEQ = 4
EDGE = (KERNEL - 1) // 2
HALO = 2 * EDGE
SWAP = [(0, 1), (1, 0)]
F32 = jnp.float32
BF16 = jnp.bfloat16


def one_head_per_chip(mesh):
    return dict(mesh.shape) == {"parts": 2, "seq": SEQ, "head": 2, "fsdp": 2}


def xor_pairs(k):
    return [(i, i ^ k) for i in range(SEQ)]


def call(kernel, outs, scratch, places, *operands, flops=0):
    moved = sum(math.prod(a.shape) * a.dtype.itemsize for a in (*operands, *outs))
    return pl.pallas_call(
        kernel,
        out_shape=outs,
        in_specs=[pl.BlockSpec(memory_space=pltpu.SMEM)]
        + [pl.BlockSpec(memory_space=pltpu.VMEM)] * len(operands),
        out_specs=[pl.BlockSpec(memory_space=pltpu.VMEM)] * len(outs),
        scratch_shapes=scratch,
        cost_estimate=pl.CostEstimate(flops=flops, bytes_accessed=moved, transcendentals=0),
        compiler_params=pltpu.CompilerParams(vmem_limit_bytes=40 << 20),
    )(places, *operands)


def aligned(value, to):
    return pl.multiple_of(value, to)


def dot(a, b):
    return jnp.dot(a, b, preferred_element_type=F32)


def project_kernel(places, *refs):
    blocks = refs[: 2 * SEQ]
    gain, mine, other, q_out, send_out, edge_out, normed, weights, x_edge, q_edge = refs[2 * SEQ :]
    s, h, f = places[0], places[1], places[2]
    rows = blocks[0].shape[0]
    half = mine.shape[2]
    gain_row = gain[...]
    for slot, block in enumerate(blocks):
        at = (s ^ (slot // 2)) * 2 + (h ^ (slot % 2))
        x = block[...].astype(F32)
        normed[pl.ds(aligned(at * rows, rows), rows), :] = layer_norm(x, gain_row).astype(BF16)
        x_edge[at, 0:EDGE, :] = x[:EDGE]
        x_edge[at, EDGE:HALO, :] = x[rows - EDGE :]
    for source in range(SEQ):
        for m in range(3):
            columns = slice(m * HD, (m + 1) * HD)
            at = source * 2 * half
            weights[pl.ds(aligned(at + f * half, half), half), columns] = mine[source, m]
            weights[pl.ds(aligned(at + (1 - f) * half, half), half), columns] = other[source, m]
    count = 2 * SEQ
    total = count * rows
    projected = dot(normed[...], weights[...])
    q_out[...] = projected[:, :HD].astype(BF16)
    send_out[0:total, :] = projected[:, HD : 2 * HD].astype(BF16)
    send_out[total : 2 * total, :] = projected[:, 2 * HD :].astype(BF16)
    for b in range(count):
        q_edge[b, 0:EDGE, :] = projected[b * rows : b * rows + EDGE, :HD]
        q_edge[b, EDGE:HALO, :] = projected[(b + 1) * rows - EDGE : (b + 1) * rows, :HD]

    def around(edge, b):
        low = jnp.maximum(b - f, 0)
        high = jnp.minimum(b + 1 - f, count - 1)
        return jnp.concatenate([edge[low, EDGE:HALO, :], edge[high, 0:EDGE, :]], axis=0)

    halos = jnp.concatenate([around(q_edge, b) for b in range(count)], axis=0)
    send_out[2 * total :, :] = halos.astype(BF16)
    edge_out[...] = around(x_edge, s * 2 + h).astype(BF16)


def attend_kernel(places, q_in, own, peer, ctx_out, q_rows):
    f, valid_len = places[2], places[4]
    count = ctx_out.shape[0]
    total = q_in.shape[0]
    rows = total // count
    step = ctx_out.shape[1]
    local = lax.broadcasted_iota(jnp.int32, (step, total), 1)
    base = (local // rows) * (2 * rows) + local % rows
    keep_own = base + f * rows < valid_len
    keep_peer = base + (1 - f) * rows < valid_len
    scale = 1.0 / math.sqrt(HD)
    keys_t = (((1,), (1,)), ((), ()))
    for b in range(count):
        q_rows[b, 0:rows, :] = q_in[b * rows : (b + 1) * rows, :].astype(F32)
        q_rows[b, rows:step, :] = peer[2 * total + b * HALO : 2 * total + (b + 1) * HALO, :].astype(F32)
    for b in range(count):
        q = q_rows[b].astype(BF16)
        first = lax.dot_general(q, own[0:total, :], keys_t, preferred_element_type=F32) * scale
        second = lax.dot_general(q, peer[0:total, :], keys_t, preferred_element_type=F32) * scale
        first = jnp.where(keep_own, first, -jnp.inf)
        second = jnp.where(keep_peer, second, -jnp.inf)
        peak = jnp.maximum(
            jnp.max(first, axis=1, keepdims=True), jnp.max(second, axis=1, keepdims=True)
        )
        first = jnp.exp(first - peak)
        second = jnp.exp(second - peak)
        weight_sum = jnp.sum(first, axis=1, keepdims=True) + jnp.sum(second, axis=1, keepdims=True)
        weighted = dot(first.astype(BF16), own[total : 2 * total, :]) + dot(
            second.astype(BF16), peer[total : 2 * total, :]
        )
        ctx_out[b] = (weighted / weight_sum).astype(BF16)


def middle_kernel(places, *refs):
    gathered = refs[: 4 * SEQ]
    far_mine, far_other, ctx, own_x, halo_x, gain, middle_out, norm_out, context, weights, mid = refs[4 * SEQ :]
    s, h, f, p = places[0], places[1], places[2], places[3]
    rows = own_x.shape[0]
    step = ctx.shape[1]
    half = far_mine.shape[1]

    def put(k, y, core, side, value):
        at = (2 * (h ^ side) + (f ^ core)) * 2 * half + (p ^ y) * half
        weights[s ^ k, pl.ds(aligned(at, half), half), :] = value

    for k in range(SEQ):
        for y in range(2):
            for core in range(2):
                put(k, y, core, 0, gathered[(k * 2 + y) * 2 + core][0])
            put(k, y, 0, 1, far_mine[k * 2 + y])
            put(k, y, 1, 1, far_other[k * 2 + y])
    for g in range(2 * SEQ):
        head = (g % 2) * SEQ + g // 2
        context[:, head * HD : (head + 1) * HD] = ctx[g]
    columns = weights.shape[2]
    mid[0:rows, :] = own_x[...].astype(F32)
    mid[rows:step, :] = halo_x[...].astype(F32)
    for j in range(SEQ):
        at = slice(j * columns, (j + 1) * columns)
        mid[:, at] = mid[:, at] + dot(context[...], weights[j])
    middle = mid[...]
    middle_out[...] = middle[:rows]
    norm_out[...] = layer_norm(middle, gain[...]).astype(BF16)


def convolve_kernel(places, *refs):
    gathered = refs[: 4 * SEQ]
    own_n, peer_n, own_c, peer_c, middle, base_out, share_out = refs[4 * SEQ : 4 * SEQ + 7]
    normed, w_value, w_gate, w_down, channel, padded, active = refs[4 * SEQ + 7 :]
    s, h, f, p, valid_len = places[0], places[1], places[2], places[3], places[4]
    half, columns = gathered[0].shape[1:]
    step = own_n.shape[0]
    rows = step - HALO
    for k in range(SEQ):
        for y in range(2):
            for core in range(2):
                stack = gathered[(k * 2 + y) * 2 + core]
                at = pl.ds(aligned((s ^ k) * 2 * half + (p ^ y) * half, half), half)
                w_value[f ^ core, at, :] = stack[1]
                w_gate[f ^ core, at, :] = stack[2]
                at = pl.ds(aligned((f ^ core) * 2 * half + (p ^ y) * half, half), half)
                w_down[s ^ k, at, :] = stack[3]
    channel[f] = own_c[...]
    channel[1 - f] = peer_c[...]
    normed[0:step, :] = own_n[...]
    normed[step : 2 * step, :] = peer_n[...]
    place = lax.broadcasted_iota(jnp.int32, (step, columns), 0)
    offset = jnp.where(place < rows, place, jnp.where(place < rows + EDGE, place - rows - EDGE, place - EDGE))
    for c in range(2):
        x = normed[...]
        value_part = dot(x, w_value[c])
        gate_part = dot(x, w_gate[c])
        gated = value_part * jax.nn.sigmoid(gate_part)
        for b in range(2):
            start = (4 * s + 2 * (h ^ b) + f) * rows
            t = offset + start
            kept = jnp.where((t >= 0) & (t < valid_len), gated[b * step : (b + 1) * step], 0.0)
            kept = kept.astype(BF16).astype(F32)
            padded[b, 8 : 8 + rows, :] = kept[:rows]
            padded[b, 8 - EDGE : 8, :] = kept[rows : rows + EDGE]
            padded[b, 8 + rows : 8 + rows + EDGE, :] = kept[rows + EDGE :]
            depth_sum = channel[c, 0:1, :] * padded[b, 8 - EDGE : 8 - EDGE + rows, :]
            for j in range(1, KERNEL):
                low = 8 - EDGE + j
                depth_sum = depth_sum + channel[c, j : j + 1, :] * padded[b, low : low + rows, :]
            shifted = depth_sum * channel[c, KERNEL : KERNEL + 1, :] + channel[c, KERNEL + 1 : KERNEL + 2, :]
            active[b * rows : (b + 1) * rows, c * columns : (c + 1) * columns] = (
                shifted * jax.nn.sigmoid(shifted)
            ).astype(BF16)
    for j in range(SEQ):
        at = slice(j * columns, (j + 1) * columns)
        share = dot(active[...], w_down[j])
        base_out[:, at] = middle[:, at] + share[:rows]
        share_out[:, at] = share[rows:].astype(BF16)


def shards_chip_per_head(
    frames,
    length,
    ln1_gain,
    w_query,
    w_key,
    w_value,
    w_out,
    ln2_gain,
    pw1_value,
    pw1_gate,
    depth_kernel,
    bn_scale,
    bn_shift,
    pw2,
):
    rows, width = frames.shape
    count = 2 * SEQ
    step = rows + HALO
    s, h, f, p = (lax.axis_index(a) for a in ("seq", "head", "fsdp", "parts"))
    places = jnp.stack([s, h, f, p, length[0]]).astype(jnp.int32)
    half = w_query.shape[0] // 2
    columns = w_query.shape[1]

    def other_core(x):
        return lax.ppermute(x, "fsdp", SWAP)

    def other_side(x):
        return lax.ppermute(x, "head", SWAP)

    projectors = jnp.stack([w_query, w_key, w_value])
    keep = lax.dynamic_slice_in_dim(projectors, f * half, half, axis=1)
    give = lax.dynamic_slice_in_dim(projectors, (1 - f) * half, half, axis=1)
    got = other_core(give)
    low = jnp.where(f == 0, keep, got)
    high = jnp.where(f == 0, got, keep)
    by_head = jnp.stack([low[:, :, :HD], low[:, :, HD:], high[:, :, :HD], high[:, :, HD:]])
    w_mine = lax.all_to_all(by_head, "seq", 0, 0, tiled=True)
    w_other = other_core(w_mine)
    blocks = []
    for k in range(SEQ):
        block = frames if k == 0 else lax.ppermute(frames, "seq", xor_pairs(k))
        blocks += [block, other_side(block)]
    stack = jnp.stack([w_out, pw1_value, pw1_gate, pw2])
    stack = lax.dynamic_slice_in_dim(stack, p * half, half, axis=1)
    gathered = []
    for k in range(SEQ):
        near = stack if k == 0 else lax.ppermute(stack, "seq", xor_pairs(k))
        for part in (near, lax.ppermute(near, "parts", SWAP)):
            gathered += [part, other_core(part)]
    far_mine = other_side(jnp.stack([a[0] for a in gathered[::2]]))
    far_other = other_core(far_mine)
    channels = jnp.concatenate([depth_kernel, bn_scale[None], bn_shift[None], jnp.zeros((5, columns), F32)])
    channels_peer = other_core(channels)

    shape = jax.ShapeDtypeStruct
    queries, send, edges = call(
        project_kernel,
        [
            shape((count * rows, HD), BF16),
            shape((2 * count * rows + count * HALO, HD), BF16),
            shape((HALO, width), BF16),
        ],
        [
            pltpu.VMEM((count * rows, width), BF16),
            pltpu.VMEM((width, 3 * HD), BF16),
            pltpu.VMEM((count, HALO, width), F32),
            pltpu.VMEM((count, HALO, HD), F32),
        ],
        places,
        *blocks,
        ln1_gain[None],
        w_mine,
        w_other,
        flops=6 * count * rows * width * HD,
    )
    received = other_core(send)
    halo_x = other_core(edges)
    (ctx,) = call(
        attend_kernel,
        [shape((count, step, HD), BF16)],
        [pltpu.VMEM((count, step, HD), F32)],
        places,
        queries,
        send,
        received,
        flops=8 * count * step * count * rows * HD,
    )
    ctx = lax.all_to_all(ctx, ("seq", "head"), 0, 0, tiled=True)
    middle, normed = call(
        middle_kernel,
        [shape((rows, width), F32), shape((step, width), BF16)],
        [
            pltpu.VMEM((step, width), BF16),
            pltpu.VMEM((SEQ, width, columns), BF16),
            pltpu.VMEM((step, width), F32),
        ],
        places,
        *gathered,
        far_mine,
        far_other,
        ctx,
        frames,
        halo_x,
        ln2_gain[None],
        flops=2 * step * width * width,
    )
    base, share = call(
        convolve_kernel,
        [shape((rows, width), F32), shape((rows, width), BF16)],
        [
            pltpu.VMEM((2 * step, width), BF16),
            pltpu.VMEM((2, width, columns), BF16),
            pltpu.VMEM((2, width, columns), BF16),
            pltpu.VMEM((SEQ, 2 * columns, columns), BF16),
            pltpu.VMEM((2, 16, columns), F32),
            pltpu.VMEM((2, 16 + rows, columns), F32),
            pltpu.VMEM((2 * rows, 2 * columns), BF16),
        ],
        places,
        *gathered,
        normed,
        other_side(normed),
        channels,
        channels_peer,
        middle,
        flops=6 * step * width * width,
    )
    return (base + other_side(share).astype(F32)).astype(BF16)


def solution(mesh):
    in_specs = (
        P(("parts", "seq", "head", "fsdp"), None),
        P("parts"),
        P(),
        P("seq", ("head", "fsdp")),
        P("seq", ("head", "fsdp")),
        P("seq", ("head", "fsdp")),
        P(("head", "fsdp"), "seq"),
        P(),
        P("seq", ("head", "fsdp")),
        P("seq", ("head", "fsdp")),
        P(None, ("head", "fsdp")),
        P(("head", "fsdp")),
        P(("head", "fsdp")),
        P(("head", "fsdp"), "seq"),
    )
    out_specs = P(("parts", "seq", "head", "fsdp"), None)
    body = shards_chip_per_head if one_head_per_chip(mesh) else shards_general
    return jax.shard_map(body, mesh=mesh, in_specs=in_specs, out_specs=out_specs, check_vma=False)
```

```python
import math

import jax
import jax.numpy as jnp
from jax import lax
from jax.experimental import pallas as pl
from jax.experimental.pallas import tpu as pltpu
from jax.sharding import PartitionSpec as P

KERNEL = 9
HD = 128


def with_halo(block, sides, width):
    for axis, dim in sides:
        count = lax.axis_size(axis)
        forward = [(i, i + 1) for i in range(count - 1)]
        backward = [(target, source) for source, target in forward]
        low = lax.ppermute(
            lax.slice_in_dim(block, block.shape[dim] - width, None, axis=dim), axis, forward
        )
        high = lax.ppermute(lax.slice_in_dim(block, 0, width, axis=dim), axis, backward)
        block = jnp.concatenate([low, block, high], axis=dim)
    return block


def layer_norm(values_in, gain_vec):
    center = jnp.mean(values_in, axis=-1, keepdims=True)
    shifted = values_in - center
    spread = jnp.mean(shifted * shifted, axis=-1, keepdims=True)
    return shifted * lax.rsqrt(spread + 1e-05) * gain_vec


def shards_general(
    frames,
    length,
    ln1_gain,
    w_query,
    w_key,
    w_value,
    w_out,
    ln2_gain,
    pw1_value,
    pw1_gate,
    depth_kernel,
    bn_scale,
    bn_shift,
    pw2,
):
    group_size = lax.axis_size(("head", "fsdp"))
    my_rows = frames.shape[0]
    block_rows = my_rows * group_size
    head_cols = w_query.shape[1]
    heads_here = head_cols // HD
    seq_start = lax.axis_index("seq") * block_rows
    valid_len = length[0]
    score_scale = 1.0 / math.sqrt(HD)
    full_query, full_key, full_value, value_cols, gate_cols = (
        lax.all_gather(w_query, "seq", axis=0, tiled=True),
        lax.all_gather(w_key, "seq", axis=0, tiled=True),
        lax.all_gather(w_value, "seq", axis=0, tiled=True),
        lax.all_gather(pw1_value, "seq", axis=0, tiled=True),
        lax.all_gather(pw1_gate, "seq", axis=0, tiled=True),
    )
    out_rows, down_rows = (
        lax.all_gather(w_out, "seq", axis=1, tiled=True),
        lax.all_gather(pw2, "seq", axis=1, tiled=True),
    )
    projector = jnp.concatenate((full_query, full_key, full_value), axis=1)
    source = frames.astype(jnp.float32)
    normed = layer_norm(source, ln1_gain).astype(jnp.bfloat16)
    projected = jnp.dot(
        lax.all_gather(normed, ("head", "fsdp"), axis=0, tiled=True),
        projector,
        preferred_element_type=jnp.float32,
    ).astype(jnp.bfloat16)
    queries = projected[:, :head_cols].reshape(block_rows, heads_here, HD)
    keys_here = projected[:, head_cols : 2 * head_cols]
    values_here = projected[:, 2 * head_cols :]
    initial = (
        jnp.full((heads_here, block_rows), -1e30, jnp.float32),
        jnp.zeros((heads_here, block_rows), jnp.float32),
        jnp.zeros((heads_here, block_rows, HD), jnp.float32),
    )
    key_piece = lax.all_gather(keys_here, "seq", axis=0, tiled=True)
    value_piece = lax.all_gather(values_here, "seq", axis=0, tiled=True)
    row_count = key_piece.shape[0]
    block_size = math.gcd(row_count, 512)
    block_count = row_count // block_size
    key_blocks = key_piece.reshape(block_count, block_size, heads_here, HD)
    value_blocks = value_piece.reshape(block_count, block_size, heads_here, HD)
    places = jnp.arange(row_count, dtype=jnp.int32).reshape(block_count, block_size)

    def advance(inner_state, block_item):
        key_block, value_block, place = block_item
        peak_score, weight_sum, weighted = inner_state
        scores = (
            jnp.einsum("qhd,khd->hqk", queries, key_block, preferred_element_type=jnp.float32)
            * score_scale
        )
        scores = jnp.where((place < valid_len)[None, None, :], scores, -jnp.inf)
        new_peak = jnp.maximum(peak_score, jnp.max(scores, axis=2))
        factor = jnp.exp(peak_score - new_peak)
        weights = jnp.exp(scores - new_peak[:, :, None])
        weight_sum = weight_sum * factor + jnp.sum(weights, axis=2)
        weighted = weighted * factor[:, :, None] + jnp.einsum(
            "hqk,khd->hqd",
            weights.astype(jnp.bfloat16),
            value_block,
            preferred_element_type=jnp.float32,
        )
        return ((new_peak, weight_sum, weighted), None)

    result, unused = lax.scan(advance, initial, (key_blocks, value_blocks, places))
    peak_score, weight_sum, weighted = result
    context = (
        (weighted / weight_sum[:, :, None])
        .astype(jnp.bfloat16)
        .transpose(1, 0, 2)
        .reshape(block_rows, head_cols)
    )
    attended = lax.psum_scatter(
        jnp.dot(context, out_rows, preferred_element_type=jnp.float32).astype(jnp.bfloat16),
        ("head", "fsdp"),
        scatter_dimension=0,
        tiled=True,
    ).astype(jnp.float32)
    middle = source + attended
    normed_two = layer_norm(middle, ln2_gain).astype(jnp.bfloat16)
    piece = lax.all_gather(normed_two, ("head", "fsdp"), axis=0, tiled=True)
    value_part = jnp.dot(piece, value_cols, preferred_element_type=jnp.float32)
    gate_part = jnp.dot(piece, gate_cols, preferred_element_type=jnp.float32)
    places = seq_start + jnp.arange(piece.shape[0], dtype=jnp.int32)
    gated_rows = jnp.where(
        (places < valid_len)[:, None], value_part * jax.nn.sigmoid(gate_part), 0.0
    ).astype(jnp.bfloat16)
    rim_width = (KERNEL - 1) // 2
    padded = with_halo(gated_rows, (("seq", 0),), rim_width).astype(jnp.float32)
    depth_sum = depth_kernel[0] * padded[0:block_rows]
    for offset in range(1, KERNEL):
        depth_sum = depth_sum + depth_kernel[offset] * padded[offset : offset + block_rows]
    shifted = depth_sum * bn_scale + bn_shift
    active = (shifted * jax.nn.sigmoid(shifted)).astype(jnp.bfloat16)
    conv_part = lax.psum_scatter(
        jnp.dot(active, down_rows, preferred_element_type=jnp.float32).astype(jnp.bfloat16),
        ("head", "fsdp"),
        scatter_dimension=0,
        tiled=True,
    ).astype(jnp.float32)
    return (middle + conv_part).astype(jnp.bfloat16)


SEQ = 4
EDGE = (KERNEL - 1) // 2
HALO = 2 * EDGE
SWAP = [(0, 1), (1, 0)]
F32 = jnp.float32
BF16 = jnp.bfloat16


def one_head_per_chip(mesh):
    return dict(mesh.shape) == {"parts": 2, "seq": SEQ, "head": 2, "fsdp": 2}


def xor_pairs(k):
    return [(i, i ^ k) for i in range(SEQ)]


def call(kernel, outs, scratch, length, *operands, flops=0, vmem=8):
    moved = sum(math.prod(a.shape) * a.dtype.itemsize for a in (*operands, *outs))
    return pl.pallas_call(
        kernel,
        out_shape=outs,
        in_specs=[pl.BlockSpec(memory_space=pltpu.SMEM)]
        + [pl.BlockSpec(memory_space=pltpu.VMEM)] * len(operands),
        out_specs=[pl.BlockSpec(memory_space=pltpu.VMEM)] * len(outs),
        scratch_shapes=scratch,
        cost_estimate=pl.CostEstimate(flops=flops, bytes_accessed=moved, transcendentals=0),
        compiler_params=pltpu.CompilerParams(vmem_limit_bytes=vmem << 20),
    )(length, *operands)


def aligned(value, to):
    return pl.multiple_of(value, to)


def dot(a, b):
    return jnp.dot(a, b, preferred_element_type=F32)


def here():
    return tuple(lax.axis_index(a) for a in ("seq", "head", "fsdp", "parts"))


def project_kernel(length, *refs):
    blocks = refs[: 2 * SEQ]
    mine, other = refs[2 * SEQ : 3 * SEQ], refs[3 * SEQ : 4 * SEQ]
    gain, q_out, send_out, edge_out, normed, weights, x_edge, q_edge = refs[4 * SEQ :]
    s, h, f, _ = here()
    rows = blocks[0].shape[0]
    depth = mine[0].shape[1]
    gain_row = gain[...]
    for slot, block in enumerate(blocks):
        at = (s ^ (slot // 2)) * 2 + (h ^ (slot % 2))
        x = block[...].astype(F32)
        normed[pl.ds(aligned(at * rows, rows), rows), :] = layer_norm(x, gain_row).astype(BF16)
        x_edge[at, 0:EDGE, :] = x[:EDGE]
        x_edge[at, EDGE:HALO, :] = x[rows - EDGE :]
    def fill(pieces):
        for k in range(SEQ):
            at = pl.ds(aligned((s ^ k) * depth, depth), depth)
            for m in range(3):
                weights[at, m * HD : (m + 1) * HD] = pieces[k][m]

    @pl.when(s // 2 == f)
    def _():
        fill(mine)

    @pl.when(s // 2 != f)
    def _():
        fill(other)

    count = 2 * SEQ
    total = count * rows
    projected = dot(normed[...], weights[...])
    q_out[...] = projected[:, :HD].astype(BF16)
    send_out[0:total, :] = projected[:, HD : 2 * HD].astype(BF16)
    send_out[total : 2 * total, :] = projected[:, 2 * HD :].astype(BF16)
    for b in range(count):
        q_edge[b, 0:EDGE, :] = projected[b * rows : b * rows + EDGE, :HD]
        q_edge[b, EDGE:HALO, :] = projected[(b + 1) * rows - EDGE : (b + 1) * rows, :HD]

    def around(edge, b):
        low = jnp.maximum(b - f, 0)
        high = jnp.minimum(b + 1 - f, count - 1)
        return jnp.concatenate([edge[low, EDGE:HALO, :], edge[high, 0:EDGE, :]], axis=0)

    halos = jnp.concatenate([around(q_edge, b) for b in range(count)], axis=0)
    send_out[2 * total :, :] = halos.astype(BF16)
    edge_out[...] = jnp.concatenate([around(x_edge, s * 2 + b) for b in range(2)], axis=0).astype(BF16)


def attend_kernel(length, q_in, own, peer, *refs):
    ctx_outs, q_rows = refs[:SEQ], refs[SEQ]
    s, _, f, _ = here()
    valid_len = length[0]
    count = q_rows.shape[0]
    total = q_in.shape[0]
    rows = total // count
    step = q_rows.shape[1]
    local = lax.broadcasted_iota(jnp.int32, (step, total), 1)
    base = (local // rows) * (2 * rows) + local % rows
    keep_own = base + f * rows < valid_len
    keep_peer = base + (1 - f) * rows < valid_len
    scale = 1.0 / math.sqrt(HD)
    keys_t = (((1,), (1,)), ((), ()))
    for b in range(count):
        q_rows[b, 0:rows, :] = q_in[b * rows : (b + 1) * rows, :].astype(F32)
        q_rows[b, rows:step, :] = peer[2 * total + b * HALO : 2 * total + (b + 1) * HALO, :].astype(F32)
    for b in range(count):
        k, side = b // 2, b % 2
        q = q_rows[(s ^ k) * 2 + side].astype(BF16)
        first = lax.dot_general(q, own[0:total, :], keys_t, preferred_element_type=F32) * scale
        second = lax.dot_general(q, peer[0:total, :], keys_t, preferred_element_type=F32) * scale
        first = jnp.where(keep_own, first, -jnp.inf)
        second = jnp.where(keep_peer, second, -jnp.inf)
        peak = jnp.maximum(
            jnp.max(first, axis=1, keepdims=True), jnp.max(second, axis=1, keepdims=True)
        )
        first = jnp.exp(first - peak)
        second = jnp.exp(second - peak)
        weight_sum = jnp.sum(first, axis=1, keepdims=True) + jnp.sum(second, axis=1, keepdims=True)
        weighted = dot(first.astype(BF16), own[total : 2 * total, :]) + dot(
            second.astype(BF16), peer[total : 2 * total, :]
        )
        ctx_outs[k][side * step : (side + 1) * step, :] = (weighted / weight_sum).astype(BF16)


def output_kernel(length, *refs):
    pieces, ctx = refs[: 4 * SEQ], refs[4 * SEQ : 5 * SEQ]
    share_out, send_out, context, weights = refs[5 * SEQ :]
    s, h, f, p = here()
    half, columns = pieces[0].shape
    for k in range(SEQ):
        for y in range(2):
            for core in range(2):
                at = pl.ds(aligned((f ^ core) * 2 * half + (p ^ y) * half, half), half)
                weights[s ^ k, at, :] = pieces[(k * 2 + y) * 2 + core][...]
    for k in range(SEQ):
        context[:, pl.ds(aligned((s ^ k) * HD, HD), HD)] = ctx[k][...]
    for j in range(SEQ):
        at = slice(j * columns, (j + 1) * columns)
        share = dot(context[...], weights[j])
        share_out[:, at] = share
        send_out[:, at] = share.astype(BF16)


def convolve_kernel(length, *refs):
    pieces = refs[: 4 * SEQ]
    own_x, peer_x, halo_x, own_share, peer_share, gain, own_c, peer_c, base_out, share_out = refs[4 * SEQ : 4 * SEQ + 10]
    mid, normed, w_value, w_gate, w_down, channel, padded, active, shares = refs[4 * SEQ + 10 :]
    s, h, f, p = here()
    valid_len = length[0]
    half, columns = pieces[0].shape[1:]
    rows = own_x.shape[0]
    step = rows + HALO
    for k in range(SEQ):
        for y in range(2):
            for core in range(2):
                stack = pieces[(k * 2 + y) * 2 + core]
                at = pl.ds(aligned((s ^ k) * 2 * half + (p ^ y) * half, half), half)
                w_value[f ^ core, at, :] = stack[0]
                w_gate[f ^ core, at, :] = stack[1]
                at = pl.ds(aligned((f ^ core) * 2 * half + (p ^ y) * half, half), half)
                w_down[s ^ k, at, :] = stack[2]
    channel[f] = own_c[...]
    channel[1 - f] = peer_c[...]
    mid[pl.ds(aligned(h * step, 8), rows), :] = own_x[...].astype(F32)
    mid[pl.ds(aligned((1 - h) * step, 8), rows), :] = peer_x[...].astype(F32)
    for b in range(2):
        mid[b * step + rows : (b + 1) * step, :] = halo_x[b * HALO : (b + 1) * HALO, :].astype(F32)
    middle = mid[...] + (own_share[...] + peer_share[...].astype(F32))
    mid[...] = middle
    normed[...] = layer_norm(middle, gain[...]).astype(BF16)
    place = lax.broadcasted_iota(jnp.int32, (step, columns), 0)
    offset = jnp.where(place < rows, place, jnp.where(place < rows + EDGE, place - rows - EDGE, place - EDGE))
    for c in range(2):
        x = normed[...]
        value_part = dot(x, w_value[c])
        gate_part = dot(x, w_gate[c])
        gated = value_part * jax.nn.sigmoid(gate_part)
        for b in range(2):
            t = offset + (4 * s + 2 * b + f) * rows
            kept = jnp.where((t >= 0) & (t < valid_len), gated[b * step : (b + 1) * step], 0.0)
            kept = kept.astype(BF16).astype(F32)
            padded[b, 8 : 8 + rows, :] = kept[:rows]
            padded[b, 8 - EDGE : 8, :] = kept[rows : rows + EDGE]
            padded[b, 8 + rows : 8 + rows + EDGE, :] = kept[rows + EDGE :]
            depth_sum = channel[c, 0:1, :] * padded[b, 8 - EDGE : 8 - EDGE + rows, :]
            for j in range(1, KERNEL):
                low = 8 - EDGE + j
                depth_sum = depth_sum + channel[c, j : j + 1, :] * padded[b, low : low + rows, :]
            shifted = depth_sum * channel[c, KERNEL : KERNEL + 1, :] + channel[c, KERNEL + 1 : KERNEL + 2, :]
            active[b * rows : (b + 1) * rows, c * columns : (c + 1) * columns] = (
                shifted * jax.nn.sigmoid(shifted)
            ).astype(BF16)
    for j in range(SEQ):
        shares[:, j * columns : (j + 1) * columns] = dot(active[...], w_down[j])
    base_out[...] = mid[pl.ds(aligned(h * step, 8), rows), :] + shares[pl.ds(aligned(h * rows, rows), rows), :]
    share_out[...] = shares[pl.ds(aligned((1 - h) * rows, rows), rows), :].astype(BF16)


def shards_chip_per_head(
    frames,
    length,
    ln1_gain,
    w_query,
    w_key,
    w_value,
    w_out,
    ln2_gain,
    pw1_value,
    pw1_gate,
    depth_kernel,
    bn_scale,
    bn_shift,
    pw2,
):
    rows, width = frames.shape
    count = 2 * SEQ
    step = rows + HALO
    f, p = lax.axis_index("fsdp"), lax.axis_index("parts")
    half = w_query.shape[0] // 2
    columns = w_query.shape[1]
    barrier = lax.optimization_barrier

    def other_core(x):
        return lax.ppermute(x, "fsdp", SWAP)

    def other_side(x):
        return lax.ppermute(x, "head", SWAP)

    def other_part(x):
        return lax.ppermute(x, "parts", SWAP)

    def planes(x):
        return [x] + [lax.ppermute(x, "seq", xor_pairs(k)) for k in range(1, SEQ)]

    def part_half(x):
        return lax.dynamic_slice_in_dim(x, p * half, half, axis=x.ndim - 2)

    def spread(mine, others):
        pieces = []
        for near in (mine, *others):
            for part in (near, other_part(near)):
                pieces += [part, other_core(part)]
        return pieces

    near = planes(frames)
    blocks = []
    for block in near:
        blocks += [block, other_side(block)]
    s = lax.axis_index("seq")
    projectors = jnp.stack([w_query, w_key, w_value])
    even = lax.dynamic_slice_in_dim(projectors, (s % 2) * HD, HD, axis=2)
    odd = lax.dynamic_slice_in_dim(projectors, (1 - s % 2) * HD, HD, axis=2)
    w_mine = [even]
    for k in range(1, SEQ):
        pairs = [
            (2 * i + core, 2 * (i ^ k) + core) for core in range(2) for i in range(SEQ) if (i ^ k) // 2 == core
        ]
        w_mine.append(lax.ppermute(odd if k % 2 else even, ("seq", "fsdp"), pairs))
    to_other = [(2 * i + i // 2, 2 * i + 1 - i // 2) for i in range(SEQ)]
    w_other = [lax.ppermute(w, ("seq", "fsdp"), to_other) for w in w_mine]

    mine = part_half(w_out)
    after, *_ = barrier((mine, *near[1:], *w_mine[1:]))
    others = planes(after)[1:]
    out_pieces = spread(mine, others)
    mine = part_half(jnp.stack([pw1_value, pw1_gate, pw2]))
    after, *_ = barrier((mine, *others))
    pw_pieces = spread(mine, planes(after)[1:])
    channels = jnp.concatenate([depth_kernel, bn_scale[None], bn_shift[None], jnp.zeros((5, columns), F32)])
    channels_peer = other_core(channels)

    shape = jax.ShapeDtypeStruct
    queries, send, edges = call(
        project_kernel,
        [
            shape((count * rows, HD), BF16),
            shape((2 * count * rows + count * HALO, HD), BF16),
            shape((2 * HALO, width), BF16),
        ],
        [
            pltpu.VMEM((count * rows, width), BF16),
            pltpu.VMEM((width, 3 * HD), BF16),
            pltpu.VMEM((count, HALO, width), F32),
            pltpu.VMEM((count, HALO, HD), F32),
        ],
        length,
        *blocks,
        *w_mine,
        *w_other,
        ln1_gain[None],
        flops=6 * count * rows * width * HD,
    )
    received = other_core(send)
    halo_x = other_core(edges)
    ctx = call(
        attend_kernel,
        [shape((2 * step, HD), BF16)] * SEQ,
        [pltpu.VMEM((count, step, HD), F32)],
        length,
        queries,
        send,
        received,
        flops=8 * count * step * count * rows * HD,
    )
    ctx = [ctx[0]] + [lax.ppermute(ctx[k], "seq", xor_pairs(k)) for k in range(1, SEQ)]
    own_share, sent_share = call(
        output_kernel,
        [shape((2 * step, width), F32), shape((2 * step, width), BF16)],
        [
            pltpu.VMEM((2 * step, SEQ * HD), BF16),
            pltpu.VMEM((SEQ, 2 * columns, columns), BF16),
        ],
        length,
        *out_pieces,
        *ctx,
        flops=2 * step * width * width,
    )
    base, share = call(
        convolve_kernel,
        [shape((rows, width), F32), shape((rows, width), BF16)],
        [
            pltpu.VMEM((2 * step, width), F32),
            pltpu.VMEM((2 * step, width), BF16),
            pltpu.VMEM((2, width, columns), BF16),
            pltpu.VMEM((2, width, columns), BF16),
            pltpu.VMEM((SEQ, 2 * columns, columns), BF16),
            pltpu.VMEM((2, 16, columns), F32),
            pltpu.VMEM((2, 16 + rows, columns), F32),
            pltpu.VMEM((2 * rows, 2 * columns), BF16),
            pltpu.VMEM((2 * rows, width), F32),
        ],
        length,
        *pw_pieces,
        frames,
        blocks[1],
        halo_x,
        own_share,
        other_side(sent_share),
        ln2_gain[None],
        channels,
        channels_peer,
        flops=6 * step * width * width,
        vmem=14,
    )
    return (base + other_side(share).astype(F32)).astype(BF16)


def solution(mesh):
    in_specs = (
        P(("parts", "seq", "head", "fsdp"), None),
        P("parts"),
        P(),
        P("seq", ("head", "fsdp")),
        P("seq", ("head", "fsdp")),
        P("seq", ("head", "fsdp")),
        P(("head", "fsdp"), "seq"),
        P(),
        P("seq", ("head", "fsdp")),
        P("seq", ("head", "fsdp")),
        P(None, ("head", "fsdp")),
        P(("head", "fsdp")),
        P(("head", "fsdp")),
        P(("head", "fsdp"), "seq"),
    )
    out_specs = P(("parts", "seq", "head", "fsdp"), None)
    body = shards_chip_per_head if one_head_per_chip(mesh) else shards_general
    return jax.shard_map(body, mesh=mesh, in_specs=in_specs, out_specs=out_specs, check_vma=False)
```

```python
import math

import jax
import jax.numpy as jnp
from jax import lax
from jax.experimental import pallas as pl
from jax.experimental.pallas import tpu as pltpu
from jax.sharding import PartitionSpec as P

KERNEL = 9
HD = 128


def with_halo(block, sides, width):
    for axis, dim in sides:
        count = lax.axis_size(axis)
        forward = [(i, i + 1) for i in range(count - 1)]
        backward = [(target, source) for source, target in forward]
        low = lax.ppermute(
            lax.slice_in_dim(block, block.shape[dim] - width, None, axis=dim), axis, forward
        )
        high = lax.ppermute(lax.slice_in_dim(block, 0, width, axis=dim), axis, backward)
        block = jnp.concatenate([low, block, high], axis=dim)
    return block


def layer_norm(values_in, gain_vec):
    center = jnp.mean(values_in, axis=-1, keepdims=True)
    shifted = values_in - center
    spread = jnp.mean(shifted * shifted, axis=-1, keepdims=True)
    return shifted * lax.rsqrt(spread + 1e-05) * gain_vec


def shards_general(
    frames,
    length,
    ln1_gain,
    w_query,
    w_key,
    w_value,
    w_out,
    ln2_gain,
    pw1_value,
    pw1_gate,
    depth_kernel,
    bn_scale,
    bn_shift,
    pw2,
):
    group_size = lax.axis_size(("head", "fsdp"))
    my_rows = frames.shape[0]
    block_rows = my_rows * group_size
    head_cols = w_query.shape[1]
    heads_here = head_cols // HD
    seq_start = lax.axis_index("seq") * block_rows
    valid_len = length[0]
    score_scale = 1.0 / math.sqrt(HD)
    full_query, full_key, full_value, value_cols, gate_cols = (
        lax.all_gather(w_query, "seq", axis=0, tiled=True),
        lax.all_gather(w_key, "seq", axis=0, tiled=True),
        lax.all_gather(w_value, "seq", axis=0, tiled=True),
        lax.all_gather(pw1_value, "seq", axis=0, tiled=True),
        lax.all_gather(pw1_gate, "seq", axis=0, tiled=True),
    )
    out_rows, down_rows = (
        lax.all_gather(w_out, "seq", axis=1, tiled=True),
        lax.all_gather(pw2, "seq", axis=1, tiled=True),
    )
    projector = jnp.concatenate((full_query, full_key, full_value), axis=1)
    source = frames.astype(jnp.float32)
    normed = layer_norm(source, ln1_gain).astype(jnp.bfloat16)
    projected = jnp.dot(
        lax.all_gather(normed, ("head", "fsdp"), axis=0, tiled=True),
        projector,
        preferred_element_type=jnp.float32,
    ).astype(jnp.bfloat16)
    queries = projected[:, :head_cols].reshape(block_rows, heads_here, HD)
    keys_here = projected[:, head_cols : 2 * head_cols]
    values_here = projected[:, 2 * head_cols :]
    initial = (
        jnp.full((heads_here, block_rows), -1e30, jnp.float32),
        jnp.zeros((heads_here, block_rows), jnp.float32),
        jnp.zeros((heads_here, block_rows, HD), jnp.float32),
    )
    key_piece = lax.all_gather(keys_here, "seq", axis=0, tiled=True)
    value_piece = lax.all_gather(values_here, "seq", axis=0, tiled=True)
    row_count = key_piece.shape[0]
    block_size = math.gcd(row_count, 512)
    block_count = row_count // block_size
    key_blocks = key_piece.reshape(block_count, block_size, heads_here, HD)
    value_blocks = value_piece.reshape(block_count, block_size, heads_here, HD)
    places = jnp.arange(row_count, dtype=jnp.int32).reshape(block_count, block_size)

    def advance(inner_state, block_item):
        key_block, value_block, place = block_item
        peak_score, weight_sum, weighted = inner_state
        scores = (
            jnp.einsum("qhd,khd->hqk", queries, key_block, preferred_element_type=jnp.float32)
            * score_scale
        )
        scores = jnp.where((place < valid_len)[None, None, :], scores, -jnp.inf)
        new_peak = jnp.maximum(peak_score, jnp.max(scores, axis=2))
        factor = jnp.exp(peak_score - new_peak)
        weights = jnp.exp(scores - new_peak[:, :, None])
        weight_sum = weight_sum * factor + jnp.sum(weights, axis=2)
        weighted = weighted * factor[:, :, None] + jnp.einsum(
            "hqk,khd->hqd",
            weights.astype(jnp.bfloat16),
            value_block,
            preferred_element_type=jnp.float32,
        )
        return ((new_peak, weight_sum, weighted), None)

    result, unused = lax.scan(advance, initial, (key_blocks, value_blocks, places))
    peak_score, weight_sum, weighted = result
    context = (
        (weighted / weight_sum[:, :, None])
        .astype(jnp.bfloat16)
        .transpose(1, 0, 2)
        .reshape(block_rows, head_cols)
    )
    attended = lax.psum_scatter(
        jnp.dot(context, out_rows, preferred_element_type=jnp.float32).astype(jnp.bfloat16),
        ("head", "fsdp"),
        scatter_dimension=0,
        tiled=True,
    ).astype(jnp.float32)
    middle = source + attended
    normed_two = layer_norm(middle, ln2_gain).astype(jnp.bfloat16)
    piece = lax.all_gather(normed_two, ("head", "fsdp"), axis=0, tiled=True)
    value_part = jnp.dot(piece, value_cols, preferred_element_type=jnp.float32)
    gate_part = jnp.dot(piece, gate_cols, preferred_element_type=jnp.float32)
    places = seq_start + jnp.arange(piece.shape[0], dtype=jnp.int32)
    gated_rows = jnp.where(
        (places < valid_len)[:, None], value_part * jax.nn.sigmoid(gate_part), 0.0
    ).astype(jnp.bfloat16)
    rim_width = (KERNEL - 1) // 2
    padded = with_halo(gated_rows, (("seq", 0),), rim_width).astype(jnp.float32)
    depth_sum = depth_kernel[0] * padded[0:block_rows]
    for offset in range(1, KERNEL):
        depth_sum = depth_sum + depth_kernel[offset] * padded[offset : offset + block_rows]
    shifted = depth_sum * bn_scale + bn_shift
    active = (shifted * jax.nn.sigmoid(shifted)).astype(jnp.bfloat16)
    conv_part = lax.psum_scatter(
        jnp.dot(active, down_rows, preferred_element_type=jnp.float32).astype(jnp.bfloat16),
        ("head", "fsdp"),
        scatter_dimension=0,
        tiled=True,
    ).astype(jnp.float32)
    return (middle + conv_part).astype(jnp.bfloat16)


SEQ = 4
EDGE = (KERNEL - 1) // 2
HALO = 2 * EDGE
SWAP = [(0, 1), (1, 0)]
F32 = jnp.float32
BF16 = jnp.bfloat16


def one_head_per_chip(mesh):
    return dict(mesh.shape) == {"parts": 2, "seq": SEQ, "head": 2, "fsdp": 2}


def xor_pairs(k):
    return [(i, i ^ k) for i in range(SEQ)]


def call(kernel, outs, scratch, length, *operands, flops=0, vmem=8):
    moved = sum(math.prod(a.shape) * a.dtype.itemsize for a in (*operands, *outs))
    return pl.pallas_call(
        kernel,
        out_shape=outs,
        in_specs=[pl.BlockSpec(memory_space=pltpu.SMEM)]
        + [pl.BlockSpec(memory_space=pltpu.VMEM)] * len(operands),
        out_specs=[pl.BlockSpec(memory_space=pltpu.VMEM)] * len(outs),
        scratch_shapes=scratch,
        cost_estimate=pl.CostEstimate(flops=0, bytes_accessed=0, transcendentals=0),
        compiler_params=pltpu.CompilerParams(vmem_limit_bytes=vmem << 20),
    )(length, *operands)


def aligned(value, to):
    return pl.multiple_of(value, to)


def dot(a, b):
    return jnp.dot(a, b, preferred_element_type=F32)


def here():
    return tuple(lax.axis_index(a) for a in ("seq", "head", "fsdp", "parts"))


def deal_kernel(length, *refs):
    mine, other, outs = refs[:3], refs[3:6], refs[6:]
    s, _, f, _ = here()
    half = outs[0].shape[1]
    rows = pl.ds(aligned(f * half, half), half)
    for k in range(SEQ):
        head = s ^ k
        columns = pl.ds(aligned((head % 2) * HD, HD), HD)

        @pl.when(head // 2 == f)
        def _():
            for m in range(3):
                outs[k][m] = mine[m][rows, columns]

        @pl.when(head // 2 != f)
        def _():
            for m in range(3):
                outs[k][m] = other[m][rows, columns]


def stack_kernel(length, *refs):
    s = lax.axis_index("seq")
    for k in range(SEQ):
        refs[SEQ][s ^ k] = refs[k][...]


def project_kernel(length, *refs):
    blocks = refs[: 2 * SEQ]
    mine, other = refs[2 * SEQ : 3 * SEQ], refs[3 * SEQ : 4 * SEQ]
    gain, q_out, send_out, edge_out, normed, weights, x_edge, q_edge = refs[4 * SEQ :]
    s, h, f, _ = here()
    rows = blocks[0].shape[0]
    half = mine[0].shape[1]
    gain_row = gain[...]
    for slot, block in enumerate(blocks):
        at = (s ^ (slot // 2)) * 2 + (h ^ (slot % 2))
        x = block[...].astype(F32)
        normed[pl.ds(aligned(at * rows, rows), rows), :] = layer_norm(x, gain_row).astype(BF16)
        x_edge[at, 0:EDGE, :] = x[:EDGE]
        x_edge[at, EDGE:HALO, :] = x[rows - EDGE :]
    for k in range(SEQ):
        for core, pieces in enumerate((mine, other)):
            at = pl.ds(aligned((s ^ k) * 2 * half + (f ^ core) * half, half), half)
            for m in range(3):
                weights[at, m * HD : (m + 1) * HD] = pieces[k][m]
    count = 2 * SEQ
    total = count * rows
    projected = dot(normed[...], weights[...])
    q_out[...] = projected[:, :HD].astype(BF16)
    send_out[0:total, :] = projected[:, HD : 2 * HD].astype(BF16)
    send_out[total : 2 * total, :] = projected[:, 2 * HD :].astype(BF16)
    for b in range(count):
        q_edge[b, 0:EDGE, :] = projected[b * rows : b * rows + EDGE, :HD]
        q_edge[b, EDGE:HALO, :] = projected[(b + 1) * rows - EDGE : (b + 1) * rows, :HD]

    def around(edge, b):
        low = jnp.maximum(b - f, 0)
        high = jnp.minimum(b + 1 - f, count - 1)
        return jnp.concatenate([edge[low, EDGE:HALO, :], edge[high, 0:EDGE, :]], axis=0)

    halos = jnp.concatenate([around(q_edge, b) for b in range(count)], axis=0)
    send_out[2 * total :, :] = halos.astype(BF16)
    edge_out[...] = jnp.concatenate([around(x_edge, s * 2 + b) for b in range(2)], axis=0).astype(BF16)


def attend_kernel(length, q_in, own, peer, *refs):
    ctx_outs, q_rows = refs[:SEQ], refs[SEQ]
    s, _, f, _ = here()
    valid_len = length[0]
    count = q_rows.shape[0]
    total = q_in.shape[0]
    rows = total // count
    step = q_rows.shape[1]
    local = lax.broadcasted_iota(jnp.int32, (step, total), 1)
    base = (local // rows) * (2 * rows) + local % rows
    keep_own = base + f * rows < valid_len
    keep_peer = base + (1 - f) * rows < valid_len
    scale = 1.0 / math.sqrt(HD)
    keys_t = (((1,), (1,)), ((), ()))
    for b in range(count):
        q_rows[b, 0:rows, :] = q_in[b * rows : (b + 1) * rows, :].astype(F32)
        q_rows[b, rows:step, :] = peer[2 * total + b * HALO : 2 * total + (b + 1) * HALO, :].astype(F32)
    for b in range(count):
        k, side = b // 2, b % 2
        q = q_rows[(s ^ k) * 2 + side].astype(BF16)
        first = lax.dot_general(q, own[0:total, :], keys_t, preferred_element_type=F32) * scale
        second = lax.dot_general(q, peer[0:total, :], keys_t, preferred_element_type=F32) * scale
        first = jnp.where(keep_own, first, -jnp.inf)
        second = jnp.where(keep_peer, second, -jnp.inf)
        peak = jnp.maximum(
            jnp.max(first, axis=1, keepdims=True), jnp.max(second, axis=1, keepdims=True)
        )
        first = jnp.exp(first - peak)
        second = jnp.exp(second - peak)
        weight_sum = jnp.sum(first, axis=1, keepdims=True) + jnp.sum(second, axis=1, keepdims=True)
        weighted = dot(first.astype(BF16), own[total : 2 * total, :]) + dot(
            second.astype(BF16), peer[total : 2 * total, :]
        )
        ctx_outs[k][side * step : (side + 1) * step, :] = (weighted / weight_sum).astype(BF16)


def output_kernel(length, *refs):
    pieces, ctx = refs[:4], refs[4 : 4 + SEQ]
    share_out, send_out, context, weights = refs[4 + SEQ :]
    s, h, f, p = here()
    half, columns = pieces[0].shape[1:]
    for y in range(2):
        for core in range(2):
            at = pl.ds(aligned((f ^ core) * 2 * half + (p ^ y) * half, half), half)
            for j in range(SEQ):
                weights[j, at, :] = pieces[y * 2 + core][j]
    for k in range(SEQ):
        context[:, pl.ds(aligned((s ^ k) * HD, HD), HD)] = ctx[k][...]
    for j in range(SEQ):
        at = slice(j * columns, (j + 1) * columns)
        share = dot(context[...], weights[j])
        share_out[:, at] = share
        send_out[:, at] = share.astype(BF16)


def convolve_kernel(length, *refs):
    pieces = refs[: 4 * SEQ]
    own_x, peer_x, halo_x, own_share, peer_share, gain, own_c, peer_c, base_out, share_out = refs[4 * SEQ : 4 * SEQ + 10]
    mid, normed, w_value, w_gate, w_down, channel, padded, active, shares = refs[4 * SEQ + 10 :]
    s, h, f, p = here()
    valid_len = length[0]
    half, columns = pieces[0].shape[1:]
    rows = own_x.shape[0]
    step = rows + HALO
    for k in range(SEQ):
        for y in range(2):
            for core in range(2):
                stack = pieces[(k * 2 + y) * 2 + core]
                at = pl.ds(aligned((s ^ k) * 2 * half + (p ^ y) * half, half), half)
                w_value[f ^ core, at, :] = stack[0]
                w_gate[f ^ core, at, :] = stack[1]
                at = pl.ds(aligned((f ^ core) * 2 * half + (p ^ y) * half, half), half)
                w_down[s ^ k, at, :] = stack[2]
    channel[f] = own_c[...]
    channel[1 - f] = peer_c[...]
    mid[pl.ds(aligned(h * step, 8), rows), :] = own_x[...].astype(F32)
    mid[pl.ds(aligned((1 - h) * step, 8), rows), :] = peer_x[...].astype(F32)
    for b in range(2):
        mid[b * step + rows : (b + 1) * step, :] = halo_x[b * HALO : (b + 1) * HALO, :].astype(F32)
    middle = mid[...] + (own_share[...] + peer_share[...].astype(F32))
    mid[...] = middle
    normed[...] = layer_norm(middle, gain[...]).astype(BF16)
    place = lax.broadcasted_iota(jnp.int32, (step, columns), 0)
    offset = jnp.where(place < rows, place, jnp.where(place < rows + EDGE, place - rows - EDGE, place - EDGE))
    for c in range(2):
        x = normed[...]
        value_part = dot(x, w_value[c])
        gate_part = dot(x, w_gate[c])
        gated = value_part * jax.nn.sigmoid(gate_part)
        for b in range(2):
            t = offset + (4 * s + 2 * b + f) * rows
            kept = jnp.where((t >= 0) & (t < valid_len), gated[b * step : (b + 1) * step], 0.0)
            kept = kept.astype(BF16).astype(F32)
            padded[b, 8 : 8 + rows, :] = kept[:rows]
            padded[b, 8 - EDGE : 8, :] = kept[rows : rows + EDGE]
            padded[b, 8 + rows : 8 + rows + EDGE, :] = kept[rows + EDGE :]
            depth_sum = channel[c, 0:1, :] * padded[b, 8 - EDGE : 8 - EDGE + rows, :]
            for j in range(1, KERNEL):
                low = 8 - EDGE + j
                depth_sum = depth_sum + channel[c, j : j + 1, :] * padded[b, low : low + rows, :]
            shifted = depth_sum * channel[c, KERNEL : KERNEL + 1, :] + channel[c, KERNEL + 1 : KERNEL + 2, :]
            active[b * rows : (b + 1) * rows, c * columns : (c + 1) * columns] = (
                shifted * jax.nn.sigmoid(shifted)
            ).astype(BF16)
    for j in range(SEQ):
        shares[:, j * columns : (j + 1) * columns] = dot(active[...], w_down[j])
    base_out[...] = mid[pl.ds(aligned(h * step, 8), rows), :] + shares[pl.ds(aligned(h * rows, rows), rows), :]
    share_out[...] = shares[pl.ds(aligned((1 - h) * rows, rows), rows), :].astype(BF16)


def shards_chip_per_head(
    frames,
    length,
    ln1_gain,
    w_query,
    w_key,
    w_value,
    w_out,
    ln2_gain,
    pw1_value,
    pw1_gate,
    depth_kernel,
    bn_scale,
    bn_shift,
    pw2,
):
    rows, width = frames.shape
    count = 2 * SEQ
    step = rows + HALO
    f, p = lax.axis_index("fsdp"), lax.axis_index("parts")
    half = w_query.shape[0] // 2
    columns = w_query.shape[1]
    barrier = lax.optimization_barrier

    def other_core(x):
        return lax.ppermute(x, "fsdp", SWAP)

    def other_side(x):
        return lax.ppermute(x, "head", SWAP)

    def other_part(x):
        return lax.ppermute(x, "parts", SWAP)

    def planes(x):
        return [x] + [lax.ppermute(x, "seq", xor_pairs(k)) for k in range(1, SEQ)]

    def part_half(x):
        return lax.dynamic_slice_in_dim(x, p * half, half, axis=x.ndim - 2)

    near = planes(frames)
    blocks = []
    for block in near:
        blocks += [block, other_side(block)]
    given = [w_query, w_key, w_value]
    shape = jax.ShapeDtypeStruct
    dealt = call(
        deal_kernel,
        [shape((3, half, HD), BF16)] * SEQ,
        [],
        length,
        *given,
        *[other_core(w) for w in given],
    )
    w_mine = [dealt[0]] + [lax.ppermute(dealt[k], "seq", xor_pairs(k)) for k in range(1, SEQ)]
    w_other = [other_core(w) for w in w_mine]

    out_mine = part_half(w_out)
    after, *_ = barrier((out_mine, *near[1:], *w_mine[1:]))
    out_others = planes(after)[1:]
    pw_mine = part_half(jnp.stack([pw1_value, pw1_gate, pw2]))
    pw_first, *_ = barrier((pw_mine, *near[1:]))
    pw_part = other_part(pw_first)
    queries, send, edges = call(
        project_kernel,
        [
            shape((count * rows, HD), BF16),
            shape((2 * count * rows + count * HALO, HD), BF16),
            shape((2 * HALO, width), BF16),
        ],
        [
            pltpu.VMEM((count * rows, width), BF16),
            pltpu.VMEM((width, 3 * HD), BF16),
            pltpu.VMEM((count, HALO, width), F32),
            pltpu.VMEM((count, HALO, HD), F32),
        ],
        length,
        *blocks,
        *w_mine,
        *w_other,
        ln1_gain[None],
        flops=6 * count * rows * width * HD,
    )
    received = other_core(send)
    out_mine, _, *out_others = barrier((out_mine, received, *out_others))
    (stack,) = call(stack_kernel, [shape((SEQ, half, columns), BF16)], [], length, out_mine, *out_others)
    stack_part = other_part(stack)
    out_pieces = [stack, other_core(stack), stack_part, other_core(stack_part)]
    queries, _ = barrier((queries, stack))
    after, *_ = barrier((pw_mine, send, *out_others))
    pw_others = planes(after)[1:]
    halo_x = other_core(edges)
    ctx = call(
        attend_kernel,
        [shape((2 * step, HD), BF16)] * SEQ,
        [pltpu.VMEM((count, step, HD), F32)],
        length,
        queries,
        send,
        received,
        flops=8 * count * step * count * rows * HD,
    )
    depth_kernel, pw_mine, pw_part, *_ = barrier((depth_kernel, pw_mine, pw_part, *ctx))
    pw_pieces = [pw_mine, other_core(pw_mine), pw_part, other_core(pw_part)]
    channels = jnp.concatenate([depth_kernel, bn_scale[None], bn_shift[None], jnp.zeros((5, columns), F32)])
    channels_peer = other_core(channels)
    ctx = [ctx[0]] + [lax.ppermute(ctx[k], "seq", xor_pairs(k)) for k in range(1, SEQ)]
    own_share, sent_share = call(
        output_kernel,
        [shape((2 * step, width), F32), shape((2 * step, width), BF16)],
        [
            pltpu.VMEM((2 * step, SEQ * HD), BF16),
            pltpu.VMEM((SEQ, 2 * columns, columns), BF16),
        ],
        length,
        *out_pieces,
        *ctx,
        flops=2 * step * width * width,
    )
    *pw_others, own_share, sent_share = barrier((*pw_others, own_share, sent_share))
    for near in pw_others:
        part = other_part(near)
        pw_pieces += [near, other_core(near), part, other_core(part)]
    base, share = call(
        convolve_kernel,
        [shape((rows, width), F32), shape((rows, width), BF16)],
        [
            pltpu.VMEM((2 * step, width), F32),
            pltpu.VMEM((2 * step, width), BF16),
            pltpu.VMEM((2, width, columns), BF16),
            pltpu.VMEM((2, width, columns), BF16),
            pltpu.VMEM((SEQ, 2 * columns, columns), BF16),
            pltpu.VMEM((2, 16, columns), F32),
            pltpu.VMEM((2, 16 + rows, columns), F32),
            pltpu.VMEM((2 * rows, 2 * columns), BF16),
            pltpu.VMEM((2 * rows, width), F32),
        ],
        length,
        *pw_pieces,
        frames,
        blocks[1],
        halo_x,
        own_share,
        other_side(sent_share),
        ln2_gain[None],
        channels,
        channels_peer,
        flops=6 * step * width * width,
        vmem=14,
    )
    return (base + other_side(share).astype(F32)).astype(BF16)


def solution(mesh):
    in_specs = (
        P(("parts", "seq", "head", "fsdp"), None),
        P("parts"),
        P(),
        P("seq", ("head", "fsdp")),
        P("seq", ("head", "fsdp")),
        P("seq", ("head", "fsdp")),
        P(("head", "fsdp"), "seq"),
        P(),
        P("seq", ("head", "fsdp")),
        P("seq", ("head", "fsdp")),
        P(None, ("head", "fsdp")),
        P(("head", "fsdp")),
        P(("head", "fsdp")),
        P(("head", "fsdp"), "seq"),
    )
    out_specs = P(("parts", "seq", "head", "fsdp"), None)
    body = shards_chip_per_head if one_head_per_chip(mesh) else shards_general
    return jax.shard_map(body, mesh=mesh, in_specs=in_specs, out_specs=out_specs, check_vma=False)
```

```python
import math

import jax
import jax.numpy as jnp
from jax import lax
from jax.experimental import pallas as pl
from jax.experimental.pallas import tpu as pltpu
from jax.sharding import PartitionSpec as P

KERNEL = 9
HD = 128


def with_halo(block, sides, width):
    for axis, dim in sides:
        count = lax.axis_size(axis)
        forward = [(i, i + 1) for i in range(count - 1)]
        backward = [(target, source) for source, target in forward]
        low = lax.ppermute(
            lax.slice_in_dim(block, block.shape[dim] - width, None, axis=dim), axis, forward
        )
        high = lax.ppermute(lax.slice_in_dim(block, 0, width, axis=dim), axis, backward)
        block = jnp.concatenate([low, block, high], axis=dim)
    return block


def layer_norm(values_in, gain_vec):
    center = jnp.mean(values_in, axis=-1, keepdims=True)
    shifted = values_in - center
    spread = jnp.mean(shifted * shifted, axis=-1, keepdims=True)
    return shifted * lax.rsqrt(spread + 1e-05) * gain_vec


def shards_general(
    frames,
    length,
    ln1_gain,
    w_query,
    w_key,
    w_value,
    w_out,
    ln2_gain,
    pw1_value,
    pw1_gate,
    depth_kernel,
    bn_scale,
    bn_shift,
    pw2,
):
    group_size = lax.axis_size(("head", "fsdp"))
    my_rows = frames.shape[0]
    block_rows = my_rows * group_size
    head_cols = w_query.shape[1]
    heads_here = head_cols // HD
    seq_start = lax.axis_index("seq") * block_rows
    valid_len = length[0]
    score_scale = 1.0 / math.sqrt(HD)
    full_query, full_key, full_value, value_cols, gate_cols = (
        lax.all_gather(w_query, "seq", axis=0, tiled=True),
        lax.all_gather(w_key, "seq", axis=0, tiled=True),
        lax.all_gather(w_value, "seq", axis=0, tiled=True),
        lax.all_gather(pw1_value, "seq", axis=0, tiled=True),
        lax.all_gather(pw1_gate, "seq", axis=0, tiled=True),
    )
    out_rows, down_rows = (
        lax.all_gather(w_out, "seq", axis=1, tiled=True),
        lax.all_gather(pw2, "seq", axis=1, tiled=True),
    )
    projector = jnp.concatenate((full_query, full_key, full_value), axis=1)
    source = frames.astype(jnp.float32)
    normed = layer_norm(source, ln1_gain).astype(jnp.bfloat16)
    projected = jnp.dot(
        lax.all_gather(normed, ("head", "fsdp"), axis=0, tiled=True),
        projector,
        preferred_element_type=jnp.float32,
    ).astype(jnp.bfloat16)
    queries = projected[:, :head_cols].reshape(block_rows, heads_here, HD)
    keys_here = projected[:, head_cols : 2 * head_cols]
    values_here = projected[:, 2 * head_cols :]
    initial = (
        jnp.full((heads_here, block_rows), -1e30, jnp.float32),
        jnp.zeros((heads_here, block_rows), jnp.float32),
        jnp.zeros((heads_here, block_rows, HD), jnp.float32),
    )
    key_piece = lax.all_gather(keys_here, "seq", axis=0, tiled=True)
    value_piece = lax.all_gather(values_here, "seq", axis=0, tiled=True)
    row_count = key_piece.shape[0]
    block_size = math.gcd(row_count, 512)
    block_count = row_count // block_size
    key_blocks = key_piece.reshape(block_count, block_size, heads_here, HD)
    value_blocks = value_piece.reshape(block_count, block_size, heads_here, HD)
    places = jnp.arange(row_count, dtype=jnp.int32).reshape(block_count, block_size)

    def advance(inner_state, block_item):
        key_block, value_block, place = block_item
        peak_score, weight_sum, weighted = inner_state
        scores = (
            jnp.einsum("qhd,khd->hqk", queries, key_block, preferred_element_type=jnp.float32)
            * score_scale
        )
        scores = jnp.where((place < valid_len)[None, None, :], scores, -jnp.inf)
        new_peak = jnp.maximum(peak_score, jnp.max(scores, axis=2))
        factor = jnp.exp(peak_score - new_peak)
        weights = jnp.exp(scores - new_peak[:, :, None])
        weight_sum = weight_sum * factor + jnp.sum(weights, axis=2)
        weighted = weighted * factor[:, :, None] + jnp.einsum(
            "hqk,khd->hqd",
            weights.astype(jnp.bfloat16),
            value_block,
            preferred_element_type=jnp.float32,
        )
        return ((new_peak, weight_sum, weighted), None)

    result, unused = lax.scan(advance, initial, (key_blocks, value_blocks, places))
    peak_score, weight_sum, weighted = result
    context = (
        (weighted / weight_sum[:, :, None])
        .astype(jnp.bfloat16)
        .transpose(1, 0, 2)
        .reshape(block_rows, head_cols)
    )
    attended = lax.psum_scatter(
        jnp.dot(context, out_rows, preferred_element_type=jnp.float32).astype(jnp.bfloat16),
        ("head", "fsdp"),
        scatter_dimension=0,
        tiled=True,
    ).astype(jnp.float32)
    middle = source + attended
    normed_two = layer_norm(middle, ln2_gain).astype(jnp.bfloat16)
    piece = lax.all_gather(normed_two, ("head", "fsdp"), axis=0, tiled=True)
    value_part = jnp.dot(piece, value_cols, preferred_element_type=jnp.float32)
    gate_part = jnp.dot(piece, gate_cols, preferred_element_type=jnp.float32)
    places = seq_start + jnp.arange(piece.shape[0], dtype=jnp.int32)
    gated_rows = jnp.where(
        (places < valid_len)[:, None], value_part * jax.nn.sigmoid(gate_part), 0.0
    ).astype(jnp.bfloat16)
    rim_width = (KERNEL - 1) // 2
    padded = with_halo(gated_rows, (("seq", 0),), rim_width).astype(jnp.float32)
    depth_sum = depth_kernel[0] * padded[0:block_rows]
    for offset in range(1, KERNEL):
        depth_sum = depth_sum + depth_kernel[offset] * padded[offset : offset + block_rows]
    shifted = depth_sum * bn_scale + bn_shift
    active = (shifted * jax.nn.sigmoid(shifted)).astype(jnp.bfloat16)
    conv_part = lax.psum_scatter(
        jnp.dot(active, down_rows, preferred_element_type=jnp.float32).astype(jnp.bfloat16),
        ("head", "fsdp"),
        scatter_dimension=0,
        tiled=True,
    ).astype(jnp.float32)
    return (middle + conv_part).astype(jnp.bfloat16)


SEQ = 4
EDGE = (KERNEL - 1) // 2
HALO = 2 * EDGE
SWAP = [(0, 1), (1, 0)]
F32 = jnp.float32
BF16 = jnp.bfloat16


def one_head_per_chip(mesh):
    return dict(mesh.shape) == {"parts": 2, "seq": SEQ, "head": 2, "fsdp": 2}


def xor_pairs(k):
    return [(i, i ^ k) for i in range(SEQ)]


def call(kernel, outs, scratch, length, *operands, vmem=8, left=0):
    return pl.pallas_call(
        kernel,
        out_shape=outs,
        in_specs=[pl.BlockSpec(memory_space=pltpu.SMEM)]
        + [pl.BlockSpec(memory_space=pl.ANY)] * left
        + [pl.BlockSpec(memory_space=pltpu.VMEM)] * (len(operands) - left),
        out_specs=[pl.BlockSpec(memory_space=pltpu.VMEM)] * len(outs),
        scratch_shapes=scratch,
        cost_estimate=pl.CostEstimate(flops=0, bytes_accessed=0, transcendentals=0),
        compiler_params=pltpu.CompilerParams(vmem_limit_bytes=vmem << 20),
    )(length, *operands)


def aligned(value, to):
    return pl.multiple_of(value, to)


def dot(a, b):
    return jnp.dot(a, b, preferred_element_type=F32)


def here():
    return tuple(lax.axis_index(a) for a in ("seq", "head", "fsdp", "parts"))


def deal_kernel(length, *refs):
    sources, other, outs, (held, sems) = refs[:4], refs[4:7], refs[7:-2], refs[-2:]
    copies = [pltpu.make_async_copy(w, held.at[i], sems.at[i]) for i, w in enumerate(sources)]
    for copy in copies:
        copy.start()
    mine, w_out = [held.at[m] for m in range(3)], held.at[3]
    s, _, f, p = here()
    for copy in copies:
        copy.wait()
    half = outs[0].shape[1]
    rows = pl.ds(aligned(f * half, half), half)
    for k in range(SEQ):
        head = s ^ k
        columns = pl.ds(aligned((head % 2) * HD, HD), HD)

        @pl.when(head // 2 == f)
        def _():
            for m in range(3):
                outs[k][m] = mine[m][rows, columns]

        @pl.when(head // 2 != f)
        def _():
            for m in range(3):
                outs[k][m] = other[m][rows, columns]

        for m in range(w_out.shape[1] // HD):
            outs[k][3 + m] = w_out[pl.ds(aligned(p * half, half), half), m * HD : (m + 1) * HD]


def project_kernel(length, *refs):
    blocks = refs[: 2 * SEQ]
    mine, other = refs[2 * SEQ : 3 * SEQ], refs[3 * SEQ : 4 * SEQ]
    gain, q_out, send_out, edge_out, stack_out, normed, weights, x_edge, q_edge = refs[4 * SEQ :]
    s, h, f, _ = here()
    rows = blocks[0].shape[0]
    half = mine[0].shape[1]
    gain_row = gain[...]
    for slot, block in enumerate(blocks):
        at = (s ^ (slot // 2)) * 2 + (h ^ (slot % 2))
        x = block[...].astype(F32)
        normed[pl.ds(aligned(at * rows, rows), rows), :] = layer_norm(x, gain_row).astype(BF16)
        x_edge[at, 0:EDGE, :] = x[:EDGE]
        x_edge[at, EDGE:HALO, :] = x[rows - EDGE :]
    for k in range(SEQ):
        for core, pieces in enumerate((mine, other)):
            at = pl.ds(aligned((s ^ k) * 2 * half + (f ^ core) * half, half), half)
            for m in range(3):
                weights[at, m * HD : (m + 1) * HD] = pieces[k][m]
        stack_out[s ^ k] = mine[k][3:]
    count = 2 * SEQ
    total = count * rows
    projected = dot(normed[...], weights[...])
    q_out[...] = projected[:, :HD].astype(BF16)
    send_out[0:total, :] = projected[:, HD : 2 * HD].astype(BF16)
    send_out[total : 2 * total, :] = projected[:, 2 * HD :].astype(BF16)
    for b in range(count):
        q_edge[b, 0:EDGE, :] = projected[b * rows : b * rows + EDGE, :HD]
        q_edge[b, EDGE:HALO, :] = projected[(b + 1) * rows - EDGE : (b + 1) * rows, :HD]

    def around(edge, b):
        low = jnp.maximum(b - f, 0)
        high = jnp.minimum(b + 1 - f, count - 1)
        return jnp.concatenate([edge[low, EDGE:HALO, :], edge[high, 0:EDGE, :]], axis=0)

    halos = jnp.concatenate([around(q_edge, b) for b in range(count)], axis=0)
    send_out[2 * total :, :] = halos.astype(BF16)
    edge_out[...] = jnp.concatenate([around(x_edge, s * 2 + b) for b in range(2)], axis=0).astype(BF16)


def attend_kernel(length, q_in, own, peer, *refs):
    ctx_outs, q_rows = refs[:SEQ], refs[SEQ]
    s, _, f, _ = here()
    valid_len = length[0]
    count = q_rows.shape[0]
    total = q_in.shape[0]
    rows = total // count
    step = q_rows.shape[1]
    local = lax.broadcasted_iota(jnp.int32, (step, total), 1)
    base = (local // rows) * (2 * rows) + local % rows
    keep_own = base + f * rows < valid_len
    keep_peer = base + (1 - f) * rows < valid_len
    scale = 1.0 / math.sqrt(HD)
    keys_t = (((1,), (1,)), ((), ()))
    for b in range(count):
        q_rows[b, 0:rows, :] = q_in[b * rows : (b + 1) * rows, :].astype(F32)
        q_rows[b, rows:step, :] = peer[2 * total + b * HALO : 2 * total + (b + 1) * HALO, :].astype(F32)
    for b in range(count):
        k, side = b // 2, b % 2
        q = q_rows[(s ^ k) * 2 + side].astype(BF16)
        first = lax.dot_general(q, own[0:total, :], keys_t, preferred_element_type=F32) * scale
        second = lax.dot_general(q, peer[0:total, :], keys_t, preferred_element_type=F32) * scale
        first = jnp.where(keep_own, first, -jnp.inf)
        second = jnp.where(keep_peer, second, -jnp.inf)
        peak = jnp.maximum(
            jnp.max(first, axis=1, keepdims=True), jnp.max(second, axis=1, keepdims=True)
        )
        first = jnp.exp(first - peak)
        second = jnp.exp(second - peak)
        weight_sum = jnp.sum(first, axis=1, keepdims=True) + jnp.sum(second, axis=1, keepdims=True)
        weighted = dot(first.astype(BF16), own[total : 2 * total, :]) + dot(
            second.astype(BF16), peer[total : 2 * total, :]
        )
        ctx_outs[k][side * step : (side + 1) * step, :] = (weighted / weight_sum).astype(BF16)


def output_kernel(length, *refs):
    near, far, ctx = refs[: 2 * SEQ], refs[2 * SEQ : 2 * SEQ + 2], refs[2 * SEQ + 2 : 3 * SEQ + 2]
    share_out, send_out, context, weights = refs[3 * SEQ + 2 :]
    s, h, f, p = here()
    half = near[0].shape[1]
    columns = weights.shape[2]
    for core in range(2):
        first = (f ^ core) * 2 * half
        here_at = pl.ds(aligned(first + p * half, half), half)
        there_at = pl.ds(aligned(first + (1 - p) * half, half), half)
        for m in range(columns // HD):
            at = slice(m * HD, (m + 1) * HD)
            for k in range(SEQ):
                weights[s ^ k, here_at, at] = near[core * SEQ + k][3 + m]
                weights[k, there_at, at] = far[core][k, m]
    for k in range(SEQ):
        context[:, pl.ds(aligned((s ^ k) * HD, HD), HD)] = ctx[k][...]
    for j in range(SEQ):
        at = slice(j * columns, (j + 1) * columns)
        share = dot(context[...], weights[j])
        share_out[:, at] = share
        send_out[:, at] = share.astype(BF16)


def convolve_kernel(length, *refs):
    pieces, own_x, peer_x, halo_x, own_share, peer_share, gain, own_c, peer_c, base_out, share_out = refs[:11]
    mid, normed, w_value, w_gate, w_down, channel, padded, active, shares = refs[11:]
    s, h, f, p = here()
    valid_len = length[0]
    half, columns = pieces.shape[1:]
    rows = own_x.shape[0]
    step = rows + HALO
    for part in range(2):
        for plane in range(SEQ):
            for core in range(2):
                first = ((part * SEQ + plane) * 2 + core) * 3
                at = slice((2 * plane + part) * half, (2 * plane + part + 1) * half)
                w_value[core, at, :] = pieces[first]
                w_gate[core, at, :] = pieces[first + 1]
                at = slice((2 * core + part) * half, (2 * core + part + 1) * half)
                w_down[plane, at, :] = pieces[first + 2]
    channel[f] = own_c[...]
    channel[1 - f] = peer_c[...]
    mid[pl.ds(aligned(h * step, 8), rows), :] = own_x[...].astype(F32)
    mid[pl.ds(aligned((1 - h) * step, 8), rows), :] = peer_x[...].astype(F32)
    for b in range(2):
        mid[b * step + rows : (b + 1) * step, :] = halo_x[b * HALO : (b + 1) * HALO, :].astype(F32)
    middle = mid[...] + (own_share[...] + peer_share[...].astype(F32))
    mid[...] = middle
    normed[...] = layer_norm(middle, gain[...]).astype(BF16)
    place = lax.broadcasted_iota(jnp.int32, (step, columns), 0)
    offset = jnp.where(place < rows, place, jnp.where(place < rows + EDGE, place - rows - EDGE, place - EDGE))
    for c in range(2):
        x = normed[...]
        value_part = dot(x, w_value[c])
        gate_part = dot(x, w_gate[c])
        gated = value_part * jax.nn.sigmoid(gate_part)
        for b in range(2):
            t = offset + (4 * s + 2 * b + f) * rows
            kept = jnp.where((t >= 0) & (t < valid_len), gated[b * step : (b + 1) * step], 0.0)
            kept = kept.astype(BF16).astype(F32)
            padded[b, 8 : 8 + rows, :] = kept[:rows]
            padded[b, 8 - EDGE : 8, :] = kept[rows : rows + EDGE]
            padded[b, 8 + rows : 8 + rows + EDGE, :] = kept[rows + EDGE :]
            depth_sum = channel[c, 0:1, :] * padded[b, 8 - EDGE : 8 - EDGE + rows, :]
            for j in range(1, KERNEL):
                low = 8 - EDGE + j
                depth_sum = depth_sum + channel[c, j : j + 1, :] * padded[b, low : low + rows, :]
            shifted = depth_sum * channel[c, KERNEL : KERNEL + 1, :] + channel[c, KERNEL + 1 : KERNEL + 2, :]
            active[b * rows : (b + 1) * rows, c * columns : (c + 1) * columns] = (
                shifted * jax.nn.sigmoid(shifted)
            ).astype(BF16)
    for j in range(SEQ):
        shares[:, j * columns : (j + 1) * columns] = dot(active[...], w_down[j])
    base_out[...] = mid[pl.ds(aligned(h * step, 8), rows), :] + shares[pl.ds(aligned(h * rows, rows), rows), :]
    share_out[...] = shares[pl.ds(aligned((1 - h) * rows, rows), rows), :].astype(BF16)


def shards_chip_per_head(
    frames,
    length,
    ln1_gain,
    w_query,
    w_key,
    w_value,
    w_out,
    ln2_gain,
    pw1_value,
    pw1_gate,
    depth_kernel,
    bn_scale,
    bn_shift,
    pw2,
):
    rows, width = frames.shape
    count = 2 * SEQ
    step = rows + HALO
    f, p = lax.axis_index("fsdp"), lax.axis_index("parts")
    half = w_query.shape[0] // 2
    columns = w_query.shape[1]
    barrier = lax.optimization_barrier

    def other_core(x):
        return lax.ppermute(x, "fsdp", SWAP)

    def other_side(x):
        return lax.ppermute(x, "head", SWAP)

    def other_part(x):
        return lax.ppermute(x, "parts", SWAP)

    def planes(x):
        return [x] + [lax.ppermute(x, "seq", xor_pairs(k)) for k in range(1, SEQ)]

    def part_half(x):
        return lax.dynamic_slice_in_dim(x, p * half, half, axis=x.ndim - 2)

    near = planes(frames)
    blocks = []
    for block in near:
        blocks += [block, other_side(block)]
    pw_mine = part_half(jnp.stack([pw1_value, pw1_gate, pw2]))
    pw_all = lax.all_gather(pw_mine, ("parts", "seq", "fsdp"), axis=0, tiled=True)
    given = [w_query, w_key, w_value]
    shape = jax.ShapeDtypeStruct
    dealt = call(
        deal_kernel,
        [shape((3 + columns // HD, half, HD), BF16)] * SEQ,
        [pltpu.VMEM((4, 2 * half, columns), BF16), pltpu.SemaphoreType.DMA((4,))],
        length,
        *given,
        w_out,
        *[other_core(w) for w in given],
        left=4,
    )
    w_mine = [dealt[0]] + [lax.ppermute(dealt[k], "seq", xor_pairs(k)) for k in range(1, SEQ)]
    w_other = [other_core(w) for w in w_mine]
    queries, send, edges, stack = call(
        project_kernel,
        [
            shape((count * rows, HD), BF16),
            shape((2 * count * rows + count * HALO, HD), BF16),
            shape((2 * HALO, width), BF16),
            shape((SEQ, columns // HD, half, HD), BF16),
        ],
        [
            pltpu.VMEM((count * rows, width), BF16),
            pltpu.VMEM((width, 3 * HD), BF16),
            pltpu.VMEM((count, HALO, width), F32),
            pltpu.VMEM((count, HALO, HD), F32),
        ],
        length,
        *blocks,
        *w_mine,
        *w_other,
        ln1_gain[None],
    )
    received = other_core(send)
    stack_part = other_part(stack)
    halo_x = other_core(edges)
    ctx = call(
        attend_kernel,
        [shape((2 * step, HD), BF16)] * SEQ,
        [pltpu.VMEM((count, step, HD), F32)],
        length,
        queries,
        send,
        received,
    )
    depth_kernel, stack_part, *_ = barrier((depth_kernel, stack_part, *ctx))
    far = [stack_part, other_core(stack_part)]
    channels = jnp.concatenate([depth_kernel, bn_scale[None], bn_shift[None], jnp.zeros((5, columns), F32)])
    channels_peer = other_core(channels)
    ctx = [ctx[0]] + [lax.ppermute(ctx[k], "seq", xor_pairs(k)) for k in range(1, SEQ)]
    own_share, sent_share = call(
        output_kernel,
        [shape((2 * step, width), F32), shape((2 * step, width), BF16)],
        [
            pltpu.VMEM((2 * step, SEQ * HD), BF16),
            pltpu.VMEM((SEQ, 2 * columns, columns), BF16),
        ],
        length,
        *w_mine,
        *w_other,
        *far,
        *ctx,
    )
    base, share = call(
        convolve_kernel,
        [shape((rows, width), F32), shape((rows, width), BF16)],
        [
            pltpu.VMEM((2 * step, width), F32),
            pltpu.VMEM((2 * step, width), BF16),
            pltpu.VMEM((2, width, columns), BF16),
            pltpu.VMEM((2, width, columns), BF16),
            pltpu.VMEM((SEQ, 2 * columns, columns), BF16),
            pltpu.VMEM((2, 16, columns), F32),
            pltpu.VMEM((2, 16 + rows, columns), F32),
            pltpu.VMEM((2 * rows, 2 * columns), BF16),
            pltpu.VMEM((2 * rows, width), F32),
        ],
        length,
        pw_all,
        frames,
        blocks[1],
        halo_x,
        own_share,
        other_side(sent_share),
        ln2_gain[None],
        channels,
        channels_peer,
        vmem=14,
    )
    return (base + other_side(share).astype(F32)).astype(BF16)


def solution(mesh):
    in_specs = (
        P(("parts", "seq", "head", "fsdp"), None),
        P("parts"),
        P(),
        P("seq", ("head", "fsdp")),
        P("seq", ("head", "fsdp")),
        P("seq", ("head", "fsdp")),
        P(("head", "fsdp"), "seq"),
        P(),
        P("seq", ("head", "fsdp")),
        P("seq", ("head", "fsdp")),
        P(None, ("head", "fsdp")),
        P(("head", "fsdp")),
        P(("head", "fsdp")),
        P(("head", "fsdp"), "seq"),
    )
    out_specs = P(("parts", "seq", "head", "fsdp"), None)
    body = shards_chip_per_head if one_head_per_chip(mesh) else shards_general
    return jax.shard_map(body, mesh=mesh, in_specs=in_specs, out_specs=out_specs, check_vma=False)
```

```python
import math

import jax
import jax.numpy as jnp
from jax import lax
from jax.experimental import pallas as pl
from jax.experimental.pallas import tpu as pltpu
from jax.sharding import PartitionSpec as P

KERNEL = 9
HD = 128


def with_halo(block, sides, width):
    for axis, dim in sides:
        count = lax.axis_size(axis)
        forward = [(i, i + 1) for i in range(count - 1)]
        backward = [(target, source) for source, target in forward]
        low = lax.ppermute(
            lax.slice_in_dim(block, block.shape[dim] - width, None, axis=dim), axis, forward
        )
        high = lax.ppermute(lax.slice_in_dim(block, 0, width, axis=dim), axis, backward)
        block = jnp.concatenate([low, block, high], axis=dim)
    return block


def layer_norm(values_in, gain_vec):
    center = jnp.mean(values_in, axis=-1, keepdims=True)
    shifted = values_in - center
    spread = jnp.mean(shifted * shifted, axis=-1, keepdims=True)
    return shifted * lax.rsqrt(spread + 1e-05) * gain_vec


def shards_general(
    frames,
    length,
    ln1_gain,
    w_query,
    w_key,
    w_value,
    w_out,
    ln2_gain,
    pw1_value,
    pw1_gate,
    depth_kernel,
    bn_scale,
    bn_shift,
    pw2,
):
    group_size = lax.axis_size(("head", "fsdp"))
    my_rows = frames.shape[0]
    block_rows = my_rows * group_size
    head_cols = w_query.shape[1]
    heads_here = head_cols // HD
    seq_start = lax.axis_index("seq") * block_rows
    valid_len = length[0]
    score_scale = 1.0 / math.sqrt(HD)
    full_query, full_key, full_value, value_cols, gate_cols = (
        lax.all_gather(w_query, "seq", axis=0, tiled=True),
        lax.all_gather(w_key, "seq", axis=0, tiled=True),
        lax.all_gather(w_value, "seq", axis=0, tiled=True),
        lax.all_gather(pw1_value, "seq", axis=0, tiled=True),
        lax.all_gather(pw1_gate, "seq", axis=0, tiled=True),
    )
    out_rows, down_rows = (
        lax.all_gather(w_out, "seq", axis=1, tiled=True),
        lax.all_gather(pw2, "seq", axis=1, tiled=True),
    )
    projector = jnp.concatenate((full_query, full_key, full_value), axis=1)
    source = frames.astype(jnp.float32)
    normed = layer_norm(source, ln1_gain).astype(jnp.bfloat16)
    projected = jnp.dot(
        lax.all_gather(normed, ("head", "fsdp"), axis=0, tiled=True),
        projector,
        preferred_element_type=jnp.float32,
    ).astype(jnp.bfloat16)
    queries = projected[:, :head_cols].reshape(block_rows, heads_here, HD)
    keys_here = projected[:, head_cols : 2 * head_cols]
    values_here = projected[:, 2 * head_cols :]
    initial = (
        jnp.full((heads_here, block_rows), -1e30, jnp.float32),
        jnp.zeros((heads_here, block_rows), jnp.float32),
        jnp.zeros((heads_here, block_rows, HD), jnp.float32),
    )
    key_piece = lax.all_gather(keys_here, "seq", axis=0, tiled=True)
    value_piece = lax.all_gather(values_here, "seq", axis=0, tiled=True)
    row_count = key_piece.shape[0]
    block_size = math.gcd(row_count, 512)
    block_count = row_count // block_size
    key_blocks = key_piece.reshape(block_count, block_size, heads_here, HD)
    value_blocks = value_piece.reshape(block_count, block_size, heads_here, HD)
    places = jnp.arange(row_count, dtype=jnp.int32).reshape(block_count, block_size)

    def advance(inner_state, block_item):
        key_block, value_block, place = block_item
        peak_score, weight_sum, weighted = inner_state
        scores = (
            jnp.einsum("qhd,khd->hqk", queries, key_block, preferred_element_type=jnp.float32)
            * score_scale
        )
        scores = jnp.where((place < valid_len)[None, None, :], scores, -jnp.inf)
        new_peak = jnp.maximum(peak_score, jnp.max(scores, axis=2))
        factor = jnp.exp(peak_score - new_peak)
        weights = jnp.exp(scores - new_peak[:, :, None])
        weight_sum = weight_sum * factor + jnp.sum(weights, axis=2)
        weighted = weighted * factor[:, :, None] + jnp.einsum(
            "hqk,khd->hqd",
            weights.astype(jnp.bfloat16),
            value_block,
            preferred_element_type=jnp.float32,
        )
        return ((new_peak, weight_sum, weighted), None)

    result, unused = lax.scan(advance, initial, (key_blocks, value_blocks, places))
    peak_score, weight_sum, weighted = result
    context = (
        (weighted / weight_sum[:, :, None])
        .astype(jnp.bfloat16)
        .transpose(1, 0, 2)
        .reshape(block_rows, head_cols)
    )
    attended = lax.psum_scatter(
        jnp.dot(context, out_rows, preferred_element_type=jnp.float32).astype(jnp.bfloat16),
        ("head", "fsdp"),
        scatter_dimension=0,
        tiled=True,
    ).astype(jnp.float32)
    middle = source + attended
    normed_two = layer_norm(middle, ln2_gain).astype(jnp.bfloat16)
    piece = lax.all_gather(normed_two, ("head", "fsdp"), axis=0, tiled=True)
    value_part = jnp.dot(piece, value_cols, preferred_element_type=jnp.float32)
    gate_part = jnp.dot(piece, gate_cols, preferred_element_type=jnp.float32)
    places = seq_start + jnp.arange(piece.shape[0], dtype=jnp.int32)
    gated_rows = jnp.where(
        (places < valid_len)[:, None], value_part * jax.nn.sigmoid(gate_part), 0.0
    ).astype(jnp.bfloat16)
    rim_width = (KERNEL - 1) // 2
    padded = with_halo(gated_rows, (("seq", 0),), rim_width).astype(jnp.float32)
    depth_sum = depth_kernel[0] * padded[0:block_rows]
    for offset in range(1, KERNEL):
        depth_sum = depth_sum + depth_kernel[offset] * padded[offset : offset + block_rows]
    shifted = depth_sum * bn_scale + bn_shift
    active = (shifted * jax.nn.sigmoid(shifted)).astype(jnp.bfloat16)
    conv_part = lax.psum_scatter(
        jnp.dot(active, down_rows, preferred_element_type=jnp.float32).astype(jnp.bfloat16),
        ("head", "fsdp"),
        scatter_dimension=0,
        tiled=True,
    ).astype(jnp.float32)
    return (middle + conv_part).astype(jnp.bfloat16)


SEQ = 4
EDGE = (KERNEL - 1) // 2
HALO = 2 * EDGE
SWAP = [(0, 1), (1, 0)]
F32 = jnp.float32
BF16 = jnp.bfloat16


def one_head_per_chip(mesh):
    return dict(mesh.shape) == {"parts": 2, "seq": SEQ, "head": 2, "fsdp": 2}


def xor_pairs(k):
    return [(i, i ^ k) for i in range(SEQ)]


def call(kernel, outs, scratch, length, *operands, vmem=8, left=0):
    fixed = [pltpu.with_memory_space_constraint(a, pltpu.HBM) for a in operands[:left]]
    return pl.pallas_call(
        kernel,
        out_shape=outs,
        in_specs=[pl.BlockSpec(memory_space=pltpu.SMEM)]
        + [pl.BlockSpec(memory_space=pltpu.HBM)] * left
        + [pl.BlockSpec(memory_space=pltpu.VMEM)] * (len(operands) - left),
        out_specs=[pl.BlockSpec(memory_space=pltpu.VMEM)] * len(outs),
        scratch_shapes=scratch,
        cost_estimate=pl.CostEstimate(flops=0, bytes_accessed=0, transcendentals=0),
        compiler_params=pltpu.CompilerParams(vmem_limit_bytes=vmem << 20),
    )(length, *fixed, *operands[left:])


def aligned(value, to):
    return pl.multiple_of(value, to)


def dot(a, b):
    return jnp.dot(a, b, preferred_element_type=F32)


def here():
    return tuple(lax.axis_index(a) for a in ("seq", "head", "fsdp", "parts"))


def deal_kernel(length, *refs):
    sources, later, other = refs[:4], refs[4:7], refs[7:10]
    outs, later_out, held, sems, later_sems = refs[10:14], *refs[14:]
    s, _, f, p = here()
    half = outs[0].shape[1]
    copies = [pltpu.make_async_copy(w, held.at[i], sems.at[i]) for i, w in enumerate(sources)]
    at = pl.ds(aligned(p * half, half), half)
    later_copies = [
        pltpu.make_async_copy(w.at[at], later_out.at[i], later_sems.at[i]) for i, w in enumerate(later)
    ]
    for copy in copies + later_copies:
        copy.start()
    mine, w_out = [held.at[m] for m in range(3)], held.at[3]
    for copy in copies:
        copy.wait()
    rows = pl.ds(aligned(f * half, half), half)
    for k in range(SEQ):
        head = s ^ k
        columns = pl.ds(aligned((head % 2) * HD, HD), HD)

        @pl.when(head // 2 == f)
        def _():
            for m in range(3):
                outs[k][m] = mine[m][rows, columns]

        @pl.when(head // 2 != f)
        def _():
            for m in range(3):
                outs[k][m] = other[m][rows, columns]

        for m in range(outs[k].shape[0] - 3):
            outs[k][3 + m] = w_out[at, m * HD : (m + 1) * HD]
    for copy in later_copies:
        copy.wait()


def stack_kernel(length, *refs):
    s = lax.axis_index("seq")
    for k in range(SEQ):
        refs[SEQ][s ^ k] = refs[k][...]


def project_kernel(length, *refs):
    frames, gain, *blocks = refs[: 2 * SEQ + 1]
    mine, other, down = refs[2 * SEQ + 1 : 3 * SEQ + 1], refs[3 * SEQ + 1 : 4 * SEQ + 1], refs[4 * SEQ + 1]
    q_out, send_out, edge_out, stack_out, normed, weights, x_edge, q_edge, own_x, own_gain, sems = refs[4 * SEQ + 2 :]
    copies = [
        pltpu.make_async_copy(frames, own_x, sems.at[0]),
        pltpu.make_async_copy(gain, own_gain, sems.at[1]),
    ]
    for copy in copies:
        copy.start()
    s, h, f, _ = here()
    blocks = [own_x, *blocks]
    rows = blocks[0].shape[0]
    half = mine[0].shape[1]
    for copy in copies:
        copy.wait()
    gain_row = own_gain[...]
    for slot, block in enumerate(blocks):
        at = (s ^ (slot // 2)) * 2 + (h ^ (slot % 2))
        x = block[...].astype(F32)
        normed[pl.ds(aligned(at * rows, rows), rows), :] = layer_norm(x, gain_row).astype(BF16)
        x_edge[at, 0:EDGE, :] = x[:EDGE]
        x_edge[at, EDGE:HALO, :] = x[rows - EDGE :]
    for k in range(SEQ):
        for core, pieces in enumerate((mine, other)):
            at = pl.ds(aligned((s ^ k) * 2 * half + (f ^ core) * half, half), half)
            for m in range(3):
                weights[at, m * HD : (m + 1) * HD] = pieces[k][m]
        stack_out[s ^ k] = down[...] if k == 2 else mine[k][3:]
    count = 2 * SEQ
    total = count * rows
    projected = dot(normed[...], weights[...])
    q_out[...] = projected[:, :HD].astype(BF16)
    send_out[0:total, :] = projected[:, HD : 2 * HD].astype(BF16)
    send_out[total : 2 * total, :] = projected[:, 2 * HD :].astype(BF16)
    for b in range(count):
        q_edge[b, 0:EDGE, :] = projected[b * rows : b * rows + EDGE, :HD]
        q_edge[b, EDGE:HALO, :] = projected[(b + 1) * rows - EDGE : (b + 1) * rows, :HD]

    def around(edge, b):
        low = jnp.maximum(b - f, 0)
        high = jnp.minimum(b + 1 - f, count - 1)
        return jnp.concatenate([edge[low, EDGE:HALO, :], edge[high, 0:EDGE, :]], axis=0)

    halos = jnp.concatenate([around(q_edge, b) for b in range(count)], axis=0)
    send_out[2 * total :, :] = halos.astype(BF16)
    edge_out[...] = jnp.concatenate([around(x_edge, s * 2 + b) for b in range(2)], axis=0).astype(BF16)


def attend_kernel(length, q_in, own, peer, *refs):
    ctx_outs, q_rows = refs[:SEQ], refs[SEQ]
    s, _, f, _ = here()
    valid_len = length[0]
    count = q_rows.shape[0]
    total = q_in.shape[0]
    rows = total // count
    step = q_rows.shape[1]
    local = lax.broadcasted_iota(jnp.int32, (step, total), 1)
    base = (local // rows) * (2 * rows) + local % rows
    keep_own = base + f * rows < valid_len
    keep_peer = base + (1 - f) * rows < valid_len
    scale = 1.0 / math.sqrt(HD)
    keys_t = (((1,), (1,)), ((), ()))
    for b in range(count):
        q_rows[b, 0:rows, :] = q_in[b * rows : (b + 1) * rows, :].astype(F32)
        q_rows[b, rows:step, :] = peer[2 * total + b * HALO : 2 * total + (b + 1) * HALO, :].astype(F32)
    for b in range(count):
        k, side = b // 2, b % 2
        q = q_rows[(s ^ k) * 2 + side].astype(BF16)
        first = lax.dot_general(q, own[0:total, :], keys_t, preferred_element_type=F32) * scale
        second = lax.dot_general(q, peer[0:total, :], keys_t, preferred_element_type=F32) * scale
        first = jnp.where(keep_own, first, -jnp.inf)
        second = jnp.where(keep_peer, second, -jnp.inf)
        peak = jnp.maximum(
            jnp.max(first, axis=1, keepdims=True), jnp.max(second, axis=1, keepdims=True)
        )
        first = jnp.exp(first - peak)
        second = jnp.exp(second - peak)
        weight_sum = jnp.sum(first, axis=1, keepdims=True) + jnp.sum(second, axis=1, keepdims=True)
        weighted = dot(first.astype(BF16), own[total : 2 * total, :]) + dot(
            second.astype(BF16), peer[total : 2 * total, :]
        )
        ctx_outs[k][side * step : (side + 1) * step, :] = (weighted / weight_sum).astype(BF16)


def output_kernel(length, *refs):
    pieces, ctx = refs[:4], refs[4 : 4 + SEQ]
    share_out, send_out, context, weights = refs[4 + SEQ :]
    s, h, f, p = here()
    half = pieces[0].shape[2]
    columns = weights.shape[2]
    for y in range(2):
        for core in range(2):
            rows = pl.ds(aligned((f ^ core) * 2 * half + (p ^ y) * half, half), half)
            for m in range(columns // HD):
                for j in range(SEQ):
                    weights[j, rows, m * HD : (m + 1) * HD] = pieces[y * 2 + core][j, m]
    for k in range(SEQ):
        context[:, pl.ds(aligned((s ^ k) * HD, HD), HD)] = ctx[k][...]
    for j in range(SEQ):
        at = slice(j * columns, (j + 1) * columns)
        share = dot(context[...], weights[j])
        share_out[:, at] = share
        send_out[:, at] = share.astype(BF16)


def convolve_kernel(length, *refs):
    pieces = refs[:4]
    own_x, peer_x, halo_x, own_share, peer_share, gain, own_c, peer_c, base_out, share_out = refs[4:14]
    mid, normed, w_value, w_gate, w_down, channel, padded, active, shares = refs[14:]
    s, h, f, p = here()
    valid_len = length[0]
    half, columns = pieces[0].shape[2:]
    rows = own_x.shape[0]
    step = rows + HALO
    for y in range(2):
        for core in range(2):
            stack = pieces[y * 2 + core]
            down = pl.ds(aligned((f ^ core) * 2 * half + (p ^ y) * half, half), half)
            for plane in range(SEQ):
                at = pl.ds(aligned(plane * 2 * half + (p ^ y) * half, half), half)
                w_value[f ^ core, at, :] = stack[plane, 0]
                w_gate[f ^ core, at, :] = stack[plane, 1]
                w_down[plane, down, :] = stack[plane, 2]
    channel[f] = own_c[...]
    channel[1 - f] = peer_c[...]
    mid[pl.ds(aligned(h * step, 8), rows), :] = own_x[...].astype(F32)
    mid[pl.ds(aligned((1 - h) * step, 8), rows), :] = peer_x[...].astype(F32)
    for b in range(2):
        mid[b * step + rows : (b + 1) * step, :] = halo_x[b * HALO : (b + 1) * HALO, :].astype(F32)
    middle = mid[...] + (own_share[...] + peer_share[...].astype(F32))
    mid[...] = middle
    normed[...] = layer_norm(middle, gain[...]).astype(BF16)
    place = lax.broadcasted_iota(jnp.int32, (step, columns), 0)
    offset = jnp.where(place < rows, place, jnp.where(place < rows + EDGE, place - rows - EDGE, place - EDGE))
    for c in range(2):
        x = normed[...]
        value_part = dot(x, w_value[c])
        gate_part = dot(x, w_gate[c])
        gated = value_part * jax.nn.sigmoid(gate_part)
        for b in range(2):
            t = offset + (4 * s + 2 * b + f) * rows
            kept = jnp.where((t >= 0) & (t < valid_len), gated[b * step : (b + 1) * step], 0.0)
            kept = kept.astype(BF16).astype(F32)
            padded[b, 8 : 8 + rows, :] = kept[:rows]
            padded[b, 8 - EDGE : 8, :] = kept[rows : rows + EDGE]
            padded[b, 8 + rows : 8 + rows + EDGE, :] = kept[rows + EDGE :]
            depth_sum = channel[c, 0:1, :] * padded[b, 8 - EDGE : 8 - EDGE + rows, :]
            for j in range(1, KERNEL):
                low = 8 - EDGE + j
                depth_sum = depth_sum + channel[c, j : j + 1, :] * padded[b, low : low + rows, :]
            shifted = depth_sum * channel[c, KERNEL : KERNEL + 1, :] + channel[c, KERNEL + 1 : KERNEL + 2, :]
            active[b * rows : (b + 1) * rows, c * columns : (c + 1) * columns] = (
                shifted * jax.nn.sigmoid(shifted)
            ).astype(BF16)
    for j in range(SEQ):
        shares[:, j * columns : (j + 1) * columns] = dot(active[...], w_down[j])
    base_out[...] = mid[pl.ds(aligned(h * step, 8), rows), :] + shares[pl.ds(aligned(h * rows, rows), rows), :]
    share_out[...] = shares[pl.ds(aligned((1 - h) * rows, rows), rows), :].astype(BF16)


def shards_chip_per_head(
    frames,
    length,
    ln1_gain,
    w_query,
    w_key,
    w_value,
    w_out,
    ln2_gain,
    pw1_value,
    pw1_gate,
    depth_kernel,
    bn_scale,
    bn_shift,
    pw2,
):
    rows, width = frames.shape
    count = 2 * SEQ
    step = rows + HALO
    f, p = lax.axis_index("fsdp"), lax.axis_index("parts")
    half = w_query.shape[0] // 2
    columns = w_query.shape[1]
    barrier = lax.optimization_barrier

    def other_core(x):
        return lax.ppermute(x, "fsdp", SWAP)

    def other_side(x):
        return lax.ppermute(x, "head", SWAP)

    def other_part(x):
        return lax.ppermute(x, "parts", SWAP)

    def across(x, k):
        return lax.ppermute(x, "seq", xor_pairs(k))

    def planes(x):
        far = across(x, 3)
        return [x, across(x, 1), across(far, 1), far]

    def part_half(x):
        return lax.dynamic_slice_in_dim(x, p * half, half, axis=x.ndim - 2)

    near = planes(frames)
    blocks = []
    for block in near:
        blocks += [block, other_side(block)]
    given = [w_query, w_key, w_value]
    shape = jax.ShapeDtypeStruct
    *dealt, pw_mine = call(
        deal_kernel,
        [shape((3 if k == 2 else 3 + columns // HD, half, HD), BF16) for k in range(SEQ)]
        + [shape((3, half, columns), BF16)],
        [
            pltpu.VMEM((4, 2 * half, columns), BF16),
            pltpu.SemaphoreType.DMA((4,)),
            pltpu.SemaphoreType.DMA((3,)),
        ],
        length,
        *given,
        w_out,
        pw1_value,
        pw1_gate,
        pw2,
        *[other_core(w) for w in given],
        left=7,
    )
    *dealt, _ = barrier((*dealt, near[1]))
    w_mine = [dealt[0]] + [across(dealt[k], k) for k in range(1, SEQ)]
    w_other = [other_core(w[:3]) for w in w_mine]
    down = across(w_mine[3][3:], 1)
    pw_part = other_part(pw_mine)
    w_other[0], pw_part = barrier((w_other[0], pw_part))
    after, *_ = barrier((pw_mine, *w_mine[1:], down))
    pw_one, pw_three = across(after, 1), across(after, 3)
    queries, send, edges, stack = call(
        project_kernel,
        [
            shape((count * rows, HD), BF16),
            shape((2 * count * rows + count * HALO, HD), BF16),
            shape((2 * HALO, width), BF16),
            shape((SEQ, columns // HD, half, HD), BF16),
        ],
        [
            pltpu.VMEM((count * rows, width), BF16),
            pltpu.VMEM((width, 3 * HD), BF16),
            pltpu.VMEM((count, HALO, width), F32),
            pltpu.VMEM((count, HALO, HD), F32),
            pltpu.VMEM((rows, width), BF16),
            pltpu.VMEM((1, width), F32),
            pltpu.SemaphoreType.DMA((2,)),
        ],
        length,
        frames,
        ln1_gain[None],
        *blocks[1:],
        *w_mine,
        *w_other,
        down,
        left=2,
    )
    received = other_core(send)
    stack_part = other_part(stack)
    ctx = call(
        attend_kernel,
        [shape((2 * step, HD), BF16)] * SEQ,
        [pltpu.VMEM((count, step, HD), F32)],
        length,
        queries,
        send,
        received,
    )
    stack, stack_part, *_ = barrier((stack, stack_part, *ctx))
    out_pieces = [stack, other_core(stack), stack_part, other_core(stack_part)]
    ctx = [ctx[0]] + [lax.ppermute(ctx[k], "seq", xor_pairs(k)) for k in range(1, SEQ)]
    pw_one, pw_three, *ctx = barrier((pw_one, pw_three, *ctx))
    pw_two = across(pw_three, 1)
    one_part, three_part = other_part(pw_one), other_part(pw_three)
    own_share, sent_share = call(
        output_kernel,
        [shape((2 * step, width), F32), shape((2 * step, width), BF16)],
        [
            pltpu.VMEM((2 * step, SEQ * HD), BF16),
            pltpu.VMEM((SEQ, 2 * columns, columns), BF16),
        ],
        length,
        *out_pieces,
        *ctx,
    )
    own_share, edges, depth_kernel = barrier((own_share, edges, depth_kernel))
    halo_x = other_core(edges)
    channels = jnp.concatenate([depth_kernel, bn_scale[None], bn_shift[None], jnp.zeros((5, columns), F32)])
    channels_peer = other_core(channels)
    peer_share = other_side(sent_share)

    def stacked(*pieces):
        (stack,) = call(stack_kernel, [shape((SEQ, *pieces[0].shape), BF16)], [], length, *pieces)
        return [stack, other_core(stack)]

    two_part = other_part(pw_two)
    pw_mine, _ = barrier((pw_mine, peer_share))
    pw_pieces = stacked(pw_mine, pw_one, pw_two, pw_three) + stacked(pw_part, one_part, two_part, three_part)
    base, share = call(
        convolve_kernel,
        [shape((rows, width), F32), shape((rows, width), BF16)],
        [
            pltpu.VMEM((2 * step, width), F32),
            pltpu.VMEM((2 * step, width), BF16),
            pltpu.VMEM((2, width, columns), BF16),
            pltpu.VMEM((2, width, columns), BF16),
            pltpu.VMEM((SEQ, 2 * columns, columns), BF16),
            pltpu.VMEM((2, 16, columns), F32),
            pltpu.VMEM((2, 16 + rows, columns), F32),
            pltpu.VMEM((2 * rows, 2 * columns), BF16),
            pltpu.VMEM((2 * rows, width), F32),
        ],
        length,
        *pw_pieces,
        frames,
        blocks[1],
        halo_x,
        own_share,
        peer_share,
        ln2_gain[None],
        channels,
        channels_peer,
        vmem=14,
    )
    return (base + other_side(share).astype(F32)).astype(BF16)


def solution(mesh):
    in_specs = (
        P(("parts", "seq", "head", "fsdp"), None),
        P("parts"),
        P(),
        P("seq", ("head", "fsdp")),
        P("seq", ("head", "fsdp")),
        P("seq", ("head", "fsdp")),
        P(("head", "fsdp"), "seq"),
        P(),
        P("seq", ("head", "fsdp")),
        P("seq", ("head", "fsdp")),
        P(None, ("head", "fsdp")),
        P(("head", "fsdp")),
        P(("head", "fsdp")),
        P(("head", "fsdp"), "seq"),
    )
    out_specs = P(("parts", "seq", "head", "fsdp"), None)
    body = shards_chip_per_head if one_head_per_chip(mesh) else shards_general
    return jax.shard_map(body, mesh=mesh, in_specs=in_specs, out_specs=out_specs, check_vma=False)
```

```python
import math

import jax
import jax.numpy as jnp
from jax import lax
from jax.experimental import pallas as pl
from jax.experimental.pallas import tpu as pltpu
from jax.sharding import PartitionSpec as P

KERNEL = 9
HD = 128


def with_halo(block, sides, width):
    for axis, dim in sides:
        count = lax.axis_size(axis)
        forward = [(i, i + 1) for i in range(count - 1)]
        backward = [(target, source) for source, target in forward]
        low = lax.ppermute(
            lax.slice_in_dim(block, block.shape[dim] - width, None, axis=dim), axis, forward
        )
        high = lax.ppermute(lax.slice_in_dim(block, 0, width, axis=dim), axis, backward)
        block = jnp.concatenate([low, block, high], axis=dim)
    return block


def layer_norm(values_in, gain_vec):
    center = jnp.mean(values_in, axis=-1, keepdims=True)
    shifted = values_in - center
    spread = jnp.mean(shifted * shifted, axis=-1, keepdims=True)
    return shifted * lax.rsqrt(spread + 1e-05) * gain_vec


def shards_general(
    frames,
    length,
    ln1_gain,
    w_query,
    w_key,
    w_value,
    w_out,
    ln2_gain,
    pw1_value,
    pw1_gate,
    depth_kernel,
    bn_scale,
    bn_shift,
    pw2,
):
    group_size = lax.axis_size(("head", "fsdp"))
    my_rows = frames.shape[0]
    block_rows = my_rows * group_size
    head_cols = w_query.shape[1]
    heads_here = head_cols // HD
    seq_start = lax.axis_index("seq") * block_rows
    valid_len = length[0]
    score_scale = 1.0 / math.sqrt(HD)
    full_query, full_key, full_value, value_cols, gate_cols = (
        lax.all_gather(w_query, "seq", axis=0, tiled=True),
        lax.all_gather(w_key, "seq", axis=0, tiled=True),
        lax.all_gather(w_value, "seq", axis=0, tiled=True),
        lax.all_gather(pw1_value, "seq", axis=0, tiled=True),
        lax.all_gather(pw1_gate, "seq", axis=0, tiled=True),
    )
    out_rows, down_rows = (
        lax.all_gather(w_out, "seq", axis=1, tiled=True),
        lax.all_gather(pw2, "seq", axis=1, tiled=True),
    )
    projector = jnp.concatenate((full_query, full_key, full_value), axis=1)
    source = frames.astype(jnp.float32)
    normed = layer_norm(source, ln1_gain).astype(jnp.bfloat16)
    projected = jnp.dot(
        lax.all_gather(normed, ("head", "fsdp"), axis=0, tiled=True),
        projector,
        preferred_element_type=jnp.float32,
    ).astype(jnp.bfloat16)
    queries = projected[:, :head_cols].reshape(block_rows, heads_here, HD)
    keys_here = projected[:, head_cols : 2 * head_cols]
    values_here = projected[:, 2 * head_cols :]
    initial = (
        jnp.full((heads_here, block_rows), -1e30, jnp.float32),
        jnp.zeros((heads_here, block_rows), jnp.float32),
        jnp.zeros((heads_here, block_rows, HD), jnp.float32),
    )
    key_piece = lax.all_gather(keys_here, "seq", axis=0, tiled=True)
    value_piece = lax.all_gather(values_here, "seq", axis=0, tiled=True)
    row_count = key_piece.shape[0]
    block_size = math.gcd(row_count, 512)
    block_count = row_count // block_size
    key_blocks = key_piece.reshape(block_count, block_size, heads_here, HD)
    value_blocks = value_piece.reshape(block_count, block_size, heads_here, HD)
    places = jnp.arange(row_count, dtype=jnp.int32).reshape(block_count, block_size)

    def advance(inner_state, block_item):
        key_block, value_block, place = block_item
        peak_score, weight_sum, weighted = inner_state
        scores = (
            jnp.einsum("qhd,khd->hqk", queries, key_block, preferred_element_type=jnp.float32)
            * score_scale
        )
        scores = jnp.where((place < valid_len)[None, None, :], scores, -jnp.inf)
        new_peak = jnp.maximum(peak_score, jnp.max(scores, axis=2))
        factor = jnp.exp(peak_score - new_peak)
        weights = jnp.exp(scores - new_peak[:, :, None])
        weight_sum = weight_sum * factor + jnp.sum(weights, axis=2)
        weighted = weighted * factor[:, :, None] + jnp.einsum(
            "hqk,khd->hqd",
            weights.astype(jnp.bfloat16),
            value_block,
            preferred_element_type=jnp.float32,
        )
        return ((new_peak, weight_sum, weighted), None)

    result, unused = lax.scan(advance, initial, (key_blocks, value_blocks, places))
    peak_score, weight_sum, weighted = result
    context = (
        (weighted / weight_sum[:, :, None])
        .astype(jnp.bfloat16)
        .transpose(1, 0, 2)
        .reshape(block_rows, head_cols)
    )
    attended = lax.psum_scatter(
        jnp.dot(context, out_rows, preferred_element_type=jnp.float32).astype(jnp.bfloat16),
        ("head", "fsdp"),
        scatter_dimension=0,
        tiled=True,
    ).astype(jnp.float32)
    middle = source + attended
    normed_two = layer_norm(middle, ln2_gain).astype(jnp.bfloat16)
    piece = lax.all_gather(normed_two, ("head", "fsdp"), axis=0, tiled=True)
    value_part = jnp.dot(piece, value_cols, preferred_element_type=jnp.float32)
    gate_part = jnp.dot(piece, gate_cols, preferred_element_type=jnp.float32)
    places = seq_start + jnp.arange(piece.shape[0], dtype=jnp.int32)
    gated_rows = jnp.where(
        (places < valid_len)[:, None], value_part * jax.nn.sigmoid(gate_part), 0.0
    ).astype(jnp.bfloat16)
    rim_width = (KERNEL - 1) // 2
    padded = with_halo(gated_rows, (("seq", 0),), rim_width).astype(jnp.float32)
    depth_sum = depth_kernel[0] * padded[0:block_rows]
    for offset in range(1, KERNEL):
        depth_sum = depth_sum + depth_kernel[offset] * padded[offset : offset + block_rows]
    shifted = depth_sum * bn_scale + bn_shift
    active = (shifted * jax.nn.sigmoid(shifted)).astype(jnp.bfloat16)
    conv_part = lax.psum_scatter(
        jnp.dot(active, down_rows, preferred_element_type=jnp.float32).astype(jnp.bfloat16),
        ("head", "fsdp"),
        scatter_dimension=0,
        tiled=True,
    ).astype(jnp.float32)
    return (middle + conv_part).astype(jnp.bfloat16)


SEQ = 4
EDGE = (KERNEL - 1) // 2
HALO = 2 * EDGE
SWAP = [(0, 1), (1, 0)]
F32 = jnp.float32
BF16 = jnp.bfloat16


def one_head_per_chip(mesh):
    return dict(mesh.shape) == {"parts": 2, "seq": SEQ, "head": 2, "fsdp": 2}


def xor_pairs(k):
    return [(i, i ^ k) for i in range(SEQ)]


def call(kernel, outs, scratch, length, *operands, vmem=8, left=0):
    fixed = [pltpu.with_memory_space_constraint(a, pltpu.HBM) for a in operands[:left]]
    return pl.pallas_call(
        kernel,
        out_shape=outs,
        in_specs=[pl.BlockSpec(memory_space=pltpu.SMEM)]
        + [pl.BlockSpec(memory_space=pltpu.HBM)] * left
        + [pl.BlockSpec(memory_space=pltpu.VMEM)] * (len(operands) - left),
        out_specs=[pl.BlockSpec(memory_space=pltpu.VMEM)] * len(outs),
        scratch_shapes=scratch,
        cost_estimate=pl.CostEstimate(flops=0, bytes_accessed=0, transcendentals=0),
        compiler_params=pltpu.CompilerParams(vmem_limit_bytes=vmem << 20),
    )(length, *fixed, *operands[left:])


def aligned(value, to):
    return pl.multiple_of(value, to)


def dot(a, b):
    return jnp.dot(a, b, preferred_element_type=F32)


def here():
    return tuple(lax.axis_index(a) for a in ("seq", "head", "fsdp", "parts"))


def deal_kernel(length, *refs):
    sources, later, other = refs[:4], refs[4:7], refs[7:10]
    outs, later_out, held, sems, later_sems = refs[10:14], *refs[14:]
    s, _, f, p = here()
    half = outs[0].shape[1]
    copies = [pltpu.make_async_copy(w, held.at[i], sems.at[i]) for i, w in enumerate(sources)]
    at = pl.ds(aligned(p * half, half), half)
    later_copies = [
        pltpu.make_async_copy(w.at[at], later_out.at[i], later_sems.at[i]) for i, w in enumerate(later)
    ]
    for copy in copies + later_copies:
        copy.start()
    mine, w_out = [held.at[m] for m in range(3)], held.at[3]
    for copy in copies:
        copy.wait()
    rows = pl.ds(aligned(f * half, half), half)
    for k in range(SEQ):
        head = s ^ k
        columns = pl.ds(aligned((head % 2) * HD, HD), HD)

        @pl.when(head // 2 == f)
        def _():
            for m in range(3):
                outs[k][m] = mine[m][rows, columns]

        @pl.when(head // 2 != f)
        def _():
            for m in range(3):
                outs[k][m] = other[m][rows, columns]

        for m in range(outs[k].shape[0] - 3):
            outs[k][3 + m] = w_out[at, m * HD : (m + 1) * HD]
    for copy in later_copies:
        copy.wait()


def join_kernel(length, *refs):
    for k, ref in enumerate(refs[:-1]):
        refs[-1][k] = ref[...]


def stack_kernel(length, *refs):
    s = lax.axis_index("seq")
    for k in range(SEQ):
        refs[SEQ][s ^ k] = refs[k][...]


def project_kernel(length, *refs):
    frames, gain, own_far, *near = refs[: SEQ + 2]
    far, mine, other = refs[SEQ + 2], refs[SEQ + 3 : 2 * SEQ + 3], refs[2 * SEQ + 3 : 3 * SEQ + 3]
    q_out, send_out, edge_out, stack_out, normed, weights, x_edge, q_edge, own_x, own_gain, sems = refs[3 * SEQ + 3 :]
    copies = [
        pltpu.make_async_copy(frames, own_x, sems.at[0]),
        pltpu.make_async_copy(gain, own_gain, sems.at[1]),
    ]
    for copy in copies:
        copy.start()
    s, h, f, _ = here()
    blocks = [own_x, own_far]
    for k in range(1, SEQ):
        blocks += [near[k - 1], far.at[k - 1]]
    rows = blocks[0].shape[0]
    half = mine[0].shape[1]
    for copy in copies:
        copy.wait()
    gain_row = own_gain[...]
    for slot, block in enumerate(blocks):
        at = (s ^ (slot // 2)) * 2 + (h ^ (slot % 2))
        x = block[...].astype(F32)
        normed[pl.ds(aligned(at * rows, rows), rows), :] = layer_norm(x, gain_row).astype(BF16)
        x_edge[at, 0:EDGE, :] = x[:EDGE]
        x_edge[at, EDGE:HALO, :] = x[rows - EDGE :]
    for k in range(SEQ):
        for core, pieces in enumerate((mine, other)):
            at = pl.ds(aligned((s ^ k) * 2 * half + (f ^ core) * half, half), half)
            for m in range(3):
                weights[at, m * HD : (m + 1) * HD] = pieces[k][m]
        stack_out[s ^ k] = mine[k][3:]
    count = 2 * SEQ
    total = count * rows
    projected = dot(normed[...], weights[...])
    q_out[...] = projected[:, :HD].astype(BF16)
    send_out[0:total, :] = projected[:, HD : 2 * HD].astype(BF16)
    send_out[total : 2 * total, :] = projected[:, 2 * HD :].astype(BF16)
    for b in range(count):
        q_edge[b, 0:EDGE, :] = projected[b * rows : b * rows + EDGE, :HD]
        q_edge[b, EDGE:HALO, :] = projected[(b + 1) * rows - EDGE : (b + 1) * rows, :HD]

    def around(edge, b):
        low = jnp.maximum(b - f, 0)
        high = jnp.minimum(b + 1 - f, count - 1)
        return jnp.concatenate([edge[low, EDGE:HALO, :], edge[high, 0:EDGE, :]], axis=0)

    halos = jnp.concatenate([around(q_edge, b) for b in range(count)], axis=0)
    send_out[2 * total :, :] = halos.astype(BF16)
    edge_out[...] = jnp.concatenate([around(x_edge, s * 2 + b) for b in range(2)], axis=0).astype(BF16)


def attend_kernel(length, q_in, own, peer, *refs):
    ctx_outs, q_rows = refs[:SEQ], refs[SEQ]
    s, _, f, _ = here()
    valid_len = length[0]
    count = q_rows.shape[0]
    total = q_in.shape[0]
    rows = total // count
    step = q_rows.shape[1]
    local = lax.broadcasted_iota(jnp.int32, (step, total), 1)
    base = (local // rows) * (2 * rows) + local % rows
    keep_own = base + f * rows < valid_len
    keep_peer = base + (1 - f) * rows < valid_len
    scale = 1.0 / math.sqrt(HD)
    keys_t = (((1,), (1,)), ((), ()))
    for b in range(count):
        q_rows[b, 0:rows, :] = q_in[b * rows : (b + 1) * rows, :].astype(F32)
        q_rows[b, rows:step, :] = peer[2 * total + b * HALO : 2 * total + (b + 1) * HALO, :].astype(F32)
    for b in range(count):
        k, side = b // 2, b % 2
        q = q_rows[(s ^ k) * 2 + side].astype(BF16)
        first = lax.dot_general(q, own[0:total, :], keys_t, preferred_element_type=F32) * scale
        second = lax.dot_general(q, peer[0:total, :], keys_t, preferred_element_type=F32) * scale
        first = jnp.where(keep_own, first, -jnp.inf)
        second = jnp.where(keep_peer, second, -jnp.inf)
        peak = jnp.maximum(
            jnp.max(first, axis=1, keepdims=True), jnp.max(second, axis=1, keepdims=True)
        )
        first = jnp.exp(first - peak)
        second = jnp.exp(second - peak)
        weight_sum = jnp.sum(first, axis=1, keepdims=True) + jnp.sum(second, axis=1, keepdims=True)
        weighted = dot(first.astype(BF16), own[total : 2 * total, :]) + dot(
            second.astype(BF16), peer[total : 2 * total, :]
        )
        ctx_outs[k][side * step : (side + 1) * step, :] = (weighted / weight_sum).astype(BF16)


def output_kernel(length, *refs):
    pieces, ctx = refs[:4], refs[4 : 4 + SEQ]
    share_out, send_out, context, weights = refs[4 + SEQ :]
    s, h, f, p = here()
    half = pieces[0].shape[2]
    columns = weights.shape[2]
    for y in range(2):
        for core in range(2):
            rows = pl.ds(aligned((f ^ core) * 2 * half + (p ^ y) * half, half), half)
            for m in range(columns // HD):
                for j in range(SEQ):
                    weights[j, rows, m * HD : (m + 1) * HD] = pieces[y * 2 + core][j, m]
    for k in range(SEQ):
        context[:, pl.ds(aligned((s ^ k) * HD, HD), HD)] = ctx[k][...]
    for j in range(SEQ):
        at = slice(j * columns, (j + 1) * columns)
        share = dot(context[...], weights[j])
        share_out[:, at] = share
        send_out[:, at] = share.astype(BF16)


def convolve_kernel(length, *refs):
    pieces = refs[:4]
    own_x, peer_x, halo_x, own_share, peer_share, gain, own_c, peer_c, base_out, share_out = refs[4:14]
    mid, normed, w_value, w_gate, w_down, channel, padded, active, shares = refs[14:]
    s, h, f, p = here()
    valid_len = length[0]
    half, columns = pieces[0].shape[2:]
    rows = own_x.shape[0]
    step = rows + HALO
    for y in range(2):
        for core in range(2):
            stack = pieces[y * 2 + core]
            down = pl.ds(aligned((f ^ core) * 2 * half + (p ^ y) * half, half), half)
            for plane in range(SEQ):
                at = pl.ds(aligned(plane * 2 * half + (p ^ y) * half, half), half)
                w_value[f ^ core, at, :] = stack[plane, 0]
                w_gate[f ^ core, at, :] = stack[plane, 1]
                w_down[plane, down, :] = stack[plane, 2]
    channel[f] = own_c[...]
    channel[1 - f] = peer_c[...]
    mid[pl.ds(aligned(h * step, 8), rows), :] = own_x[...].astype(F32)
    mid[pl.ds(aligned((1 - h) * step, 8), rows), :] = peer_x[...].astype(F32)
    for b in range(2):
        mid[b * step + rows : (b + 1) * step, :] = halo_x[b * HALO : (b + 1) * HALO, :].astype(F32)
    middle = mid[...] + (own_share[...] + peer_share[...].astype(F32))
    mid[...] = middle
    normed[...] = layer_norm(middle, gain[...]).astype(BF16)
    place = lax.broadcasted_iota(jnp.int32, (step, columns), 0)
    offset = jnp.where(place < rows, place, jnp.where(place < rows + EDGE, place - rows - EDGE, place - EDGE))
    for c in range(2):
        x = normed[...]
        value_part = dot(x, w_value[c])
        gate_part = dot(x, w_gate[c])
        gated = value_part * jax.nn.sigmoid(gate_part)
        for b in range(2):
            t = offset + (4 * s + 2 * b + f) * rows
            kept = jnp.where((t >= 0) & (t < valid_len), gated[b * step : (b + 1) * step], 0.0)
            kept = kept.astype(BF16).astype(F32)
            padded[b, 8 : 8 + rows, :] = kept[:rows]
            padded[b, 8 - EDGE : 8, :] = kept[rows : rows + EDGE]
            padded[b, 8 + rows : 8 + rows + EDGE, :] = kept[rows + EDGE :]
            depth_sum = channel[c, 0:1, :] * padded[b, 8 - EDGE : 8 - EDGE + rows, :]
            for j in range(1, KERNEL):
                low = 8 - EDGE + j
                depth_sum = depth_sum + channel[c, j : j + 1, :] * padded[b, low : low + rows, :]
            shifted = depth_sum * channel[c, KERNEL : KERNEL + 1, :] + channel[c, KERNEL + 1 : KERNEL + 2, :]
            active[b * rows : (b + 1) * rows, c * columns : (c + 1) * columns] = (
                shifted * jax.nn.sigmoid(shifted)
            ).astype(BF16)
    for j in range(SEQ):
        shares[:, j * columns : (j + 1) * columns] = dot(active[...], w_down[j])
    base_out[...] = mid[pl.ds(aligned(h * step, 8), rows), :] + shares[pl.ds(aligned(h * rows, rows), rows), :]
    share_out[...] = shares[pl.ds(aligned((1 - h) * rows, rows), rows), :].astype(BF16)


def shards_chip_per_head(
    frames,
    length,
    ln1_gain,
    w_query,
    w_key,
    w_value,
    w_out,
    ln2_gain,
    pw1_value,
    pw1_gate,
    depth_kernel,
    bn_scale,
    bn_shift,
    pw2,
):
    rows, width = frames.shape
    count = 2 * SEQ
    step = rows + HALO
    f, p = lax.axis_index("fsdp"), lax.axis_index("parts")
    half = w_query.shape[0] // 2
    columns = w_query.shape[1]
    barrier = lax.optimization_barrier

    def other_core(x):
        return lax.ppermute(x, "fsdp", SWAP)

    def other_side(x):
        return lax.ppermute(x, "head", SWAP)

    def other_part(x):
        return lax.ppermute(x, "parts", SWAP)

    def across(x, k):
        return lax.ppermute(x, "seq", xor_pairs(k))

    def planes(x):
        far = across(x, 3)
        return [x, across(x, 1), across(far, 1), far]

    def part_half(x):
        return lax.dynamic_slice_in_dim(x, p * half, half, axis=x.ndim - 2)

    near = planes(frames)
    given = [w_query, w_key, w_value]
    shape = jax.ShapeDtypeStruct
    *dealt, pw_mine = call(
        deal_kernel,
        [shape((3 + columns // HD, half, HD), BF16)] * SEQ
        + [shape((3, half, columns), BF16)],
        [
            pltpu.VMEM((4, 2 * half, columns), BF16),
            pltpu.SemaphoreType.DMA((4,)),
            pltpu.SemaphoreType.DMA((3,)),
        ],
        length,
        *given,
        w_out,
        pw1_value,
        pw1_gate,
        pw2,
        *[other_core(w) for w in given],
        left=7,
    )
    *dealt, _ = barrier((*dealt, near[1]))
    w_mine = [dealt[0]] + [across(dealt[k], k) for k in range(1, SEQ)]
    own_far = other_side(frames)
    *near[1:], own_far, _ = barrier((*near[1:], own_far, w_mine[1]))
    (joined,) = call(join_kernel, [shape((SEQ - 1, rows, width), BF16)], [], length, *near[1:])
    far = other_side(joined)
    w_other = [other_core(w[:3]) for w in w_mine]
    after, *_ = barrier((pw_mine, joined, w_mine[2], w_mine[3]))
    pw_part, pw_one, pw_three = other_part(after), across(after, 1), across(after, 3)
    w_other[0], pw_part, pw_one = barrier((w_other[0], pw_part, pw_one))
    pw_two, one_part, three_part = across(pw_three, 1), other_part(pw_one), other_part(pw_three)
    queries, send, edges, stack = call(
        project_kernel,
        [
            shape((count * rows, HD), BF16),
            shape((2 * count * rows + count * HALO, HD), BF16),
            shape((2 * HALO, width), BF16),
            shape((SEQ, columns // HD, half, HD), BF16),
        ],
        [
            pltpu.VMEM((count * rows, width), BF16),
            pltpu.VMEM((width, 3 * HD), BF16),
            pltpu.VMEM((count, HALO, width), F32),
            pltpu.VMEM((count, HALO, HD), F32),
            pltpu.VMEM((rows, width), BF16),
            pltpu.VMEM((1, width), F32),
            pltpu.SemaphoreType.DMA((2,)),
        ],
        length,
        frames,
        ln1_gain[None],
        own_far,
        *near[1:],
        far,
        *w_mine,
        *w_other,
        left=2,
    )
    received = other_core(send)
    queries, pw_three = barrier((queries, pw_three))
    stack_part = other_part(stack)
    ctx = call(
        attend_kernel,
        [shape((2 * step, HD), BF16)] * SEQ,
        [pltpu.VMEM((count, step, HD), F32)],
        length,
        queries,
        send,
        received,
    )
    ctx = [ctx[0]] + [lax.ppermute(ctx[k], "seq", xor_pairs(k)) for k in range(1, SEQ)]
    pw_two, one_part, stack, stack_part, *ctx[2:] = barrier((pw_two, one_part, stack, stack_part, *ctx[2:]))
    out_pieces = [stack, other_core(stack), stack_part, other_core(stack_part)]
    own_share, sent_share = call(
        output_kernel,
        [shape((2 * step, width), F32), shape((2 * step, width), BF16)],
        [
            pltpu.VMEM((2 * step, SEQ * HD), BF16),
            pltpu.VMEM((SEQ, 2 * columns, columns), BF16),
        ],
        length,
        *out_pieces,
        *ctx,
    )
    own_share, edges, depth_kernel = barrier((own_share, edges, depth_kernel))
    halo_x = other_core(edges)
    channels = jnp.concatenate([depth_kernel, bn_scale[None], bn_shift[None], jnp.zeros((5, columns), F32)])
    channels_peer = other_core(channels)
    peer_share = other_side(sent_share)

    def stacked(*pieces):
        (stack,) = call(stack_kernel, [shape((SEQ, *pieces[0].shape), BF16)], [], length, *pieces)
        return [stack, other_core(stack)]

    two_part = other_part(pw_two)
    pw_mine, _ = barrier((pw_mine, peer_share))
    pw_pieces = stacked(pw_mine, pw_one, pw_two, pw_three) + stacked(pw_part, one_part, two_part, three_part)
    base, share = call(
        convolve_kernel,
        [shape((rows, width), F32), shape((rows, width), BF16)],
        [
            pltpu.VMEM((2 * step, width), F32),
            pltpu.VMEM((2 * step, width), BF16),
            pltpu.VMEM((2, width, columns), BF16),
            pltpu.VMEM((2, width, columns), BF16),
            pltpu.VMEM((SEQ, 2 * columns, columns), BF16),
            pltpu.VMEM((2, 16, columns), F32),
            pltpu.VMEM((2, 16 + rows, columns), F32),
            pltpu.VMEM((2 * rows, 2 * columns), BF16),
            pltpu.VMEM((2 * rows, width), F32),
        ],
        length,
        *pw_pieces,
        frames,
        own_far,
        halo_x,
        own_share,
        peer_share,
        ln2_gain[None],
        channels,
        channels_peer,
        vmem=14,
    )
    return (base + other_side(share).astype(F32)).astype(BF16)


def solution(mesh):
    in_specs = (
        P(("parts", "seq", "head", "fsdp"), None),
        P("parts"),
        P(),
        P("seq", ("head", "fsdp")),
        P("seq", ("head", "fsdp")),
        P("seq", ("head", "fsdp")),
        P(("head", "fsdp"), "seq"),
        P(),
        P("seq", ("head", "fsdp")),
        P("seq", ("head", "fsdp")),
        P(None, ("head", "fsdp")),
        P(("head", "fsdp")),
        P(("head", "fsdp")),
        P(("head", "fsdp"), "seq"),
    )
    out_specs = P(("parts", "seq", "head", "fsdp"), None)
    body = shards_chip_per_head if one_head_per_chip(mesh) else shards_general
    return jax.shard_map(body, mesh=mesh, in_specs=in_specs, out_specs=out_specs, check_vma=False)
```

```python
import math

import jax
import jax.numpy as jnp
from jax import lax
from jax.experimental import pallas as pl
from jax.experimental.pallas import tpu as pltpu
from jax.sharding import PartitionSpec as P

KERNEL = 9
HD = 128


def with_halo(block, sides, width):
    for axis, dim in sides:
        count = lax.axis_size(axis)
        forward = [(i, i + 1) for i in range(count - 1)]
        backward = [(target, source) for source, target in forward]
        low = lax.ppermute(
            lax.slice_in_dim(block, block.shape[dim] - width, None, axis=dim), axis, forward
        )
        high = lax.ppermute(lax.slice_in_dim(block, 0, width, axis=dim), axis, backward)
        block = jnp.concatenate([low, block, high], axis=dim)
    return block


def layer_norm(values_in, gain_vec):
    center = jnp.mean(values_in, axis=-1, keepdims=True)
    shifted = values_in - center
    spread = jnp.mean(shifted * shifted, axis=-1, keepdims=True)
    return shifted * lax.rsqrt(spread + 1e-05) * gain_vec


def shards_general(
    frames,
    length,
    ln1_gain,
    w_query,
    w_key,
    w_value,
    w_out,
    ln2_gain,
    pw1_value,
    pw1_gate,
    depth_kernel,
    bn_scale,
    bn_shift,
    pw2,
):
    group_size = lax.axis_size(("head", "fsdp"))
    my_rows = frames.shape[0]
    block_rows = my_rows * group_size
    head_cols = w_query.shape[1]
    heads_here = head_cols // HD
    seq_start = lax.axis_index("seq") * block_rows
    valid_len = length[0]
    score_scale = 1.0 / math.sqrt(HD)
    full_query, full_key, full_value, value_cols, gate_cols = (
        lax.all_gather(w_query, "seq", axis=0, tiled=True),
        lax.all_gather(w_key, "seq", axis=0, tiled=True),
        lax.all_gather(w_value, "seq", axis=0, tiled=True),
        lax.all_gather(pw1_value, "seq", axis=0, tiled=True),
        lax.all_gather(pw1_gate, "seq", axis=0, tiled=True),
    )
    out_rows, down_rows = (
        lax.all_gather(w_out, "seq", axis=1, tiled=True),
        lax.all_gather(pw2, "seq", axis=1, tiled=True),
    )
    projector = jnp.concatenate((full_query, full_key, full_value), axis=1)
    source = frames.astype(jnp.float32)
    normed = layer_norm(source, ln1_gain).astype(jnp.bfloat16)
    projected = jnp.dot(
        lax.all_gather(normed, ("head", "fsdp"), axis=0, tiled=True),
        projector,
        preferred_element_type=jnp.float32,
    ).astype(jnp.bfloat16)
    queries = projected[:, :head_cols].reshape(block_rows, heads_here, HD)
    keys_here = projected[:, head_cols : 2 * head_cols]
    values_here = projected[:, 2 * head_cols :]
    initial = (
        jnp.full((heads_here, block_rows), -1e30, jnp.float32),
        jnp.zeros((heads_here, block_rows), jnp.float32),
        jnp.zeros((heads_here, block_rows, HD), jnp.float32),
    )
    key_piece = lax.all_gather(keys_here, "seq", axis=0, tiled=True)
    value_piece = lax.all_gather(values_here, "seq", axis=0, tiled=True)
    row_count = key_piece.shape[0]
    block_size = math.gcd(row_count, 512)
    block_count = row_count // block_size
    key_blocks = key_piece.reshape(block_count, block_size, heads_here, HD)
    value_blocks = value_piece.reshape(block_count, block_size, heads_here, HD)
    places = jnp.arange(row_count, dtype=jnp.int32).reshape(block_count, block_size)

    def advance(inner_state, block_item):
        key_block, value_block, place = block_item
        peak_score, weight_sum, weighted = inner_state
        scores = (
            jnp.einsum("qhd,khd->hqk", queries, key_block, preferred_element_type=jnp.float32)
            * score_scale
        )
        scores = jnp.where((place < valid_len)[None, None, :], scores, -jnp.inf)
        new_peak = jnp.maximum(peak_score, jnp.max(scores, axis=2))
        factor = jnp.exp(peak_score - new_peak)
        weights = jnp.exp(scores - new_peak[:, :, None])
        weight_sum = weight_sum * factor + jnp.sum(weights, axis=2)
        weighted = weighted * factor[:, :, None] + jnp.einsum(
            "hqk,khd->hqd",
            weights.astype(jnp.bfloat16),
            value_block,
            preferred_element_type=jnp.float32,
        )
        return ((new_peak, weight_sum, weighted), None)

    result, unused = lax.scan(advance, initial, (key_blocks, value_blocks, places))
    peak_score, weight_sum, weighted = result
    context = (
        (weighted / weight_sum[:, :, None])
        .astype(jnp.bfloat16)
        .transpose(1, 0, 2)
        .reshape(block_rows, head_cols)
    )
    attended = lax.psum_scatter(
        jnp.dot(context, out_rows, preferred_element_type=jnp.float32).astype(jnp.bfloat16),
        ("head", "fsdp"),
        scatter_dimension=0,
        tiled=True,
    ).astype(jnp.float32)
    middle = source + attended
    normed_two = layer_norm(middle, ln2_gain).astype(jnp.bfloat16)
    piece = lax.all_gather(normed_two, ("head", "fsdp"), axis=0, tiled=True)
    value_part = jnp.dot(piece, value_cols, preferred_element_type=jnp.float32)
    gate_part = jnp.dot(piece, gate_cols, preferred_element_type=jnp.float32)
    places = seq_start + jnp.arange(piece.shape[0], dtype=jnp.int32)
    gated_rows = jnp.where(
        (places < valid_len)[:, None], value_part * jax.nn.sigmoid(gate_part), 0.0
    ).astype(jnp.bfloat16)
    rim_width = (KERNEL - 1) // 2
    padded = with_halo(gated_rows, (("seq", 0),), rim_width).astype(jnp.float32)
    depth_sum = depth_kernel[0] * padded[0:block_rows]
    for offset in range(1, KERNEL):
        depth_sum = depth_sum + depth_kernel[offset] * padded[offset : offset + block_rows]
    shifted = depth_sum * bn_scale + bn_shift
    active = (shifted * jax.nn.sigmoid(shifted)).astype(jnp.bfloat16)
    conv_part = lax.psum_scatter(
        jnp.dot(active, down_rows, preferred_element_type=jnp.float32).astype(jnp.bfloat16),
        ("head", "fsdp"),
        scatter_dimension=0,
        tiled=True,
    ).astype(jnp.float32)
    return (middle + conv_part).astype(jnp.bfloat16)


SEQ = 4
EDGE = (KERNEL - 1) // 2
HALO = 2 * EDGE
SWAP = [(0, 1), (1, 0)]
F32 = jnp.float32
BF16 = jnp.bfloat16


def one_head_per_chip(mesh):
    return dict(mesh.shape) == {"parts": 2, "seq": SEQ, "head": 2, "fsdp": 2}


def xor_pairs(k):
    return [(i, i ^ k) for i in range(SEQ)]


def call(kernel, outs, scratch, length, *operands, vmem=8, left=0, flops=0):
    fixed = [pltpu.with_memory_space_constraint(a, pltpu.HBM) for a in operands[:left]]
    return pl.pallas_call(
        kernel,
        out_shape=outs,
        in_specs=[pl.BlockSpec(memory_space=pltpu.SMEM)]
        + [pl.BlockSpec(memory_space=pltpu.HBM)] * left
        + [pl.BlockSpec(memory_space=pltpu.VMEM)] * (len(operands) - left),
        out_specs=[pl.BlockSpec(memory_space=pltpu.VMEM)] * len(outs),
        scratch_shapes=scratch,
        cost_estimate=pl.CostEstimate(flops=flops, bytes_accessed=0, transcendentals=0),
        compiler_params=pltpu.CompilerParams(vmem_limit_bytes=vmem << 20),
    )(length, *fixed, *operands[left:])


def aligned(value, to):
    return pl.multiple_of(value, to)


def dot(a, b):
    return jnp.dot(a, b, preferred_element_type=F32)


def here():
    return tuple(lax.axis_index(a) for a in ("seq", "head", "fsdp", "parts"))


def deal_kernel(length, *refs):
    sources, later, other = refs[:3], refs[3:6], refs[6:9]
    outs, whole, part, held, sems, later_sems = refs[9:13], *refs[13:]
    s, _, f, p = here()
    half = outs[0].shape[1]
    copies = [pltpu.make_async_copy(w, held.at[i], sems.at[i]) for i, w in enumerate(sources)]
    at = pl.ds(aligned(p * half, half), half)
    later_copies = [pltpu.make_async_copy(w, whole.at[i], later_sems.at[0, i]) for i, w in enumerate(later)]
    later_copies += [pltpu.make_async_copy(w.at[at], part.at[i], later_sems.at[1, i]) for i, w in enumerate(later)]
    for copy in copies + later_copies:
        copy.start()
    for copy in copies:
        copy.wait()
    rows = pl.ds(aligned(f * half, half), half)
    for k in range(SEQ):
        head = s ^ k
        columns = pl.ds(aligned((head % 2) * HD, HD), HD)

        @pl.when(head // 2 == f)
        def _():
            for m in range(3):
                outs[k][m] = held[m, rows, columns]

        @pl.when(head // 2 != f)
        def _():
            for m in range(3):
                outs[k][m] = other[m][rows, columns]

    for copy in later_copies:
        copy.wait()


def join_kernel(length, *refs):
    for k, ref in enumerate(refs[:-1]):
        refs[-1][k] = ref[...]


def project_kernel(length, *refs):
    frames, gain, own_far, *near = refs[: SEQ + 2]
    far, mine, other = refs[SEQ + 2], refs[SEQ + 3 : 2 * SEQ + 3], refs[2 * SEQ + 3 : 3 * SEQ + 3]
    q_out, send_out, edge_out, normed, weights, x_edge, q_edge, own_x, own_gain, sems = refs[3 * SEQ + 3 :]
    copies = [
        pltpu.make_async_copy(frames, own_x, sems.at[0]),
        pltpu.make_async_copy(gain, own_gain, sems.at[1]),
    ]
    for copy in copies:
        copy.start()
    s, h, f, _ = here()
    blocks = [own_x, own_far]
    for k in range(1, SEQ):
        blocks += [near[k - 1], far.at[k - 1]]
    rows = blocks[0].shape[0]
    half = mine[0].shape[1]
    for copy in copies:
        copy.wait()
    gain_row = own_gain[...]
    for slot, block in enumerate(blocks):
        at = (s ^ (slot // 2)) * 2 + (h ^ (slot % 2))
        x = block[...].astype(F32)
        normed[pl.ds(aligned(at * rows, rows), rows), :] = layer_norm(x, gain_row).astype(BF16)
        x_edge[at, 0:EDGE, :] = x[:EDGE]
        x_edge[at, EDGE:HALO, :] = x[rows - EDGE :]
    for k in range(SEQ):
        for core, pieces in enumerate((mine, other)):
            at = pl.ds(aligned((s ^ k) * 2 * half + (f ^ core) * half, half), half)
            for m in range(3):
                weights[at, m * HD : (m + 1) * HD] = pieces[k][m]
    count = 2 * SEQ
    total = count * rows
    projected = dot(normed[...], weights[...])
    q_out[...] = projected[:, :HD].astype(BF16)
    send_out[0:total, :] = projected[:, HD : 2 * HD].astype(BF16)
    send_out[total : 2 * total, :] = projected[:, 2 * HD :].astype(BF16)
    for b in range(count):
        q_edge[b, 0:EDGE, :] = projected[b * rows : b * rows + EDGE, :HD]
        q_edge[b, EDGE:HALO, :] = projected[(b + 1) * rows - EDGE : (b + 1) * rows, :HD]

    def around(edge, b):
        low = jnp.maximum(b - f, 0)
        high = jnp.minimum(b + 1 - f, count - 1)
        return jnp.concatenate([edge[low, EDGE:HALO, :], edge[high, 0:EDGE, :]], axis=0)

    halos = jnp.concatenate([around(q_edge, b) for b in range(count)], axis=0)
    send_out[2 * total :, :] = halos.astype(BF16)
    edge_out[...] = jnp.concatenate([around(x_edge, s * 2 + b) for b in range(2)], axis=0).astype(BF16)


def attend_kernel(length, q_in, own, peer, *refs):
    ctx_outs, q_rows = refs[:SEQ], refs[SEQ]
    s, _, f, _ = here()
    valid_len = length[0]
    count = q_rows.shape[0]
    total = q_in.shape[0]
    rows = total // count
    step = q_rows.shape[1]
    local = lax.broadcasted_iota(jnp.int32, (step, total), 1)
    base = (local // rows) * (2 * rows) + local % rows
    keep_own = base + f * rows < valid_len
    keep_peer = base + (1 - f) * rows < valid_len
    scale = 1.0 / math.sqrt(HD)
    keys_t = (((1,), (1,)), ((), ()))
    for b in range(count):
        q_rows[b, 0:rows, :] = q_in[b * rows : (b + 1) * rows, :].astype(F32)
        q_rows[b, rows:step, :] = peer[2 * total + b * HALO : 2 * total + (b + 1) * HALO, :].astype(F32)
    for b in range(count):
        k, side = b // 2, b % 2
        q = q_rows[(s ^ k) * 2 + side].astype(BF16)
        first = lax.dot_general(q, own[0:total, :], keys_t, preferred_element_type=F32) * scale
        second = lax.dot_general(q, peer[0:total, :], keys_t, preferred_element_type=F32) * scale
        first = jnp.where(keep_own, first, -jnp.inf)
        second = jnp.where(keep_peer, second, -jnp.inf)
        peak = jnp.maximum(
            jnp.max(first, axis=1, keepdims=True), jnp.max(second, axis=1, keepdims=True)
        )
        first = jnp.exp(first - peak)
        second = jnp.exp(second - peak)
        weight_sum = jnp.sum(first, axis=1, keepdims=True) + jnp.sum(second, axis=1, keepdims=True)
        weighted = dot(first.astype(BF16), own[total : 2 * total, :]) + dot(
            second.astype(BF16), peer[total : 2 * total, :]
        )
        ctx_outs[k][side * step : (side + 1) * step, :] = (weighted / weight_sum).astype(BF16)


def output_kernel(length, *refs):
    pieces, ctx = refs[:2], refs[2 : 2 + SEQ]
    share_out, send_out, context, weights = refs[2 + SEQ :]
    s, h, f, p = here()
    columns = weights.shape[2]
    depth = columns
    for core in range(2):
        rows = pl.ds(aligned((f ^ core) * depth, depth), depth)
        for k in range(SEQ):
            weights[s ^ k, rows, :] = pieces[core][k]
    for k in range(SEQ):
        context[:, pl.ds(aligned((s ^ k) * HD, HD), HD)] = ctx[k][...]
    for j in range(SEQ):
        at = slice(j * columns, (j + 1) * columns)
        share = dot(context[...], weights[j])
        share_out[:, at] = share
        send_out[:, at] = share.astype(BF16)


def convolve_kernel(length, *refs):
    near, far = refs[:4], refs[4:6]
    own_x, peer_x, halo_x, own_share, peer_share, gain, own_c, peer_c, base_out, share_out = refs[6:16]
    mid, normed, w_value, w_gate, w_down, channel, padded, active, shares = refs[16:]
    s, h, f, p = here()
    valid_len = length[0]
    half, columns = far[0].shape[2:]
    rows = own_x.shape[0]
    step = rows + HALO

    def put(core, plane, first, count, block):
        at = pl.ds(aligned(plane * 2 * half + first, half), count)
        w_value[f ^ core, at, :] = block[0]
        w_gate[f ^ core, at, :] = block[1]
        w_down[plane, pl.ds(aligned((f ^ core) * 2 * half + first, half), count), :] = block[2]

    for core in range(2):
        for k in range(2):
            put(core, s ^ k, 0, 2 * half, near[2 * k + core])
        for y in range(2):
            for i, k in enumerate((3, 2)):
                put(core, s ^ k, (p ^ y) * half, half, far[core].at[2 * y + i])
    channel[f] = own_c[...]
    channel[1 - f] = peer_c[...]
    mid[pl.ds(aligned(h * step, 8), rows), :] = own_x[...].astype(F32)
    mid[pl.ds(aligned((1 - h) * step, 8), rows), :] = peer_x[...].astype(F32)
    for b in range(2):
        mid[b * step + rows : (b + 1) * step, :] = halo_x[b * HALO : (b + 1) * HALO, :].astype(F32)
    middle = mid[...] + (own_share[...] + peer_share[...].astype(F32))
    mid[...] = middle
    normed[...] = layer_norm(middle, gain[...]).astype(BF16)
    place = lax.broadcasted_iota(jnp.int32, (step, columns), 0)
    offset = jnp.where(place < rows, place, jnp.where(place < rows + EDGE, place - rows - EDGE, place - EDGE))
    for c in range(2):
        x = normed[...]
        value_part = dot(x, w_value[c])
        gate_part = dot(x, w_gate[c])
        gated = value_part * jax.nn.sigmoid(gate_part)
        for b in range(2):
            t = offset + (4 * s + 2 * b + f) * rows
            kept = jnp.where((t >= 0) & (t < valid_len), gated[b * step : (b + 1) * step], 0.0)
            kept = kept.astype(BF16).astype(F32)
            padded[b, 8 : 8 + rows, :] = kept[:rows]
            padded[b, 8 - EDGE : 8, :] = kept[rows : rows + EDGE]
            padded[b, 8 + rows : 8 + rows + EDGE, :] = kept[rows + EDGE :]
            depth_sum = channel[c, 0:1, :] * padded[b, 8 - EDGE : 8 - EDGE + rows, :]
            for j in range(1, KERNEL):
                low = 8 - EDGE + j
                depth_sum = depth_sum + channel[c, j : j + 1, :] * padded[b, low : low + rows, :]
            shifted = depth_sum * channel[c, KERNEL : KERNEL + 1, :] + channel[c, KERNEL + 1 : KERNEL + 2, :]
            active[b * rows : (b + 1) * rows, c * columns : (c + 1) * columns] = (
                shifted * jax.nn.sigmoid(shifted)
            ).astype(BF16)
    for j in range(SEQ):
        shares[:, j * columns : (j + 1) * columns] = dot(active[...], w_down[j])
    base_out[...] = mid[pl.ds(aligned(h * step, 8), rows), :] + shares[pl.ds(aligned(h * rows, rows), rows), :]
    share_out[...] = shares[pl.ds(aligned((1 - h) * rows, rows), rows), :].astype(BF16)


def shards_chip_per_head(
    frames,
    length,
    ln1_gain,
    w_query,
    w_key,
    w_value,
    w_out,
    ln2_gain,
    pw1_value,
    pw1_gate,
    depth_kernel,
    bn_scale,
    bn_shift,
    pw2,
):
    rows, width = frames.shape
    count = 2 * SEQ
    step = rows + HALO
    f, p = lax.axis_index("fsdp"), lax.axis_index("parts")
    half = w_query.shape[0] // 2
    columns = w_query.shape[1]
    barrier = lax.optimization_barrier

    def other_core(x):
        return lax.ppermute(x, "fsdp", SWAP)

    def other_side(x):
        return lax.ppermute(x, "head", SWAP)

    def other_part(x):
        return lax.ppermute(x, "parts", SWAP)

    def across(x, k):
        return lax.ppermute(x, "seq", xor_pairs(k))

    def planes(x):
        return [x] + [across(x, k) for k in range(1, SEQ)]

    near = planes(frames)
    own_far = other_side(frames)
    given = [w_query, w_key, w_value]
    shape = jax.ShapeDtypeStruct
    *dealt, pw_whole, pw_half = call(
        deal_kernel,
        [shape((3, half, HD), BF16)] * SEQ
        + [shape((3, 2 * half, columns), BF16), shape((3, half, columns), BF16)],
        [
            pltpu.VMEM((3, 2 * half, columns), BF16),
            pltpu.SemaphoreType.DMA((3,)),
            pltpu.SemaphoreType.DMA((2, 3)),
        ],
        length,
        *given,
        pw1_value,
        pw1_gate,
        pw2,
        *[other_core(w) for w in given],
        left=6,
    )
    *dealt, _ = barrier((*dealt, near[1]))
    w_mine = [dealt[0]] + [across(dealt[k], k) for k in range(1, SEQ)]
    *near[1:], own_far, _ = barrier((*near[1:], own_far, w_mine[3]))

    def joined(*pieces, flops=0):
        (stack,) = call(join_kernel, [shape((len(pieces), *pieces[0].shape), BF16)], [], length, *pieces, flops=flops)
        return stack

    far = other_side(joined(*near[1:]))
    w_other = [other_core(w) for w in w_mine]
    out_whole, *_ = barrier((w_out, *w_mine[1:]))
    out_one, out_three = across(out_whole, 1), across(out_whole, 3)
    out_two = across(out_three, 1)
    queries, send, edges = call(
        project_kernel,
        [
            shape((count * rows, HD), BF16),
            shape((2 * count * rows + count * HALO, HD), BF16),
            shape((2 * HALO, width), BF16),
        ],
        [
            pltpu.VMEM((count * rows, width), BF16),
            pltpu.VMEM((width, 3 * HD), BF16),
            pltpu.VMEM((count, HALO, width), F32),
            pltpu.VMEM((count, HALO, HD), F32),
            pltpu.VMEM((rows, width), BF16),
            pltpu.VMEM((1, width), F32),
            pltpu.SemaphoreType.DMA((2,)),
        ],
        length,
        frames,
        ln1_gain[None],
        own_far,
        *near[1:],
        far,
        *w_mine,
        *w_other,
        left=2,
    )
    received = other_core(send)
    later_whole, later_half, *_ = barrier((pw_whole, pw_half, send, out_one, out_three))
    pw_one, pw_three = across(later_whole, 1), across(later_half, 3)
    ctx = call(
        attend_kernel,
        [shape((2 * step, HD), BF16)] * SEQ,
        [pltpu.VMEM((count, step, HD), F32)],
        length,
        queries,
        send,
        received,
    )
    out_two, *ctx = barrier((out_two, *ctx))
    stack = joined(w_out, out_one, out_two, out_three)
    stack, *ctx = barrier((stack, *ctx))
    out_pieces = [stack, other_core(stack)]
    ctx = [ctx[0]] + [lax.ppermute(ctx[k], "seq", xor_pairs(k)) for k in range(1, SEQ)]
    pw_one, pw_three, *ctx[1:] = barrier((pw_one, pw_three, *ctx[1:]))
    pw_two, three_part = across(pw_three, 1), other_part(pw_three)
    own_share, sent_share = call(
        output_kernel,
        [shape((2 * step, width), F32), shape((2 * step, width), BF16)],
        [
            pltpu.VMEM((2 * step, SEQ * HD), BF16),
            pltpu.VMEM((SEQ, 2 * columns, columns), BF16),
        ],
        length,
        *out_pieces,
        *ctx,
    )
    late = (own_share, edges, depth_kernel, pw_whole, pw_one, pw_two)
    own_share, edges, depth_kernel, pw_whole, pw_one, pw_two = barrier(late)
    halo_x = other_core(edges)
    channels = jnp.concatenate([depth_kernel, bn_scale[None], bn_shift[None], jnp.zeros((5, columns), F32)])
    channels_peer = other_core(channels)
    peer_share = other_side(sent_share)
    far_pieces = joined(pw_three, pw_two, three_part, other_part(pw_two), flops=10**10)
    pw_pieces = [pw_whole, other_core(pw_whole), pw_one, other_core(pw_one), far_pieces, other_core(far_pieces)]
    base, share = call(
        convolve_kernel,
        [shape((rows, width), F32), shape((rows, width), BF16)],
        [
            pltpu.VMEM((2 * step, width), F32),
            pltpu.VMEM((2 * step, width), BF16),
            pltpu.VMEM((2, width, columns), BF16),
            pltpu.VMEM((2, width, columns), BF16),
            pltpu.VMEM((SEQ, 2 * columns, columns), BF16),
            pltpu.VMEM((2, 16, columns), F32),
            pltpu.VMEM((2, 16 + rows, columns), F32),
            pltpu.VMEM((2 * rows, 2 * columns), BF16),
            pltpu.VMEM((2 * rows, width), F32),
        ],
        length,
        *pw_pieces,
        frames,
        own_far,
        halo_x,
        own_share,
        peer_share,
        ln2_gain[None],
        channels,
        channels_peer,
        vmem=14,
    )
    return (base + other_side(share).astype(F32)).astype(BF16)


def solution(mesh):
    in_specs = (
        P(("parts", "seq", "head", "fsdp"), None),
        P("parts"),
        P(),
        P("seq", ("head", "fsdp")),
        P("seq", ("head", "fsdp")),
        P("seq", ("head", "fsdp")),
        P(("head", "fsdp"), "seq"),
        P(),
        P("seq", ("head", "fsdp")),
        P("seq", ("head", "fsdp")),
        P(None, ("head", "fsdp")),
        P(("head", "fsdp")),
        P(("head", "fsdp")),
        P(("head", "fsdp"), "seq"),
    )
    out_specs = P(("parts", "seq", "head", "fsdp"), None)
    body = shards_chip_per_head if one_head_per_chip(mesh) else shards_general
    return jax.shard_map(body, mesh=mesh, in_specs=in_specs, out_specs=out_specs, check_vma=False)
```

```python
import math

import jax
import jax.numpy as jnp
from jax import lax
from jax.experimental import pallas as pl
from jax.experimental.pallas import tpu as pltpu
from jax.sharding import PartitionSpec as P

KERNEL = 9
HD = 128


def with_halo(block, sides, width):
    for axis, dim in sides:
        count = lax.axis_size(axis)
        forward = [(i, i + 1) for i in range(count - 1)]
        backward = [(target, source) for source, target in forward]
        low = lax.ppermute(
            lax.slice_in_dim(block, block.shape[dim] - width, None, axis=dim), axis, forward
        )
        high = lax.ppermute(lax.slice_in_dim(block, 0, width, axis=dim), axis, backward)
        block = jnp.concatenate([low, block, high], axis=dim)
    return block


def layer_norm(values_in, gain_vec):
    center = jnp.mean(values_in, axis=-1, keepdims=True)
    shifted = values_in - center
    spread = jnp.mean(shifted * shifted, axis=-1, keepdims=True)
    return shifted * lax.rsqrt(spread + 1e-05) * gain_vec


def shards_general(
    frames,
    length,
    ln1_gain,
    w_query,
    w_key,
    w_value,
    w_out,
    ln2_gain,
    pw1_value,
    pw1_gate,
    depth_kernel,
    bn_scale,
    bn_shift,
    pw2,
):
    group_size = lax.axis_size(("head", "fsdp"))
    my_rows = frames.shape[0]
    block_rows = my_rows * group_size
    head_cols = w_query.shape[1]
    heads_here = head_cols // HD
    seq_start = lax.axis_index("seq") * block_rows
    valid_len = length[0]
    score_scale = 1.0 / math.sqrt(HD)
    full_query, full_key, full_value, value_cols, gate_cols = (
        lax.all_gather(w_query, "seq", axis=0, tiled=True),
        lax.all_gather(w_key, "seq", axis=0, tiled=True),
        lax.all_gather(w_value, "seq", axis=0, tiled=True),
        lax.all_gather(pw1_value, "seq", axis=0, tiled=True),
        lax.all_gather(pw1_gate, "seq", axis=0, tiled=True),
    )
    out_rows, down_rows = (
        lax.all_gather(w_out, "seq", axis=1, tiled=True),
        lax.all_gather(pw2, "seq", axis=1, tiled=True),
    )
    projector = jnp.concatenate((full_query, full_key, full_value), axis=1)
    source = frames.astype(jnp.float32)
    normed = layer_norm(source, ln1_gain).astype(jnp.bfloat16)
    projected = jnp.dot(
        lax.all_gather(normed, ("head", "fsdp"), axis=0, tiled=True),
        projector,
        preferred_element_type=jnp.float32,
    ).astype(jnp.bfloat16)
    queries = projected[:, :head_cols].reshape(block_rows, heads_here, HD)
    keys_here = projected[:, head_cols : 2 * head_cols]
    values_here = projected[:, 2 * head_cols :]
    initial = (
        jnp.full((heads_here, block_rows), -1e30, jnp.float32),
        jnp.zeros((heads_here, block_rows), jnp.float32),
        jnp.zeros((heads_here, block_rows, HD), jnp.float32),
    )
    key_piece = lax.all_gather(keys_here, "seq", axis=0, tiled=True)
    value_piece = lax.all_gather(values_here, "seq", axis=0, tiled=True)
    row_count = key_piece.shape[0]
    block_size = math.gcd(row_count, 512)
    block_count = row_count // block_size
    key_blocks = key_piece.reshape(block_count, block_size, heads_here, HD)
    value_blocks = value_piece.reshape(block_count, block_size, heads_here, HD)
    places = jnp.arange(row_count, dtype=jnp.int32).reshape(block_count, block_size)

    def advance(inner_state, block_item):
        key_block, value_block, place = block_item
        peak_score, weight_sum, weighted = inner_state
        scores = (
            jnp.einsum("qhd,khd->hqk", queries, key_block, preferred_element_type=jnp.float32)
            * score_scale
        )
        scores = jnp.where((place < valid_len)[None, None, :], scores, -jnp.inf)
        new_peak = jnp.maximum(peak_score, jnp.max(scores, axis=2))
        factor = jnp.exp(peak_score - new_peak)
        weights = jnp.exp(scores - new_peak[:, :, None])
        weight_sum = weight_sum * factor + jnp.sum(weights, axis=2)
        weighted = weighted * factor[:, :, None] + jnp.einsum(
            "hqk,khd->hqd",
            weights.astype(jnp.bfloat16),
            value_block,
            preferred_element_type=jnp.float32,
        )
        return ((new_peak, weight_sum, weighted), None)

    result, unused = lax.scan(advance, initial, (key_blocks, value_blocks, places))
    peak_score, weight_sum, weighted = result
    context = (
        (weighted / weight_sum[:, :, None])
        .astype(jnp.bfloat16)
        .transpose(1, 0, 2)
        .reshape(block_rows, head_cols)
    )
    attended = lax.psum_scatter(
        jnp.dot(context, out_rows, preferred_element_type=jnp.float32).astype(jnp.bfloat16),
        ("head", "fsdp"),
        scatter_dimension=0,
        tiled=True,
    ).astype(jnp.float32)
    middle = source + attended
    normed_two = layer_norm(middle, ln2_gain).astype(jnp.bfloat16)
    piece = lax.all_gather(normed_two, ("head", "fsdp"), axis=0, tiled=True)
    value_part = jnp.dot(piece, value_cols, preferred_element_type=jnp.float32)
    gate_part = jnp.dot(piece, gate_cols, preferred_element_type=jnp.float32)
    places = seq_start + jnp.arange(piece.shape[0], dtype=jnp.int32)
    gated_rows = jnp.where(
        (places < valid_len)[:, None], value_part * jax.nn.sigmoid(gate_part), 0.0
    ).astype(jnp.bfloat16)
    rim_width = (KERNEL - 1) // 2
    padded = with_halo(gated_rows, (("seq", 0),), rim_width).astype(jnp.float32)
    depth_sum = depth_kernel[0] * padded[0:block_rows]
    for offset in range(1, KERNEL):
        depth_sum = depth_sum + depth_kernel[offset] * padded[offset : offset + block_rows]
    shifted = depth_sum * bn_scale + bn_shift
    active = (shifted * jax.nn.sigmoid(shifted)).astype(jnp.bfloat16)
    conv_part = lax.psum_scatter(
        jnp.dot(active, down_rows, preferred_element_type=jnp.float32).astype(jnp.bfloat16),
        ("head", "fsdp"),
        scatter_dimension=0,
        tiled=True,
    ).astype(jnp.float32)
    return (middle + conv_part).astype(jnp.bfloat16)


SEQ = 4
EDGE = (KERNEL - 1) // 2
HALO = 2 * EDGE
SWAP = [(0, 1), (1, 0)]
F32 = jnp.float32
BF16 = jnp.bfloat16


def one_head_per_chip(mesh):
    return dict(mesh.shape) == {"parts": 2, "seq": SEQ, "head": 2, "fsdp": 2}


def xor_pairs(k):
    return [(i, i ^ k) for i in range(SEQ)]


def call(kernel, outs, scratch, length, *operands, vmem=8, left=0):
    fixed = [pltpu.with_memory_space_constraint(a, pltpu.HBM) for a in operands[:left]]
    return pl.pallas_call(
        kernel,
        out_shape=outs,
        in_specs=[pl.BlockSpec(memory_space=pltpu.SMEM)]
        + [pl.BlockSpec(memory_space=pltpu.HBM)] * left
        + [pl.BlockSpec(memory_space=pltpu.VMEM)] * (len(operands) - left),
        out_specs=[pl.BlockSpec(memory_space=pltpu.VMEM)] * len(outs),
        scratch_shapes=scratch,
        cost_estimate=pl.CostEstimate(flops=0, bytes_accessed=0, transcendentals=0),
        compiler_params=pltpu.CompilerParams(vmem_limit_bytes=vmem << 20),
    )(length, *fixed, *operands[left:])


def aligned(value, to):
    return pl.multiple_of(value, to)


def dot(a, b):
    return jnp.dot(a, b, preferred_element_type=F32)


def here():
    return tuple(lax.axis_index(a) for a in ("seq", "head", "fsdp", "parts"))


def deal_kernel(length, *refs):
    sources, later, other = refs[:4], refs[4:7], refs[7:10]
    outs, later_out, held, sems, later_sems = refs[10:14], *refs[14:]
    s, _, f, p = here()
    half = outs[0].shape[1]
    copies = [pltpu.make_async_copy(w, held.at[i], sems.at[i]) for i, w in enumerate(sources)]
    at = pl.ds(aligned(p * half, half), half)
    later_copies = [
        pltpu.make_async_copy(w.at[at], later_out.at[i], later_sems.at[i]) for i, w in enumerate(later)
    ]
    for copy in copies + later_copies:
        copy.start()
    mine, w_out = [held.at[m] for m in range(3)], held.at[3]
    for copy in copies:
        copy.wait()
    rows = pl.ds(aligned(f * half, half), half)
    for k in range(SEQ):
        head = s ^ k
        columns = pl.ds(aligned((head % 2) * HD, HD), HD)

        @pl.when(head // 2 == f)
        def _():
            for m in range(3):
                outs[k][m] = mine[m][rows, columns]

        @pl.when(head // 2 != f)
        def _():
            for m in range(3):
                outs[k][m] = other[m][rows, columns]

        for m in range(outs[k].shape[0] - 3):
            outs[k][3 + m] = w_out[at, m * HD : (m + 1) * HD]
    for copy in later_copies:
        copy.wait()


def stack_kernel(length, *refs):
    s = lax.axis_index("seq")
    for k in range(SEQ):
        refs[SEQ][s ^ k] = refs[k][...]


def project_kernel(length, *refs):
    frames, gain, *blocks = refs[: 2 * SEQ + 1]
    mine, other, down = refs[2 * SEQ + 1 : 3 * SEQ + 1], refs[3 * SEQ + 1 : 4 * SEQ + 1], refs[4 * SEQ + 1]
    q_out, send_out, edge_out, stack_out, normed, weights, x_edge, q_edge, own_x, own_gain, sems = refs[4 * SEQ + 2 :]
    copies = [
        pltpu.make_async_copy(frames, own_x, sems.at[0]),
        pltpu.make_async_copy(gain, own_gain, sems.at[1]),
    ]
    for copy in copies:
        copy.start()
    s, h, f, _ = here()
    blocks = [own_x, *blocks]
    rows = blocks[0].shape[0]
    half = mine[0].shape[1]
    for copy in copies:
        copy.wait()
    gain_row = own_gain[...]
    for slot, block in enumerate(blocks):
        at = (s ^ (slot // 2)) * 2 + (h ^ (slot % 2))
        x = block[...].astype(F32)
        normed[pl.ds(aligned(at * rows, rows), rows), :] = layer_norm(x, gain_row).astype(BF16)
        x_edge[at, 0:EDGE, :] = x[:EDGE]
        x_edge[at, EDGE:HALO, :] = x[rows - EDGE :]
    for k in range(SEQ):
        for core, pieces in enumerate((mine, other)):
            at = pl.ds(aligned((s ^ k) * 2 * half + (f ^ core) * half, half), half)
            for m in range(3):
                weights[at, m * HD : (m + 1) * HD] = pieces[k][m]
        stack_out[s ^ k] = down[...] if k == 2 else mine[k][3:]
    count = 2 * SEQ
    total = count * rows
    projected = dot(normed[...], weights[...])
    q_out[...] = projected[:, :HD].astype(BF16)
    send_out[0:total, :] = projected[:, HD : 2 * HD].astype(BF16)
    send_out[total : 2 * total, :] = projected[:, 2 * HD :].astype(BF16)
    for b in range(count):
        q_edge[b, 0:EDGE, :] = projected[b * rows : b * rows + EDGE, :HD]
        q_edge[b, EDGE:HALO, :] = projected[(b + 1) * rows - EDGE : (b + 1) * rows, :HD]

    def around(edge, b):
        low = jnp.maximum(b - f, 0)
        high = jnp.minimum(b + 1 - f, count - 1)
        return jnp.concatenate([edge[low, EDGE:HALO, :], edge[high, 0:EDGE, :]], axis=0)

    halos = jnp.concatenate([around(q_edge, b) for b in range(count)], axis=0)
    send_out[2 * total :, :] = halos.astype(BF16)
    edge_out[...] = jnp.concatenate([around(x_edge, s * 2 + b) for b in range(2)], axis=0).astype(BF16)


def attend_kernel(length, q_in, own, peer, *refs):
    ctx_outs, q_rows = refs[:SEQ], refs[SEQ]
    s, _, f, _ = here()
    valid_len = length[0]
    count = q_rows.shape[0]
    total = q_in.shape[0]
    rows = total // count
    step = q_rows.shape[1]
    local = lax.broadcasted_iota(jnp.int32, (step, total), 1)
    base = (local // rows) * (2 * rows) + local % rows
    keep_own = base + f * rows < valid_len
    keep_peer = base + (1 - f) * rows < valid_len
    scale = 1.0 / math.sqrt(HD)
    keys_t = (((1,), (1,)), ((), ()))
    for b in range(count):
        q_rows[b, 0:rows, :] = q_in[b * rows : (b + 1) * rows, :].astype(F32)
        q_rows[b, rows:step, :] = peer[2 * total + b * HALO : 2 * total + (b + 1) * HALO, :].astype(F32)
    for b in range(count):
        k, side = b // 2, b % 2
        q = q_rows[(s ^ k) * 2 + side].astype(BF16)
        first = lax.dot_general(q, own[0:total, :], keys_t, preferred_element_type=F32) * scale
        second = lax.dot_general(q, peer[0:total, :], keys_t, preferred_element_type=F32) * scale
        first = jnp.where(keep_own, first, -jnp.inf)
        second = jnp.where(keep_peer, second, -jnp.inf)
        peak = jnp.maximum(
            jnp.max(first, axis=1, keepdims=True), jnp.max(second, axis=1, keepdims=True)
        )
        first = jnp.exp(first - peak)
        second = jnp.exp(second - peak)
        weight_sum = jnp.sum(first, axis=1, keepdims=True) + jnp.sum(second, axis=1, keepdims=True)
        weighted = dot(first.astype(BF16), own[total : 2 * total, :]) + dot(
            second.astype(BF16), peer[total : 2 * total, :]
        )
        ctx_outs[k][side * step : (side + 1) * step, :] = (weighted / weight_sum).astype(BF16)


def output_kernel(length, *refs):
    pieces, ctx = refs[:4], refs[4 : 4 + SEQ]
    share_out, send_out, context, weights = refs[4 + SEQ :]
    s, h, f, p = here()
    half = pieces[0].shape[2]
    columns = weights.shape[2]
    for y in range(2):
        for core in range(2):
            rows = pl.ds(aligned((f ^ core) * 2 * half + (p ^ y) * half, half), half)
            for m in range(columns // HD):
                for j in range(SEQ):
                    weights[j, rows, m * HD : (m + 1) * HD] = pieces[y * 2 + core][j, m]
    for k in range(SEQ):
        context[:, pl.ds(aligned((s ^ k) * HD, HD), HD)] = ctx[k][...]
    for j in range(SEQ):
        at = slice(j * columns, (j + 1) * columns)
        share = dot(context[...], weights[j])
        share_out[:, at] = share
        send_out[:, at] = share.astype(BF16)


def convolve_kernel(length, *refs):
    own_x, gain, pieces = refs[0], refs[1], refs[2:6]
    peer_x, halo_x, own_share, peer_share, own_c, peer_c, base_out, share_out = refs[6:14]
    mid, normed, w_value, w_gate, w_down, channel, padded, active, shares = refs[14:]
    s, h, f, p = here()
    valid_len = length[0]
    half, columns = pieces[0].shape[2:]
    rows = own_x.shape[0]
    step = rows + HALO
    for y in range(2):
        for core in range(2):
            stack = pieces[y * 2 + core]
            down = pl.ds(aligned((f ^ core) * 2 * half + (p ^ y) * half, half), half)
            for plane in range(SEQ):
                at = pl.ds(aligned(plane * 2 * half + (p ^ y) * half, half), half)
                w_value[f ^ core, at, :] = stack[plane, 0]
                w_gate[f ^ core, at, :] = stack[plane, 1]
                w_down[plane, down, :] = stack[plane, 2]
    channel[f] = own_c[...]
    channel[1 - f] = peer_c[...]
    mid[pl.ds(aligned(h * step, 8), rows), :] = own_x[...].astype(F32)
    mid[pl.ds(aligned((1 - h) * step, 8), rows), :] = peer_x[...].astype(F32)
    for b in range(2):
        mid[b * step + rows : (b + 1) * step, :] = halo_x[b * HALO : (b + 1) * HALO, :].astype(F32)
    middle = mid[...] + (own_share[...] + peer_share[...].astype(F32))
    mid[...] = middle
    normed[...] = layer_norm(middle, gain[...]).astype(BF16)
    place = lax.broadcasted_iota(jnp.int32, (step, columns), 0)
    offset = jnp.where(place < rows, place, jnp.where(place < rows + EDGE, place - rows - EDGE, place - EDGE))
    for c in range(2):
        x = normed[...]
        value_part = dot(x, w_value[c])
        gate_part = dot(x, w_gate[c])
        gated = value_part * jax.nn.sigmoid(gate_part)
        for b in range(2):
            t = offset + (4 * s + 2 * b + f) * rows
            kept = jnp.where((t >= 0) & (t < valid_len), gated[b * step : (b + 1) * step], 0.0)
            kept = kept.astype(BF16).astype(F32)
            padded[b, 8 : 8 + rows, :] = kept[:rows]
            padded[b, 8 - EDGE : 8, :] = kept[rows : rows + EDGE]
            padded[b, 8 + rows : 8 + rows + EDGE, :] = kept[rows + EDGE :]
            depth_sum = channel[c, 0:1, :] * padded[b, 8 - EDGE : 8 - EDGE + rows, :]
            for j in range(1, KERNEL):
                low = 8 - EDGE + j
                depth_sum = depth_sum + channel[c, j : j + 1, :] * padded[b, low : low + rows, :]
            shifted = depth_sum * channel[c, KERNEL : KERNEL + 1, :] + channel[c, KERNEL + 1 : KERNEL + 2, :]
            active[b * rows : (b + 1) * rows, c * columns : (c + 1) * columns] = (
                shifted * jax.nn.sigmoid(shifted)
            ).astype(BF16)
    for j in range(SEQ):
        shares[:, j * columns : (j + 1) * columns] = dot(active[...], w_down[j])
    base_out[...] = mid[pl.ds(aligned(h * step, 8), rows), :] + shares[pl.ds(aligned(h * rows, rows), rows), :]
    share_out[...] = shares[pl.ds(aligned((1 - h) * rows, rows), rows), :].astype(BF16)


def shards_chip_per_head(
    frames,
    length,
    ln1_gain,
    w_query,
    w_key,
    w_value,
    w_out,
    ln2_gain,
    pw1_value,
    pw1_gate,
    depth_kernel,
    bn_scale,
    bn_shift,
    pw2,
):
    rows, width = frames.shape
    count = 2 * SEQ
    step = rows + HALO
    f, p = lax.axis_index("fsdp"), lax.axis_index("parts")
    half = w_query.shape[0] // 2
    columns = w_query.shape[1]
    barrier = lax.optimization_barrier

    def after(x, *others):
        return barrier((x, *others))[0]

    def other_core(x):
        return lax.ppermute(x, "fsdp", SWAP)

    def other_side(x):
        return lax.ppermute(x, "head", SWAP)

    def other_part(x):
        return lax.ppermute(x, "parts", SWAP)

    def across(x, k):
        return lax.ppermute(x, "seq", xor_pairs(k))

    def planes(x):
        far = across(x, 3)
        return [x, across(x, 1), across(far, 1), far]

    def part_half(x):
        return lax.dynamic_slice_in_dim(x, p * half, half, axis=x.ndim - 2)

    near = planes(frames)
    blocks = []
    for block in near:
        blocks += [block, other_side(block)]
    given = [w_query, w_key, w_value]
    shape = jax.ShapeDtypeStruct
    *dealt, pw_mine = call(
        deal_kernel,
        [shape((3 if k == 2 else 3 + columns // HD, half, HD), BF16) for k in range(SEQ)]
        + [shape((3, half, columns), BF16)],
        [
            pltpu.VMEM((4, 2 * half, columns), BF16),
            pltpu.SemaphoreType.DMA((4,)),
            pltpu.SemaphoreType.DMA((3,)),
        ],
        length,
        *given,
        w_out,
        pw1_value,
        pw1_gate,
        pw2,
        *[other_core(w) for w in given],
        left=7,
    )
    *dealt, _ = barrier((*dealt, near[1]))
    w_mine = [dealt[0]] + [across(dealt[k], k) for k in range(1, SEQ)]
    w_other = [other_core(w[:3]) for w in w_mine]
    down = across(w_mine[3][3:], 1)
    pw_part = other_part(pw_mine)
    w_other[0], pw_part = barrier((w_other[0], pw_part))
    pw_later = after(pw_mine, *w_mine[1:], down)
    pw_one, pw_three = across(pw_later, 1), across(pw_later, 3)
    queries, send, edges, stack = call(
        project_kernel,
        [
            shape((count * rows, HD), BF16),
            shape((2 * count * rows + count * HALO, HD), BF16),
            shape((2 * HALO, width), BF16),
            shape((SEQ, columns // HD, half, HD), BF16),
        ],
        [
            pltpu.VMEM((count * rows, width), BF16),
            pltpu.VMEM((width, 3 * HD), BF16),
            pltpu.VMEM((count, HALO, width), F32),
            pltpu.VMEM((count, HALO, HD), F32),
            pltpu.VMEM((rows, width), BF16),
            pltpu.VMEM((1, width), F32),
            pltpu.SemaphoreType.DMA((2,)),
        ],
        length,
        frames,
        ln1_gain[None],
        *blocks[1:],
        *w_mine,
        *w_other,
        down,
        left=2,
    )
    received = other_core(send)
    stack_part = other_part(stack)
    ctx = call(
        attend_kernel,
        [shape((2 * step, HD), BF16)] * SEQ,
        [pltpu.VMEM((count, step, HD), F32)],
        length,
        queries,
        send,
        received,
    )
    stack, stack_part, *_ = barrier((stack, stack_part, *ctx))
    out_pieces = [stack, other_core(stack), stack_part, other_core(stack_part)]
    ctx = [ctx[0]] + [lax.ppermute(ctx[k], "seq", xor_pairs(k)) for k in range(1, SEQ)]
    one_part = other_part(pw_one)
    ctx[0] = after(ctx[0], one_part)
    pw_far = after(pw_three, *ctx[1:])
    pw_two, three_part = across(pw_far, 1), other_part(pw_far)
    own_share, sent_share = call(
        output_kernel,
        [shape((2 * step, width), F32), shape((2 * step, width), BF16)],
        [
            pltpu.VMEM((2 * step, SEQ * HD), BF16),
            pltpu.VMEM((SEQ, 2 * columns, columns), BF16),
        ],
        length,
        *out_pieces,
        *ctx,
    )
    edges, depth_kernel = after(edges, own_share), after(depth_kernel, own_share)
    halo_x = other_core(edges)
    channels = jnp.concatenate([depth_kernel, bn_scale[None], bn_shift[None], jnp.zeros((5, columns), F32)])
    channels_peer = other_core(channels)
    peer_share = other_side(sent_share)

    def stacked(*pieces):
        (stack,) = call(stack_kernel, [shape((SEQ, *pieces[0].shape), BF16)], [], length, *pieces)
        return [stack, other_core(stack)]

    two_part = other_part(pw_two)
    pw_mine = after(pw_mine, own_share)
    pw_pieces = stacked(pw_mine, pw_one, pw_two, pw_three) + stacked(after(pw_part, channels_peer, halo_x, peer_share), one_part, two_part, three_part)
    base, share = call(
        convolve_kernel,
        [shape((rows, width), F32), shape((rows, width), BF16)],
        [
            pltpu.VMEM((2 * step, width), F32),
            pltpu.VMEM((2 * step, width), BF16),
            pltpu.VMEM((2, width, columns), BF16),
            pltpu.VMEM((2, width, columns), BF16),
            pltpu.VMEM((SEQ, 2 * columns, columns), BF16),
            pltpu.VMEM((2, 16, columns), F32),
            pltpu.VMEM((2, 16 + rows, columns), F32),
            pltpu.VMEM((2 * rows, 2 * columns), BF16),
            pltpu.VMEM((2 * rows, width), F32),
        ],
        length,
        frames,
        ln2_gain[None],
        *pw_pieces,
        blocks[1],
        halo_x,
        own_share,
        peer_share,
        channels,
        channels_peer,
        vmem=14,
    )
    return (base + other_side(share).astype(F32)).astype(BF16)


def solution(mesh):
    in_specs = (
        P(("parts", "seq", "head", "fsdp"), None),
        P("parts"),
        P(),
        P("seq", ("head", "fsdp")),
        P("seq", ("head", "fsdp")),
        P("seq", ("head", "fsdp")),
        P(("head", "fsdp"), "seq"),
        P(),
        P("seq", ("head", "fsdp")),
        P("seq", ("head", "fsdp")),
        P(None, ("head", "fsdp")),
        P(("head", "fsdp")),
        P(("head", "fsdp")),
        P(("head", "fsdp"), "seq"),
    )
    out_specs = P(("parts", "seq", "head", "fsdp"), None)
    body = shards_chip_per_head if one_head_per_chip(mesh) else shards_general
    return jax.shard_map(body, mesh=mesh, in_specs=in_specs, out_specs=out_specs, check_vma=False)
```

```python
import math

import jax
import jax.numpy as jnp
from jax import lax
from jax.experimental import pallas as pl
from jax.experimental.pallas import tpu as pltpu
from jax.sharding import PartitionSpec as P

KERNEL = 9
HD = 128


def with_halo(block, sides, width):
    for axis, dim in sides:
        count = lax.axis_size(axis)
        forward = [(i, i + 1) for i in range(count - 1)]
        backward = [(target, source) for source, target in forward]
        low = lax.ppermute(
            lax.slice_in_dim(block, block.shape[dim] - width, None, axis=dim), axis, forward
        )
        high = lax.ppermute(lax.slice_in_dim(block, 0, width, axis=dim), axis, backward)
        block = jnp.concatenate([low, block, high], axis=dim)
    return block


def layer_norm(values_in, gain_vec):
    center = jnp.mean(values_in, axis=-1, keepdims=True)
    shifted = values_in - center
    spread = jnp.mean(shifted * shifted, axis=-1, keepdims=True)
    return shifted * lax.rsqrt(spread + 1e-05) * gain_vec


def shards_general(
    frames,
    length,
    ln1_gain,
    w_query,
    w_key,
    w_value,
    w_out,
    ln2_gain,
    pw1_value,
    pw1_gate,
    depth_kernel,
    bn_scale,
    bn_shift,
    pw2,
):
    group_size = lax.axis_size(("head", "fsdp"))
    my_rows = frames.shape[0]
    block_rows = my_rows * group_size
    head_cols = w_query.shape[1]
    heads_here = head_cols // HD
    seq_start = lax.axis_index("seq") * block_rows
    valid_len = length[0]
    score_scale = 1.0 / math.sqrt(HD)
    full_query, full_key, full_value, value_cols, gate_cols = (
        lax.all_gather(w_query, "seq", axis=0, tiled=True),
        lax.all_gather(w_key, "seq", axis=0, tiled=True),
        lax.all_gather(w_value, "seq", axis=0, tiled=True),
        lax.all_gather(pw1_value, "seq", axis=0, tiled=True),
        lax.all_gather(pw1_gate, "seq", axis=0, tiled=True),
    )
    out_rows, down_rows = (
        lax.all_gather(w_out, "seq", axis=1, tiled=True),
        lax.all_gather(pw2, "seq", axis=1, tiled=True),
    )
    projector = jnp.concatenate((full_query, full_key, full_value), axis=1)
    source = frames.astype(jnp.float32)
    normed = layer_norm(source, ln1_gain).astype(jnp.bfloat16)
    projected = jnp.dot(
        lax.all_gather(normed, ("head", "fsdp"), axis=0, tiled=True),
        projector,
        preferred_element_type=jnp.float32,
    ).astype(jnp.bfloat16)
    queries = projected[:, :head_cols].reshape(block_rows, heads_here, HD)
    keys_here = projected[:, head_cols : 2 * head_cols]
    values_here = projected[:, 2 * head_cols :]
    initial = (
        jnp.full((heads_here, block_rows), -1e30, jnp.float32),
        jnp.zeros((heads_here, block_rows), jnp.float32),
        jnp.zeros((heads_here, block_rows, HD), jnp.float32),
    )
    key_piece = lax.all_gather(keys_here, "seq", axis=0, tiled=True)
    value_piece = lax.all_gather(values_here, "seq", axis=0, tiled=True)
    row_count = key_piece.shape[0]
    block_size = math.gcd(row_count, 512)
    block_count = row_count // block_size
    key_blocks = key_piece.reshape(block_count, block_size, heads_here, HD)
    value_blocks = value_piece.reshape(block_count, block_size, heads_here, HD)
    places = jnp.arange(row_count, dtype=jnp.int32).reshape(block_count, block_size)

    def advance(inner_state, block_item):
        key_block, value_block, place = block_item
        peak_score, weight_sum, weighted = inner_state
        scores = (
            jnp.einsum("qhd,khd->hqk", queries, key_block, preferred_element_type=jnp.float32)
            * score_scale
        )
        scores = jnp.where((place < valid_len)[None, None, :], scores, -jnp.inf)
        new_peak = jnp.maximum(peak_score, jnp.max(scores, axis=2))
        factor = jnp.exp(peak_score - new_peak)
        weights = jnp.exp(scores - new_peak[:, :, None])
        weight_sum = weight_sum * factor + jnp.sum(weights, axis=2)
        weighted = weighted * factor[:, :, None] + jnp.einsum(
            "hqk,khd->hqd",
            weights.astype(jnp.bfloat16),
            value_block,
            preferred_element_type=jnp.float32,
        )
        return ((new_peak, weight_sum, weighted), None)

    result, unused = lax.scan(advance, initial, (key_blocks, value_blocks, places))
    peak_score, weight_sum, weighted = result
    context = (
        (weighted / weight_sum[:, :, None])
        .astype(jnp.bfloat16)
        .transpose(1, 0, 2)
        .reshape(block_rows, head_cols)
    )
    attended = lax.psum_scatter(
        jnp.dot(context, out_rows, preferred_element_type=jnp.float32).astype(jnp.bfloat16),
        ("head", "fsdp"),
        scatter_dimension=0,
        tiled=True,
    ).astype(jnp.float32)
    middle = source + attended
    normed_two = layer_norm(middle, ln2_gain).astype(jnp.bfloat16)
    piece = lax.all_gather(normed_two, ("head", "fsdp"), axis=0, tiled=True)
    value_part = jnp.dot(piece, value_cols, preferred_element_type=jnp.float32)
    gate_part = jnp.dot(piece, gate_cols, preferred_element_type=jnp.float32)
    places = seq_start + jnp.arange(piece.shape[0], dtype=jnp.int32)
    gated_rows = jnp.where(
        (places < valid_len)[:, None], value_part * jax.nn.sigmoid(gate_part), 0.0
    ).astype(jnp.bfloat16)
    rim_width = (KERNEL - 1) // 2
    padded = with_halo(gated_rows, (("seq", 0),), rim_width).astype(jnp.float32)
    depth_sum = depth_kernel[0] * padded[0:block_rows]
    for offset in range(1, KERNEL):
        depth_sum = depth_sum + depth_kernel[offset] * padded[offset : offset + block_rows]
    shifted = depth_sum * bn_scale + bn_shift
    active = (shifted * jax.nn.sigmoid(shifted)).astype(jnp.bfloat16)
    conv_part = lax.psum_scatter(
        jnp.dot(active, down_rows, preferred_element_type=jnp.float32).astype(jnp.bfloat16),
        ("head", "fsdp"),
        scatter_dimension=0,
        tiled=True,
    ).astype(jnp.float32)
    return (middle + conv_part).astype(jnp.bfloat16)


SEQ = 4
EDGE = (KERNEL - 1) // 2
HALO = 2 * EDGE
SWAP = [(0, 1), (1, 0)]
F32 = jnp.float32
BF16 = jnp.bfloat16


def one_head_per_chip(mesh):
    return dict(mesh.shape) == {"parts": 2, "seq": SEQ, "head": 2, "fsdp": 2}


def xor_pairs(k):
    return [(i, i ^ k) for i in range(SEQ)]


def call(kernel, outs, scratch, length, *operands, vmem=8, left=0):
    fixed = [pltpu.with_memory_space_constraint(a, pltpu.HBM) for a in operands[:left]]
    return pl.pallas_call(
        kernel,
        out_shape=outs,
        in_specs=[pl.BlockSpec(memory_space=pltpu.SMEM)]
        + [pl.BlockSpec(memory_space=pltpu.HBM)] * left
        + [pl.BlockSpec(memory_space=pltpu.VMEM)] * (len(operands) - left),
        out_specs=[pl.BlockSpec(memory_space=pltpu.VMEM)] * len(outs),
        scratch_shapes=scratch,
        cost_estimate=pl.CostEstimate(flops=0, bytes_accessed=0, transcendentals=0),
        compiler_params=pltpu.CompilerParams(vmem_limit_bytes=vmem << 20),
    )(length, *fixed, *operands[left:])


def aligned(value, to):
    return pl.multiple_of(value, to)


def dot(a, b):
    return jnp.dot(a, b, preferred_element_type=F32)


def here():
    return tuple(lax.axis_index(a) for a in ("seq", "head", "fsdp", "parts"))


def deal_kernel(length, *refs):
    sources, later, other = refs[:4], refs[4:7], refs[7:10]
    outs, later_out, held, sems, later_sems = refs[10:14], *refs[14:]
    s, _, f, p = here()
    half = outs[0].shape[1]
    copies = [pltpu.make_async_copy(w, held.at[i], sems.at[i]) for i, w in enumerate(sources)]
    at = pl.ds(aligned(p * half, half), half)
    later_copies = [
        pltpu.make_async_copy(w.at[at], later_out.at[i], later_sems.at[i]) for i, w in enumerate(later)
    ]
    for copy in copies + later_copies:
        copy.start()
    mine, w_out = [held.at[m] for m in range(3)], held.at[3]
    for copy in copies:
        copy.wait()
    rows = pl.ds(aligned(f * half, half), half)
    for k in range(SEQ):
        head = s ^ k
        columns = pl.ds(aligned((head % 2) * HD, HD), HD)

        @pl.when(head // 2 == f)
        def _():
            for m in range(3):
                outs[k][m] = mine[m][rows, columns]

        @pl.when(head // 2 != f)
        def _():
            for m in range(3):
                outs[k][m] = other[m][rows, columns]

        for m in range(outs[k].shape[0] - 3):
            outs[k][3 + m] = w_out[at, m * HD : (m + 1) * HD]
    for copy in later_copies:
        copy.wait()


def stack_kernel(length, *refs):
    s = lax.axis_index("seq")
    for k in range(SEQ):
        refs[SEQ][s ^ k] = refs[k][...]


def project_kernel(length, *refs):
    frames, gain, *blocks = refs[: 2 * SEQ + 1]
    mine, other, down = refs[2 * SEQ + 1 : 3 * SEQ + 1], refs[3 * SEQ + 1 : 4 * SEQ + 1], refs[4 * SEQ + 1]
    q_out, send_out, edge_out, stack_out, normed, weights, x_edge, q_edge, own_x, own_gain, sems = refs[4 * SEQ + 2 :]
    copies = [
        pltpu.make_async_copy(frames, own_x, sems.at[0]),
        pltpu.make_async_copy(gain, own_gain, sems.at[1]),
    ]
    for copy in copies:
        copy.start()
    s, h, f, _ = here()
    blocks = [own_x, *blocks]
    rows = blocks[0].shape[0]
    half = mine[0].shape[1]
    for copy in copies:
        copy.wait()
    gain_row = own_gain[...]
    for slot, block in enumerate(blocks):
        at = (s ^ (slot // 2)) * 2 + (h ^ (slot % 2))
        x = block[...].astype(F32)
        normed[pl.ds(aligned(at * rows, rows), rows), :] = layer_norm(x, gain_row).astype(BF16)
        x_edge[at, 0:EDGE, :] = x[:EDGE]
        x_edge[at, EDGE:HALO, :] = x[rows - EDGE :]
    for k in range(SEQ):
        for core, pieces in enumerate((mine, other)):
            at = pl.ds(aligned((s ^ k) * 2 * half + (f ^ core) * half, half), half)
            for m in range(3):
                weights[at, m * HD : (m + 1) * HD] = pieces[k][m]
        stack_out[s ^ k] = down[...] if k == 2 else mine[k][3:]
    count = 2 * SEQ
    total = count * rows
    projected = dot(normed[...], weights[...])
    q_out[...] = projected[:, :HD].astype(BF16)
    send_out[0:total, :] = projected[:, HD : 2 * HD].astype(BF16)
    send_out[total : 2 * total, :] = projected[:, 2 * HD :].astype(BF16)
    for b in range(count):
        q_edge[b, 0:EDGE, :] = projected[b * rows : b * rows + EDGE, :HD]
        q_edge[b, EDGE:HALO, :] = projected[(b + 1) * rows - EDGE : (b + 1) * rows, :HD]

    def around(edge, b):
        low = jnp.maximum(b - f, 0)
        high = jnp.minimum(b + 1 - f, count - 1)
        return jnp.concatenate([edge[low, EDGE:HALO, :], edge[high, 0:EDGE, :]], axis=0)

    halos = jnp.concatenate([around(q_edge, b) for b in range(count)], axis=0)
    send_out[2 * total :, :] = halos.astype(BF16)
    edge_out[...] = jnp.concatenate([around(x_edge, s * 2 + b) for b in range(2)], axis=0).astype(BF16)


def attend_kernel(length, q_in, own, peer, *refs):
    ctx_outs, q_rows = refs[:SEQ], refs[SEQ]
    s, _, f, _ = here()
    valid_len = length[0]
    count = q_rows.shape[0]
    total = q_in.shape[0]
    rows = total // count
    step = q_rows.shape[1]
    local = lax.broadcasted_iota(jnp.int32, (1, total), 1)
    base = (local // rows) * (2 * rows) + local % rows
    keep_own = base + f * rows < valid_len
    keep_peer = base + (1 - f) * rows < valid_len
    scale = 1.0 / math.sqrt(HD)
    keys_t = (((1,), (1,)), ((), ()))
    for b in range(count):
        q_rows[b, 0:rows, :] = q_in[b * rows : (b + 1) * rows, :].astype(F32)
        q_rows[b, rows:step, :] = peer[2 * total + b * HALO : 2 * total + (b + 1) * HALO, :].astype(F32)
    for k in range(SEQ):
        q = jnp.concatenate([q_rows[(s ^ k) * 2 + side] for side in range(2)], axis=0).astype(BF16)
        first = lax.dot_general(q, own[0:total, :], keys_t, preferred_element_type=F32) * scale
        second = lax.dot_general(q, peer[0:total, :], keys_t, preferred_element_type=F32) * scale
        first = jnp.where(keep_own, first, -jnp.inf)
        second = jnp.where(keep_peer, second, -jnp.inf)
        peak = jnp.maximum(
            jnp.max(first, axis=1, keepdims=True), jnp.max(second, axis=1, keepdims=True)
        )
        first = jnp.exp(first - peak)
        second = jnp.exp(second - peak)
        weight_sum = jnp.sum(first, axis=1, keepdims=True) + jnp.sum(second, axis=1, keepdims=True)
        weighted = dot(first.astype(BF16), own[total : 2 * total, :]) + dot(
            second.astype(BF16), peer[total : 2 * total, :]
        )
        ctx_outs[k][...] = (weighted / weight_sum).astype(BF16)


def output_kernel(length, *refs):
    pieces, ctx = refs[:4], refs[4 : 4 + SEQ]
    share_out, send_out, context, weights = refs[4 + SEQ :]
    s, h, f, p = here()
    half = pieces[0].shape[2]
    columns = weights.shape[2]
    for y in range(2):
        for core in range(2):
            rows = pl.ds(aligned((f ^ core) * 2 * half + (p ^ y) * half, half), half)
            for m in range(columns // HD):
                for j in range(SEQ):
                    weights[j, rows, m * HD : (m + 1) * HD] = pieces[y * 2 + core][j, m]
    for k in range(SEQ):
        context[:, pl.ds(aligned((s ^ k) * HD, HD), HD)] = ctx[k][...]
    for j in range(SEQ):
        at = slice(j * columns, (j + 1) * columns)
        share = dot(context[...], weights[j])
        share_out[:, at] = share
        send_out[:, at] = share.astype(BF16)


def convolve_kernel(length, *refs):
    own_x, gain, pieces = refs[0], refs[1], refs[2:6]
    peer_x, halo_x, own_share, peer_share, own_c, peer_c, base_out, share_out = refs[6:14]
    mid, normed, w_value, w_gate, w_down, channel, padded, active, shares = refs[14:]
    s, h, f, p = here()
    valid_len = length[0]
    half, columns = pieces[0].shape[2:]
    rows = own_x.shape[0]
    step = rows + HALO
    for y in range(2):
        for core in range(2):
            stack = pieces[y * 2 + core]
            down = pl.ds(aligned((f ^ core) * 2 * half + (p ^ y) * half, half), half)
            for plane in range(SEQ):
                at = pl.ds(aligned(plane * 2 * half + (p ^ y) * half, half), half)
                w_value[f ^ core, at, :] = stack[plane, 0]
                w_gate[f ^ core, at, :] = stack[plane, 1]
                w_down[plane, down, :] = stack[plane, 2]
    channel[f] = own_c[...]
    channel[1 - f] = peer_c[...]
    mid[pl.ds(aligned(h * step, 8), rows), :] = own_x[...].astype(F32)
    mid[pl.ds(aligned((1 - h) * step, 8), rows), :] = peer_x[...].astype(F32)
    for b in range(2):
        mid[b * step + rows : (b + 1) * step, :] = halo_x[b * HALO : (b + 1) * HALO, :].astype(F32)
    middle = mid[...] + (own_share[...] + peer_share[...].astype(F32))
    mid[...] = middle
    normed[...] = layer_norm(middle, gain[...]).astype(BF16)
    place = lax.broadcasted_iota(jnp.int32, (step, columns), 0)
    offset = jnp.where(place < rows, place, jnp.where(place < rows + EDGE, place - rows - EDGE, place - EDGE))
    for c in range(2):
        x = normed[...]
        value_part = dot(x, w_value[c])
        gate_part = dot(x, w_gate[c])
        gated = value_part * jax.nn.sigmoid(gate_part)
        for b in range(2):
            t = offset + (4 * s + 2 * b + f) * rows
            kept = jnp.where((t >= 0) & (t < valid_len), gated[b * step : (b + 1) * step], 0.0)
            kept = kept.astype(BF16).astype(F32)
            padded[b, 8 : 8 + rows, :] = kept[:rows]
            padded[b, 8 - EDGE : 8, :] = kept[rows : rows + EDGE]
            padded[b, 8 + rows : 8 + rows + EDGE, :] = kept[rows + EDGE :]
            depth_sum = channel[c, 0:1, :] * padded[b, 8 - EDGE : 8 - EDGE + rows, :]
            for j in range(1, KERNEL):
                low = 8 - EDGE + j
                depth_sum = depth_sum + channel[c, j : j + 1, :] * padded[b, low : low + rows, :]
            shifted = depth_sum * channel[c, KERNEL : KERNEL + 1, :] + channel[c, KERNEL + 1 : KERNEL + 2, :]
            active[b * rows : (b + 1) * rows, c * columns : (c + 1) * columns] = (
                shifted * jax.nn.sigmoid(shifted)
            ).astype(BF16)
    for j in range(SEQ):
        shares[:, j * columns : (j + 1) * columns] = dot(active[...], w_down[j])
    base_out[...] = mid[pl.ds(aligned(h * step, 8), rows), :] + shares[pl.ds(aligned(h * rows, rows), rows), :]
    share_out[...] = shares[pl.ds(aligned((1 - h) * rows, rows), rows), :].astype(BF16)


def shards_chip_per_head(
    frames,
    length,
    ln1_gain,
    w_query,
    w_key,
    w_value,
    w_out,
    ln2_gain,
    pw1_value,
    pw1_gate,
    depth_kernel,
    bn_scale,
    bn_shift,
    pw2,
):
    rows, width = frames.shape
    count = 2 * SEQ
    step = rows + HALO
    f, p = lax.axis_index("fsdp"), lax.axis_index("parts")
    half = w_query.shape[0] // 2
    columns = w_query.shape[1]
    barrier = lax.optimization_barrier

    def after(x, *others):
        return barrier((x, *others))[0]

    def other_core(x):
        return lax.ppermute(x, "fsdp", SWAP)

    def other_side(x):
        return lax.ppermute(x, "head", SWAP)

    def other_part(x):
        return lax.ppermute(x, "parts", SWAP)

    def across(x, k):
        return lax.ppermute(x, "seq", xor_pairs(k))

    def planes(x):
        far = across(x, 3)
        return [x, across(x, 1), across(far, 1), far]

    def part_half(x):
        return lax.dynamic_slice_in_dim(x, p * half, half, axis=x.ndim - 2)

    near = planes(frames)
    blocks = []
    for block in near:
        blocks += [block, other_side(block)]
    given = [w_query, w_key, w_value]
    shape = jax.ShapeDtypeStruct
    *dealt, pw_mine = call(
        deal_kernel,
        [shape((3 if k == 2 else 3 + columns // HD, half, HD), BF16) for k in range(SEQ)]
        + [shape((3, half, columns), BF16)],
        [
            pltpu.VMEM((4, 2 * half, columns), BF16),
            pltpu.SemaphoreType.DMA((4,)),
            pltpu.SemaphoreType.DMA((3,)),
        ],
        length,
        *given,
        w_out,
        pw1_value,
        pw1_gate,
        pw2,
        *[other_core(w) for w in given],
        left=7,
    )
    *dealt, _ = barrier((*dealt, near[1]))
    w_mine = [dealt[0]] + [across(dealt[k], k) for k in range(1, SEQ)]
    w_other = [other_core(w[:3]) for w in w_mine]
    down = across(w_mine[3][3:], 1)
    pw_part = other_part(pw_mine)
    w_other[0], pw_part = barrier((w_other[0], pw_part))
    pw_later = after(pw_mine, *w_mine[1:], down)
    pw_one, pw_three = across(pw_later, 1), across(pw_later, 3)
    queries, send, edges, stack = call(
        project_kernel,
        [
            shape((count * rows, HD), BF16),
            shape((2 * count * rows + count * HALO, HD), BF16),
            shape((2 * HALO, width), BF16),
            shape((SEQ, columns // HD, half, HD), BF16),
        ],
        [
            pltpu.VMEM((count * rows, width), BF16),
            pltpu.VMEM((width, 3 * HD), BF16),
            pltpu.VMEM((count, HALO, width), F32),
            pltpu.VMEM((count, HALO, HD), F32),
            pltpu.VMEM((rows, width), BF16),
            pltpu.VMEM((1, width), F32),
            pltpu.SemaphoreType.DMA((2,)),
        ],
        length,
        frames,
        ln1_gain[None],
        *blocks[1:],
        *w_mine,
        *w_other,
        down,
        left=2,
    )
    received = other_core(send)
    stack_part = other_part(stack)
    ctx = call(
        attend_kernel,
        [shape((2 * step, HD), BF16)] * SEQ,
        [pltpu.VMEM((count, step, HD), F32)],
        length,
        queries,
        send,
        received,
    )
    stack, stack_part, *_ = barrier((stack, stack_part, *ctx))
    out_pieces = [stack, other_core(stack), stack_part, other_core(stack_part)]
    ctx = [ctx[0]] + [lax.ppermute(ctx[k], "seq", xor_pairs(k)) for k in range(1, SEQ)]
    one_part = other_part(pw_one)
    ctx[0] = after(ctx[0], one_part)
    pw_far = after(pw_three, *ctx[1:])
    pw_two, three_part = across(pw_far, 1), other_part(pw_far)
    own_share, sent_share = call(
        output_kernel,
        [shape((2 * step, width), F32), shape((2 * step, width), BF16)],
        [
            pltpu.VMEM((2 * step, SEQ * HD), BF16),
            pltpu.VMEM((SEQ, 2 * columns, columns), BF16),
        ],
        length,
        *out_pieces,
        *ctx,
    )
    edges, depth_kernel = after(edges, own_share), after(depth_kernel, own_share)
    halo_x = other_core(edges)
    channels = jnp.concatenate([depth_kernel, bn_scale[None], bn_shift[None], jnp.zeros((5, columns), F32)])
    channels_peer = other_core(channels)
    peer_share = other_side(sent_share)

    def stacked(*pieces):
        (stack,) = call(stack_kernel, [shape((SEQ, *pieces[0].shape), BF16)], [], length, *pieces)
        return [stack, other_core(stack)]

    two_part = other_part(pw_two)
    pw_mine = after(pw_mine, own_share)
    pw_pieces = stacked(pw_mine, pw_one, pw_two, pw_three) + stacked(after(pw_part, channels_peer, halo_x, peer_share), one_part, two_part, three_part)
    base, share = call(
        convolve_kernel,
        [shape((rows, width), F32), shape((rows, width), BF16)],
        [
            pltpu.VMEM((2 * step, width), F32),
            pltpu.VMEM((2 * step, width), BF16),
            pltpu.VMEM((2, width, columns), BF16),
            pltpu.VMEM((2, width, columns), BF16),
            pltpu.VMEM((SEQ, 2 * columns, columns), BF16),
            pltpu.VMEM((2, 16, columns), F32),
            pltpu.VMEM((2, 16 + rows, columns), F32),
            pltpu.VMEM((2 * rows, 2 * columns), BF16),
            pltpu.VMEM((2 * rows, width), F32),
        ],
        length,
        frames,
        ln2_gain[None],
        *pw_pieces,
        blocks[1],
        halo_x,
        own_share,
        peer_share,
        channels,
        channels_peer,
        vmem=14,
    )
    return (base + other_side(share).astype(F32)).astype(BF16)


def solution(mesh):
    in_specs = (
        P(("parts", "seq", "head", "fsdp"), None),
        P("parts"),
        P(),
        P("seq", ("head", "fsdp")),
        P("seq", ("head", "fsdp")),
        P("seq", ("head", "fsdp")),
        P(("head", "fsdp"), "seq"),
        P(),
        P("seq", ("head", "fsdp")),
        P("seq", ("head", "fsdp")),
        P(None, ("head", "fsdp")),
        P(("head", "fsdp")),
        P(("head", "fsdp")),
        P(("head", "fsdp"), "seq"),
    )
    out_specs = P(("parts", "seq", "head", "fsdp"), None)
    body = shards_chip_per_head if one_head_per_chip(mesh) else shards_general
    return jax.shard_map(body, mesh=mesh, in_specs=in_specs, out_specs=out_specs, check_vma=False)
```

```python
import math

import jax
import jax.numpy as jnp
from jax import lax
from jax.experimental import pallas as pl
from jax.experimental.pallas import tpu as pltpu
from jax.sharding import PartitionSpec as P

KERNEL = 9
HD = 128


def with_halo(block, sides, width):
    for axis, dim in sides:
        count = lax.axis_size(axis)
        forward = [(i, i + 1) for i in range(count - 1)]
        backward = [(target, source) for source, target in forward]
        low = lax.ppermute(
            lax.slice_in_dim(block, block.shape[dim] - width, None, axis=dim), axis, forward
        )
        high = lax.ppermute(lax.slice_in_dim(block, 0, width, axis=dim), axis, backward)
        block = jnp.concatenate([low, block, high], axis=dim)
    return block


def layer_norm(values_in, gain_vec):
    center = jnp.mean(values_in, axis=-1, keepdims=True)
    shifted = values_in - center
    spread = jnp.mean(shifted * shifted, axis=-1, keepdims=True)
    return shifted * lax.rsqrt(spread + 1e-05) * gain_vec


def shards_general(
    frames,
    length,
    ln1_gain,
    w_query,
    w_key,
    w_value,
    w_out,
    ln2_gain,
    pw1_value,
    pw1_gate,
    depth_kernel,
    bn_scale,
    bn_shift,
    pw2,
):
    group_size = lax.axis_size(("head", "fsdp"))
    my_rows = frames.shape[0]
    block_rows = my_rows * group_size
    head_cols = w_query.shape[1]
    heads_here = head_cols // HD
    seq_start = lax.axis_index("seq") * block_rows
    valid_len = length[0]
    score_scale = 1.0 / math.sqrt(HD)
    full_query, full_key, full_value, value_cols, gate_cols = (
        lax.all_gather(w_query, "seq", axis=0, tiled=True),
        lax.all_gather(w_key, "seq", axis=0, tiled=True),
        lax.all_gather(w_value, "seq", axis=0, tiled=True),
        lax.all_gather(pw1_value, "seq", axis=0, tiled=True),
        lax.all_gather(pw1_gate, "seq", axis=0, tiled=True),
    )
    out_rows, down_rows = (
        lax.all_gather(w_out, "seq", axis=1, tiled=True),
        lax.all_gather(pw2, "seq", axis=1, tiled=True),
    )
    projector = jnp.concatenate((full_query, full_key, full_value), axis=1)
    source = frames.astype(jnp.float32)
    normed = layer_norm(source, ln1_gain).astype(jnp.bfloat16)
    projected = jnp.dot(
        lax.all_gather(normed, ("head", "fsdp"), axis=0, tiled=True),
        projector,
        preferred_element_type=jnp.float32,
    ).astype(jnp.bfloat16)
    queries = projected[:, :head_cols].reshape(block_rows, heads_here, HD)
    keys_here = projected[:, head_cols : 2 * head_cols]
    values_here = projected[:, 2 * head_cols :]
    initial = (
        jnp.full((heads_here, block_rows), -1e30, jnp.float32),
        jnp.zeros((heads_here, block_rows), jnp.float32),
        jnp.zeros((heads_here, block_rows, HD), jnp.float32),
    )
    key_piece = lax.all_gather(keys_here, "seq", axis=0, tiled=True)
    value_piece = lax.all_gather(values_here, "seq", axis=0, tiled=True)
    row_count = key_piece.shape[0]
    block_size = math.gcd(row_count, 512)
    block_count = row_count // block_size
    key_blocks = key_piece.reshape(block_count, block_size, heads_here, HD)
    value_blocks = value_piece.reshape(block_count, block_size, heads_here, HD)
    places = jnp.arange(row_count, dtype=jnp.int32).reshape(block_count, block_size)

    def advance(inner_state, block_item):
        key_block, value_block, place = block_item
        peak_score, weight_sum, weighted = inner_state
        scores = (
            jnp.einsum("qhd,khd->hqk", queries, key_block, preferred_element_type=jnp.float32)
            * score_scale
        )
        scores = jnp.where((place < valid_len)[None, None, :], scores, -jnp.inf)
        new_peak = jnp.maximum(peak_score, jnp.max(scores, axis=2))
        factor = jnp.exp(peak_score - new_peak)
        weights = jnp.exp(scores - new_peak[:, :, None])
        weight_sum = weight_sum * factor + jnp.sum(weights, axis=2)
        weighted = weighted * factor[:, :, None] + jnp.einsum(
            "hqk,khd->hqd",
            weights.astype(jnp.bfloat16),
            value_block,
            preferred_element_type=jnp.float32,
        )
        return ((new_peak, weight_sum, weighted), None)

    result, unused = lax.scan(advance, initial, (key_blocks, value_blocks, places))
    peak_score, weight_sum, weighted = result
    context = (
        (weighted / weight_sum[:, :, None])
        .astype(jnp.bfloat16)
        .transpose(1, 0, 2)
        .reshape(block_rows, head_cols)
    )
    attended = lax.psum_scatter(
        jnp.dot(context, out_rows, preferred_element_type=jnp.float32).astype(jnp.bfloat16),
        ("head", "fsdp"),
        scatter_dimension=0,
        tiled=True,
    ).astype(jnp.float32)
    middle = source + attended
    normed_two = layer_norm(middle, ln2_gain).astype(jnp.bfloat16)
    piece = lax.all_gather(normed_two, ("head", "fsdp"), axis=0, tiled=True)
    value_part = jnp.dot(piece, value_cols, preferred_element_type=jnp.float32)
    gate_part = jnp.dot(piece, gate_cols, preferred_element_type=jnp.float32)
    places = seq_start + jnp.arange(piece.shape[0], dtype=jnp.int32)
    gated_rows = jnp.where(
        (places < valid_len)[:, None], value_part * jax.nn.sigmoid(gate_part), 0.0
    ).astype(jnp.bfloat16)
    rim_width = (KERNEL - 1) // 2
    padded = with_halo(gated_rows, (("seq", 0),), rim_width).astype(jnp.float32)
    depth_sum = depth_kernel[0] * padded[0:block_rows]
    for offset in range(1, KERNEL):
        depth_sum = depth_sum + depth_kernel[offset] * padded[offset : offset + block_rows]
    shifted = depth_sum * bn_scale + bn_shift
    active = (shifted * jax.nn.sigmoid(shifted)).astype(jnp.bfloat16)
    conv_part = lax.psum_scatter(
        jnp.dot(active, down_rows, preferred_element_type=jnp.float32).astype(jnp.bfloat16),
        ("head", "fsdp"),
        scatter_dimension=0,
        tiled=True,
    ).astype(jnp.float32)
    return (middle + conv_part).astype(jnp.bfloat16)


SEQ = 4
EDGE = (KERNEL - 1) // 2
HALO = 2 * EDGE
SWAP = [(0, 1), (1, 0)]
F32 = jnp.float32
BF16 = jnp.bfloat16


def one_head_per_chip(mesh):
    return dict(mesh.shape) == {"parts": 2, "seq": SEQ, "head": 2, "fsdp": 2}


def xor_pairs(k):
    return [(i, i ^ k) for i in range(SEQ)]


def call(kernel, outs, scratch, length, *operands, vmem=8, left=0):
    fixed = [pltpu.with_memory_space_constraint(a, pltpu.HBM) for a in operands[:left]]
    return pl.pallas_call(
        kernel,
        out_shape=outs,
        in_specs=[pl.BlockSpec(memory_space=pltpu.SMEM)]
        + [pl.BlockSpec(memory_space=pltpu.HBM)] * left
        + [pl.BlockSpec(memory_space=pltpu.VMEM)] * (len(operands) - left),
        out_specs=[pl.BlockSpec(memory_space=pltpu.VMEM)] * len(outs),
        scratch_shapes=scratch,
        cost_estimate=pl.CostEstimate(flops=0, bytes_accessed=0, transcendentals=0),
        compiler_params=pltpu.CompilerParams(vmem_limit_bytes=vmem << 20),
    )(length, *fixed, *operands[left:])


def aligned(value, to):
    return pl.multiple_of(value, to)


def dot(a, b):
    return jnp.dot(a, b, preferred_element_type=F32)


def here():
    return tuple(lax.axis_index(a) for a in ("seq", "head", "fsdp", "parts"))


def deal_kernel(length, *refs):
    sources, later, other = refs[:4], refs[4:7], refs[7:10]
    outs, later_out, held, sems, later_sems = refs[10:14], *refs[14:]
    s, _, f, p = here()
    half = outs[0].shape[1]
    copies = [pltpu.make_async_copy(w, held.at[i], sems.at[i]) for i, w in enumerate(sources)]
    at = pl.ds(aligned(p * half, half), half)
    later_copies = [
        pltpu.make_async_copy(w.at[at], later_out.at[i], later_sems.at[i]) for i, w in enumerate(later)
    ]
    for copy in copies + later_copies:
        copy.start()
    mine, w_out = [held.at[m] for m in range(3)], held.at[3]
    for copy in copies:
        copy.wait()
    rows = pl.ds(aligned(f * half, half), half)
    for k in range(SEQ):
        head = s ^ k
        columns = pl.ds(aligned((head % 2) * HD, HD), HD)

        @pl.when(head // 2 == f)
        def _():
            for m in range(3):
                outs[k][m] = mine[m][rows, columns]

        @pl.when(head // 2 != f)
        def _():
            for m in range(3):
                outs[k][m] = other[m][rows, columns]

        for m in range(outs[k].shape[0] - 3):
            outs[k][3 + m] = w_out[at, m * HD : (m + 1) * HD]
    for copy in later_copies:
        copy.wait()


def stack_kernel(length, *refs):
    s = lax.axis_index("seq")
    for k in range(SEQ):
        refs[SEQ][s ^ k] = refs[k][...]


def project_kernel(length, *refs):
    frames, gain, *blocks = refs[: 2 * SEQ + 1]
    mine, other, down = refs[2 * SEQ + 1 : 3 * SEQ + 1], refs[3 * SEQ + 1 : 4 * SEQ + 1], refs[4 * SEQ + 1]
    q_out, send_out, edge_out, stack_out, normed, weights, x_edge, q_edge, own_x, own_gain, sems = refs[4 * SEQ + 2 :]
    copies = [
        pltpu.make_async_copy(frames, own_x, sems.at[0]),
        pltpu.make_async_copy(gain, own_gain, sems.at[1]),
    ]
    for copy in copies:
        copy.start()
    s, h, f, _ = here()
    blocks = [own_x, *blocks]
    rows = blocks[0].shape[0]
    half = mine[0].shape[1]
    for copy in copies:
        copy.wait()
    gain_row = own_gain[...]
    for k in range(SEQ):
        for core, pieces in enumerate((mine, other)):
            at = pl.ds(aligned((s ^ k) * 2 * half + (f ^ core) * half, half), half)
            for m in range(3):
                weights[at, m * HD : (m + 1) * HD] = pieces[k][m]
        stack_out[s ^ k] = down[...] if k == 2 else mine[k][3:]
    count = 2 * SEQ
    total = count * rows
    for k in range(SEQ):
        for side in range(2):
            at = (s ^ k) * 2 + (h ^ side)
            x = blocks[2 * k + side][...].astype(F32)
            normed[k, side * rows : (side + 1) * rows, :] = layer_norm(x, gain_row).astype(BF16)
            x_edge[at, 0:EDGE, :] = x[:EDGE]
            x_edge[at, EDGE:HALO, :] = x[rows - EDGE :]
        both = dot(normed[k], weights[...])
        for side in range(2):
            at = (s ^ k) * 2 + (h ^ side)
            start = aligned(at * rows, rows)
            part = both[side * rows : (side + 1) * rows]
            q_out[pl.ds(start, rows), :] = part[:, :HD].astype(BF16)
            send_out[pl.ds(start, rows), :] = part[:, HD : 2 * HD].astype(BF16)
            send_out[pl.ds(aligned(start + total, rows), rows), :] = part[:, 2 * HD :].astype(BF16)
            q_edge[at, 0:EDGE, :] = part[:EDGE, :HD]
            q_edge[at, EDGE:HALO, :] = part[rows - EDGE :, :HD]

    def around(edge, b):
        low = jnp.maximum(b - f, 0)
        high = jnp.minimum(b + 1 - f, count - 1)
        return jnp.concatenate([edge[low, EDGE:HALO, :], edge[high, 0:EDGE, :]], axis=0)

    halos = jnp.concatenate([around(q_edge, b) for b in range(count)], axis=0)
    send_out[2 * total :, :] = halos.astype(BF16)
    edge_out[...] = jnp.concatenate([around(x_edge, s * 2 + b) for b in range(2)], axis=0).astype(BF16)


def attend_kernel(length, q_in, own, peer, *refs):
    ctx_outs, q_rows = refs[:SEQ], refs[SEQ]
    s, _, f, _ = here()
    valid_len = length[0]
    count = q_rows.shape[0]
    total = q_in.shape[0]
    rows = total // count
    step = q_rows.shape[1]
    local = lax.broadcasted_iota(jnp.int32, (1, total), 1)
    base = (local // rows) * (2 * rows) + local % rows
    keep_own = base + f * rows < valid_len
    keep_peer = base + (1 - f) * rows < valid_len
    scale = 1.0 / math.sqrt(HD)
    keys_t = (((1,), (1,)), ((), ()))
    for b in range(count):
        q_rows[b, 0:rows, :] = q_in[b * rows : (b + 1) * rows, :].astype(F32)
        q_rows[b, rows:step, :] = peer[2 * total + b * HALO : 2 * total + (b + 1) * HALO, :].astype(F32)
    for k in range(SEQ):
        q = jnp.concatenate([q_rows[(s ^ k) * 2 + side] for side in range(2)], axis=0).astype(BF16)
        first = lax.dot_general(q, own[0:total, :], keys_t, preferred_element_type=F32) * scale
        second = lax.dot_general(q, peer[0:total, :], keys_t, preferred_element_type=F32) * scale
        first = jnp.where(keep_own, first, -jnp.inf)
        second = jnp.where(keep_peer, second, -jnp.inf)
        peak = jnp.maximum(
            jnp.max(first, axis=1, keepdims=True), jnp.max(second, axis=1, keepdims=True)
        )
        first = jnp.exp(first - peak)
        second = jnp.exp(second - peak)
        weight_sum = jnp.sum(first, axis=1, keepdims=True) + jnp.sum(second, axis=1, keepdims=True)
        weighted = dot(first.astype(BF16), own[total : 2 * total, :]) + dot(
            second.astype(BF16), peer[total : 2 * total, :]
        )
        ctx_outs[k][...] = (weighted / weight_sum).astype(BF16)


def output_kernel(length, *refs):
    pieces, ctx = refs[:4], refs[4 : 4 + SEQ]
    share_out, send_out, context, weights = refs[4 + SEQ :]
    s, h, f, p = here()
    half = pieces[0].shape[2]
    columns = weights.shape[2]
    for y in range(2):
        for core in range(2):
            rows = pl.ds(aligned((f ^ core) * 2 * half + (p ^ y) * half, half), half)
            for m in range(columns // HD):
                for j in range(SEQ):
                    weights[j, rows, m * HD : (m + 1) * HD] = pieces[y * 2 + core][j, m]
    for k in range(SEQ):
        context[:, pl.ds(aligned((s ^ k) * HD, HD), HD)] = ctx[k][...]
    for j in range(SEQ):
        at = slice(j * columns, (j + 1) * columns)
        share = dot(context[...], weights[j])
        share_out[:, at] = share
        send_out[:, at] = share.astype(BF16)


def convolve_kernel(length, *refs):
    own_x, gain, pieces = refs[0], refs[1], refs[2:6]
    peer_x, halo_x, own_share, peer_share, own_c, peer_c, base_out, share_out = refs[6:14]
    mid, normed, w_value, w_gate, w_down, channel, padded, active, shares = refs[14:]
    s, h, f, p = here()
    valid_len = length[0]
    half, columns = pieces[0].shape[2:]
    rows = own_x.shape[0]
    step = rows + HALO
    for y in range(2):
        for core in range(2):
            stack = pieces[y * 2 + core]
            down = pl.ds(aligned((f ^ core) * 2 * half + (p ^ y) * half, half), half)
            for plane in range(SEQ):
                at = pl.ds(aligned(plane * 2 * half + (p ^ y) * half, half), half)
                w_value[f ^ core, at, :] = stack[plane, 0]
                w_gate[f ^ core, at, :] = stack[plane, 1]
                w_down[plane, down, :] = stack[plane, 2]
    channel[f] = own_c[...]
    channel[1 - f] = peer_c[...]
    mid[pl.ds(aligned(h * step, 8), rows), :] = own_x[...].astype(F32)
    mid[pl.ds(aligned((1 - h) * step, 8), rows), :] = peer_x[...].astype(F32)
    for b in range(2):
        mid[b * step + rows : (b + 1) * step, :] = halo_x[b * HALO : (b + 1) * HALO, :].astype(F32)
    middle = mid[...] + (own_share[...] + peer_share[...].astype(F32))
    mid[...] = middle
    normed[...] = layer_norm(middle, gain[...]).astype(BF16)
    place = lax.broadcasted_iota(jnp.int32, (step, columns), 0)
    offset = jnp.where(place < rows, place, jnp.where(place < rows + EDGE, place - rows - EDGE, place - EDGE))
    for c in range(2):
        x = normed[...]
        value_part = dot(x, w_value[c])
        gate_part = dot(x, w_gate[c])
        gated = value_part * jax.nn.sigmoid(gate_part)
        for b in range(2):
            t = offset + (4 * s + 2 * b + f) * rows
            kept = jnp.where((t >= 0) & (t < valid_len), gated[b * step : (b + 1) * step], 0.0)
            kept = kept.astype(BF16).astype(F32)
            padded[b, 8 : 8 + rows, :] = kept[:rows]
            padded[b, 8 - EDGE : 8, :] = kept[rows : rows + EDGE]
            padded[b, 8 + rows : 8 + rows + EDGE, :] = kept[rows + EDGE :]
            depth_sum = channel[c, 0:1, :] * padded[b, 8 - EDGE : 8 - EDGE + rows, :]
            for j in range(1, KERNEL):
                low = 8 - EDGE + j
                depth_sum = depth_sum + channel[c, j : j + 1, :] * padded[b, low : low + rows, :]
            shifted = depth_sum * channel[c, KERNEL : KERNEL + 1, :] + channel[c, KERNEL + 1 : KERNEL + 2, :]
            active[b * rows : (b + 1) * rows, c * columns : (c + 1) * columns] = (
                shifted * jax.nn.sigmoid(shifted)
            ).astype(BF16)
    for j in range(SEQ):
        shares[:, j * columns : (j + 1) * columns] = dot(active[...], w_down[j])
    base_out[...] = mid[pl.ds(aligned(h * step, 8), rows), :] + shares[pl.ds(aligned(h * rows, rows), rows), :]
    share_out[...] = shares[pl.ds(aligned((1 - h) * rows, rows), rows), :].astype(BF16)


def shards_chip_per_head(
    frames,
    length,
    ln1_gain,
    w_query,
    w_key,
    w_value,
    w_out,
    ln2_gain,
    pw1_value,
    pw1_gate,
    depth_kernel,
    bn_scale,
    bn_shift,
    pw2,
):
    rows, width = frames.shape
    count = 2 * SEQ
    step = rows + HALO
    f, p = lax.axis_index("fsdp"), lax.axis_index("parts")
    half = w_query.shape[0] // 2
    columns = w_query.shape[1]
    barrier = lax.optimization_barrier

    def after(x, *others):
        return barrier((x, *others))[0]

    def other_core(x):
        return lax.ppermute(x, "fsdp", SWAP)

    def other_side(x):
        return lax.ppermute(x, "head", SWAP)

    def other_part(x):
        return lax.ppermute(x, "parts", SWAP)

    def across(x, k):
        return lax.ppermute(x, "seq", xor_pairs(k))

    def planes(x):
        far = across(x, 3)
        return [x, across(x, 1), across(far, 1), far]

    def part_half(x):
        return lax.dynamic_slice_in_dim(x, p * half, half, axis=x.ndim - 2)

    near = planes(frames)
    blocks = []
    for block in near:
        blocks += [block, other_side(block)]
    given = [w_query, w_key, w_value]
    shape = jax.ShapeDtypeStruct
    *dealt, pw_mine = call(
        deal_kernel,
        [shape((3 if k == 2 else 3 + columns // HD, half, HD), BF16) for k in range(SEQ)]
        + [shape((3, half, columns), BF16)],
        [
            pltpu.VMEM((4, 2 * half, columns), BF16),
            pltpu.SemaphoreType.DMA((4,)),
            pltpu.SemaphoreType.DMA((3,)),
        ],
        length,
        *given,
        w_out,
        pw1_value,
        pw1_gate,
        pw2,
        *[other_core(w) for w in given],
        left=7,
    )
    *dealt, _ = barrier((*dealt, near[1]))
    w_mine = [dealt[0]] + [across(dealt[k], k) for k in range(1, SEQ)]
    w_other = [other_core(w[:3]) for w in w_mine]
    down = across(w_mine[3][3:], 1)
    pw_part = other_part(pw_mine)
    w_other[0], pw_part = barrier((w_other[0], pw_part))
    pw_later = after(pw_mine, *w_mine[1:], down)
    pw_one, pw_three = across(pw_later, 1), across(pw_later, 3)
    queries, send, edges, stack = call(
        project_kernel,
        [
            shape((count * rows, HD), BF16),
            shape((2 * count * rows + count * HALO, HD), BF16),
            shape((2 * HALO, width), BF16),
            shape((SEQ, columns // HD, half, HD), BF16),
        ],
        [
            pltpu.VMEM((SEQ, 2 * rows, width), BF16),
            pltpu.VMEM((width, 3 * HD), BF16),
            pltpu.VMEM((count, HALO, width), F32),
            pltpu.VMEM((count, HALO, HD), F32),
            pltpu.VMEM((rows, width), BF16),
            pltpu.VMEM((1, width), F32),
            pltpu.SemaphoreType.DMA((2,)),
        ],
        length,
        frames,
        ln1_gain[None],
        *blocks[1:],
        *w_mine,
        *w_other,
        down,
        left=2,
    )
    received = other_core(send)
    stack_part = other_part(stack)
    ctx = call(
        attend_kernel,
        [shape((2 * step, HD), BF16)] * SEQ,
        [pltpu.VMEM((count, step, HD), F32)],
        length,
        queries,
        send,
        received,
    )
    stack, stack_part, *_ = barrier((stack, stack_part, *ctx))
    out_pieces = [stack, other_core(stack), stack_part, other_core(stack_part)]
    ctx = [ctx[0]] + [lax.ppermute(ctx[k], "seq", xor_pairs(k)) for k in range(1, SEQ)]
    one_part = other_part(pw_one)
    ctx[0] = after(ctx[0], one_part)
    pw_far = after(pw_three, *ctx[1:])
    pw_two, three_part = across(pw_far, 1), other_part(pw_far)
    own_share, sent_share = call(
        output_kernel,
        [shape((2 * step, width), F32), shape((2 * step, width), BF16)],
        [
            pltpu.VMEM((2 * step, SEQ * HD), BF16),
            pltpu.VMEM((SEQ, 2 * columns, columns), BF16),
        ],
        length,
        *out_pieces,
        *ctx,
    )
    edges, depth_kernel = after(edges, own_share), after(depth_kernel, own_share)
    halo_x = other_core(edges)
    channels = jnp.concatenate([depth_kernel, bn_scale[None], bn_shift[None], jnp.zeros((5, columns), F32)])
    channels_peer = other_core(channels)
    peer_share = other_side(sent_share)

    def stacked(*pieces):
        (stack,) = call(stack_kernel, [shape((SEQ, *pieces[0].shape), BF16)], [], length, *pieces)
        return [stack, other_core(stack)]

    two_part = other_part(pw_two)
    pw_mine = after(pw_mine, own_share)
    pw_pieces = stacked(pw_mine, pw_one, pw_two, pw_three) + stacked(after(pw_part, channels_peer, halo_x, peer_share), one_part, two_part, three_part)
    base, share = call(
        convolve_kernel,
        [shape((rows, width), F32), shape((rows, width), BF16)],
        [
            pltpu.VMEM((2 * step, width), F32),
            pltpu.VMEM((2 * step, width), BF16),
            pltpu.VMEM((2, width, columns), BF16),
            pltpu.VMEM((2, width, columns), BF16),
            pltpu.VMEM((SEQ, 2 * columns, columns), BF16),
            pltpu.VMEM((2, 16, columns), F32),
            pltpu.VMEM((2, 16 + rows, columns), F32),
            pltpu.VMEM((2 * rows, 2 * columns), BF16),
            pltpu.VMEM((2 * rows, width), F32),
        ],
        length,
        frames,
        ln2_gain[None],
        *pw_pieces,
        blocks[1],
        halo_x,
        own_share,
        peer_share,
        channels,
        channels_peer,
        vmem=14,
    )
    return (base + other_side(share).astype(F32)).astype(BF16)


def solution(mesh):
    in_specs = (
        P(("parts", "seq", "head", "fsdp"), None),
        P("parts"),
        P(),
        P("seq", ("head", "fsdp")),
        P("seq", ("head", "fsdp")),
        P("seq", ("head", "fsdp")),
        P(("head", "fsdp"), "seq"),
        P(),
        P("seq", ("head", "fsdp")),
        P("seq", ("head", "fsdp")),
        P(None, ("head", "fsdp")),
        P(("head", "fsdp")),
        P(("head", "fsdp")),
        P(("head", "fsdp"), "seq"),
    )
    out_specs = P(("parts", "seq", "head", "fsdp"), None)
    body = shards_chip_per_head if one_head_per_chip(mesh) else shards_general
    return jax.shard_map(body, mesh=mesh, in_specs=in_specs, out_specs=out_specs, check_vma=False)
```
